32 devices in a mesh: dp: 4 (over y, x), ctx: 8 (over z, core).
Axes of the slice: x: 2, y: 2, z: 4, core: 2. Of those that a mesh axis runs over, the one named last changes fastest.
Arguments:
- tokens: bfloat16 [8, 512, 2560], P('dp', 'ctx'), may hold values from -6 to 6
- lengths: int32 [8], P('dp'), may hold values from 128 to 512, as said below
- cotangent: bfloat16 [8, 512, 2560], P('dp', 'ctx'), may hold values from -6 to 6
- input_gain: bfloat16 [2560], P(('dp', 'ctx')), may hold values from 0.5 to 1.5
- query_gain: bfloat16 [768], P(('dp', 'ctx')), may hold values from 0.5 to 1.5
- latent_gain: bfloat16 [256], P(('dp', 'ctx')), may hold values from 0.5 to 1.5
- post_gain: bfloat16 [2560], P(('dp', 'ctx')), may hold values from 0.5 to 1.5
- query_down: bfloat16 [2560, 768], P(('dp', 'ctx')), may hold values from -0.125 to 0.125
- query_up: bfloat16 [768, 3840], P(('dp', 'ctx')), may hold values from -0.21875 to 0.21875
- latent_down: bfloat16 [2560, 288], P(('dp', 'ctx')), may hold values from -0.125 to 0.125
- latent_up: bfloat16 [256, 5120], P(('dp', 'ctx')), may hold values from -0.375 to 0.375
- out_proj: bfloat16 [2560, 2560], P(('dp', 'ctx')), may hold values from -6 to 6
- gate_proj: bfloat16 [2560, 6400], P(('dp', 'ctx')), may hold values from -0.125 to 0.125
- up_proj: bfloat16 [2560, 6400], P(('dp', 'ctx')), may hold values from -0.125 to 0.125
- down_proj: bfloat16 [6400, 2560], P(('dp', 'ctx')), may hold values from -0.75 to 0.75
Outputs:
- layer_out: bfloat16 [8, 512, 2560], P('dp', 'ctx')
- input_grad: float32 [8, 512, 2560], P('dp', 'ctx')
- grad_input_gain: float32 [2560], P(('dp', 'ctx'))
- grad_query_gain: float32 [768], P(('dp', 'ctx'))
- grad_latent_gain: float32 [256], P(('dp', 'ctx'))
- grad_post_gain: float32 [2560], P(('dp', 'ctx'))
- grad_query_down: float32 [2560, 768], P(('dp', 'ctx'))
- grad_query_up: float32 [768, 3840], P(('dp', 'ctx'))
- grad_latent_down: float32 [2560, 288], P(('dp', 'ctx'))
- grad_latent_up: float32 [256, 5120], P(('dp', 'ctx'))
- grad_out_proj: float32 [2560, 2560], P(('dp', 'ctx'))
- grad_gate_proj: float32 [2560, 6400], P(('dp', 'ctx'))
- grad_up_proj: float32 [2560, 6400], P(('dp', 'ctx'))
- grad_down_proj: float32 [6400, 2560], P(('dp', 'ctx'))
The draws below stay inside these ranges and needn't reach their ends.
Inputs may be any that keep to these rules, and one draw needn't show every extreme that they name: `lengths`: positions at or past a slot's length are padding; some slot has all 512 positions valid.
All inputs are finite; a program needn't handle non-finite values.
Results may differ from the reference program's by a relative error of at most 0.018.
Values may be sent and summed in bfloat16 or wider, within the bound.
A program may use at most 640 MiB of HBM per device.

```python
import jax
import jax.numpy as jnp
from jax import lax

D = 2560
FF = 6400
HEADS = 40
QRANK = 768
KVRANK = 256
NOPE = 64
ROPE = 32
VDIM = 64
SEQS = 8
SLOT = 512


def draw_lengths(key, part):
    first_key, second_key = jax.random.split(jax.random.fold_in(key, 11))
    values = jax.random.randint(first_key, (SEQS,), SLOT // 4, SLOT + 1)
    chosen = jax.random.randint(second_key, (), 0, SEQS)
    return jnp.where(jnp.arange(SEQS) == chosen, SLOT, values).astype(jnp.int32)


def block_scale(rng, extent, pieces, smallest, top_value):
    def one(position, blocks):
        heights = jax.random.uniform(jax.random.fold_in(jax.random.fold_in(rng, 6), position), (blocks,), jnp.float32, smallest / len(pieces), top_value / len(pieces))
        return jnp.repeat(jnp.exp(heights), extent[position] // blocks).reshape((-1,) + (1,) * (len(extent) - position - 1))

    level = one(*pieces[0])
    for cut in pieces[1:]:
        level = level * one(*cut)
    return level


def gaussian(stream_key, dims, width, limit, shards=(), kind=jnp.bfloat16):
    entries = jax.random.normal(stream_key, dims, jnp.float32) * width
    if len(shards) > 0:
        entries = block_scale(stream_key, dims, shards, -0.22, 0.18) * entries
    return jnp.clip(entries, min=-limit, max=limit).astype(kind)


def setup_inputs(seed: int = 0) -> dict:
    key_of = jax.random.split(jax.random.key(seed), 16)
    tokens = gaussian(key_of[0], (SEQS, SLOT, D), 1.0, 6.0, ((0, 4), (1, 8)))
    lengths = draw_lengths(jax.random.fold_in(key_of[15], 71), 0)
    cotangent = gaussian(key_of[2], (SEQS, SLOT, D), 1.0, 6.0, ((0, 4), (1, 8)))
    input_gain = jnp.clip(1.0 + 0.1 * jax.random.normal(key_of[3], (D,), jnp.float32), 0.5, 1.5).astype(jnp.bfloat16)
    query_gain = jnp.clip(1.0 + 0.1 * jax.random.normal(key_of[4], (QRANK,), jnp.float32), 0.5, 1.5).astype(jnp.bfloat16)
    latent_gain = jnp.clip(1.0 + 0.1 * jax.random.normal(key_of[5], (KVRANK,), jnp.float32), 0.5, 1.5).astype(jnp.bfloat16)
    post_gain = jnp.clip(1.0 + 0.1 * jax.random.normal(key_of[6], (D,), jnp.float32), 0.5, 1.5).astype(jnp.bfloat16)
    query_down = gaussian(key_of[7], (D, QRANK), D ** -0.5, 0.125, ((0, 32),))
    query_up = gaussian(key_of[8], (QRANK, HEADS * (NOPE + ROPE)), QRANK ** -0.5, 0.21875, ((0, 32),))
    latent_down = gaussian(key_of[9], (D, KVRANK + ROPE), D ** -0.5, 0.125, ((0, 32),))
    latent_up = gaussian(key_of[10], (KVRANK, HEADS * (NOPE + VDIM)), KVRANK ** -0.5, 0.375, ((0, 32),))
    out_proj = gaussian(key_of[11], (D, HEADS * VDIM), 1.0, 6.0, ((0, 32),))
    gate_proj = gaussian(key_of[12], (D, FF), D ** -0.5, 0.125, ((0, 32),))
    up_proj = gaussian(key_of[13], (D, FF), D ** -0.5, 0.125, ((0, 32),))
    down_proj = gaussian(key_of[14], (FF, D), 64 ** -0.5, 0.75, ((0, 32),))
    return {"tokens": tokens, "lengths": lengths, "cotangent": cotangent, "input_gain": input_gain, "query_gain": query_gain, "latent_gain": latent_gain, "post_gain": post_gain, "query_down": query_down, "query_up": query_up, "latent_down": latent_down, "latent_up": latent_up, "out_proj": out_proj, "gate_proj": gate_proj, "up_proj": up_proj, "down_proj": down_proj}


@jax.custom_vjp
def low(v):
    return lax.optimization_barrier(v.astype(jnp.bfloat16)).astype(jnp.float32)

@jax.custom_vjp
def low_back(v):
    return v

def low_keep(v):
    return (low(v), None)

def low_pass(kept, grad):
    return (grad,)

def back_keep(v):
    return (v, None)

def back_low(kept, grad):
    return (low(grad),)
low.defvjp(low_keep, low_pass)
low_back.defvjp(back_keep, back_low)
epsilon = 1e-05
highest = lax.Precision.HIGHEST
branch_scale = 1.4 / 62 ** 0.5
neg_large = -1e+30

def matmul(left, right):
    return jnp.dot(left, right, precision=highest, preferred_element_type=jnp.float32)

def rms_norm(values, gain):
    return values * lax.rsqrt(lax.optimization_barrier(jnp.mean(values * values, axis=-1, keepdims=True)) + epsilon) * gain

def rotate(values, cosine, sine):
    half_width = values.shape[-1] // 2
    leading = values[..., :half_width]
    trailing = values[..., half_width:]
    return jnp.concatenate([leading * cosine - trailing * sine, trailing * cosine + leading * sine], axis=-1)

def layer(inputs, weights, length):
    input_gain, query_gain, latent_gain, post_gain, query_down, query_up, latent_down, latent_up, out_proj, gate_proj, up_proj, down_proj = weights
    positions = jnp.arange(SLOT, dtype=jnp.int32)
    freqs = 10000.0 ** (-(2.0 * jnp.arange(ROPE // 2, dtype=jnp.float32)) / ROPE)
    angles = positions.astype(jnp.float32)[:, None] * freqs[None, :]
    cosine = jnp.cos(angles)
    sine = jnp.sin(angles)
    score_scale = 1.0 / (NOPE + ROPE) ** 0.5
    normed_in = low(rms_norm(inputs, input_gain))
    query_latent = low_back(matmul(normed_in, query_down))
    query_normed = low(rms_norm(query_latent, query_gain))
    query_full = low_back(matmul(query_normed, query_up)).reshape(SLOT, HEADS, NOPE + ROPE)
    query_rot = rotate(query_full[..., NOPE:], cosine[:, None, :], sine[:, None, :])
    query = low_back(low(jnp.concatenate([query_full[..., :NOPE], query_rot], axis=-1)))
    latent_all = low_back(matmul(normed_in, latent_down))
    latent_normed = low(rms_norm(latent_all[:, :KVRANK], latent_gain))
    key_rope = low(rotate(latent_all[:, KVRANK:], cosine, sine))
    key_value = low(matmul(latent_normed, latent_up)).reshape(SLOT, HEADS, NOPE + VDIM)
    allowed = (positions[None, :] <= positions[:, None]) & (positions[None, :] < length)

    def one_head(items):
        head_query, head_kv = items
        keys = jnp.concatenate([head_kv[:, :NOPE], key_rope], axis=-1)
        scores = low_back(matmul(head_query, keys.T) * score_scale)
        masked = jnp.where(allowed, scores, neg_large)
        log_total = jax.nn.logsumexp(masked, axis=-1)
        probs = low(jnp.exp(masked - log_total[:, None]))
        return low_back(low(matmul(probs, head_kv[:, NOPE:])))
    heads_out = lax.map(jax.checkpoint(one_head), (query.transpose(1, 0, 2), key_value.transpose(1, 0, 2)))
    attn = heads_out.transpose(1, 0, 2).reshape(SLOT, HEADS * VDIM)
    middle = inputs + branch_scale * low_back(matmul(attn, out_proj.T))
    normed_mid = low(rms_norm(middle, post_gain))
    gate_act = low_back(matmul(normed_mid, gate_proj))
    up_act = low_back(matmul(normed_mid, up_proj))
    hidden = low(jax.nn.silu(gate_act) * up_act)
    return middle + branch_scale * low_back(matmul(hidden, down_proj))

def reference(tokens, lengths, cotangent, input_gain, query_gain, latent_gain, post_gain, query_down, query_up, latent_down, latent_up, out_proj, gate_proj, up_proj, down_proj):
    weights = tuple((weight.astype(jnp.float32) for weight in (input_gain, query_gain, latent_gain, post_gain, query_down, query_up, latent_down, latent_up, out_proj, gate_proj, up_proj, down_proj)))

    def one_sequence(totals, items):
        sequence, length, grad_out = items

        def forward(values, params):
            return layer(values, params, length)
        output, pull = jax.vjp(forward, sequence.astype(jnp.float32), weights)
        grad_in, grad_weights = pull(grad_out.astype(jnp.float32))
        totals = tuple((before + extra for before, extra in zip(totals, grad_weights)))
        return (totals, (output.astype(jnp.bfloat16), grad_in))
    zeros = tuple((jnp.zeros_like(weight) for weight in weights))
    sums, (outputs, input_grads) = lax.scan(one_sequence, zeros, (tokens, lengths, cotangent))
    return (outputs, input_grads, sums[0], sums[1], sums[2], sums[3], sums[4], sums[5], sums[6], sums[7], sums[8], sums[9], sums[10], sums[11])
```

```python
import functools

import jax
import jax.numpy as jnp
from jax import lax
from jax.experimental import pallas as pl
from jax.experimental.pallas import tpu as pltpu
from jax.sharding import PartitionSpec as P

D = 2560
FF = 6400
HEADS = 40
QRANK = 768
KVRANK = 256
NOPE = 64
ROPE = 32
VDIM = 64

LANES = 128
LATENT = QRANK + KVRANK + LANES

epsilon = 1e-05
branch_scale = 1.4 / 62**0.5
score_scale = 1.0 / (NOPE + ROPE) ** 0.5
neg_large = -1e30
bfloat = jnp.bfloat16
single = jnp.float32
highest = lax.Precision.HIGHEST


def dot(left, right, left_dim=1, right_dim=0, precision=None):
    return lax.dot_general(
        left,
        right,
        (((left_dim,), (right_dim,)), ((), ())),
        precision=precision,
        preferred_element_type=single,
    )


def normalize(values):
    factor = lax.rsqrt(jnp.mean(values * values, axis=-1, keepdims=True) + epsilon)
    return (values * factor, factor)


def norm_back(grad_scaled, normed, factor):
    return factor * (grad_scaled - normed * jnp.mean(grad_scaled * normed, axis=-1, keepdims=True))


def gather_ctx(values):
    return lax.all_gather(values, "ctx", axis=0, tiled=True)


def scatter_ctx(values):
    return lax.psum_scatter(values, "ctx", scatter_dimension=0, tiled=True)


def exchange_ctx(values):
    return lax.all_to_all(values, "ctx", 0, 0, tiled=True)


def gather_dp(values):
    return lax.all_gather(values, "dp", axis=0, tiled=True)


def scatter_dp(values):
    return lax.psum_scatter(values, "dp", scatter_dimension=0, tiled=True)


def rows_of(ref):
    block = ref[...]
    return block.reshape(block.shape[0] * block.shape[2], block.shape[3])


def store_rows(ref, lanes, values):
    ref[:, :, :, lanes] = values.reshape(ref.shape[0], 1, ref.shape[2], values.shape[-1])


def head_lanes(head):
    return pl.ds(head * LANES, LANES)


def valid_pairs(total, length):
    row = lax.broadcasted_iota(jnp.int32, (total, total), 0)
    col = lax.broadcasted_iota(jnp.int32, (total, total), 1)
    return (col <= row) & (col < length)


def attend_kernel(
    heads, length_ref, latent_ref, query_up_ref, latent_up_ref, table_ref,
    query_ref, kv_ref, attn_ref, total_ref,
):
    latent = rows_of(latent_ref)
    total = latent.shape[0]
    query_normed = latent[:, :QRANK]
    latent_normed = latent[:, QRANK : QRANK + KVRANK]
    rope = latent[:, QRANK + KVRANK :]
    allowed = valid_pairs(total, length_ref[pl.program_id(0)])
    lane = lax.broadcasted_iota(jnp.int32, (total, LANES), 1)
    cosine, sine_low, sine_high = table_ref[0], table_ref[1], table_ref[2]
    totals = jnp.zeros((total, LANES), single)
    held = None
    for head in range(heads):
        full = dot(query_normed, query_up_ref[:, head_lanes(head)])
        query = (
            full * cosine
            + pltpu.roll(full, LANES - ROPE // 2, 1) * sine_low
            + pltpu.roll(full, ROPE // 2, 1) * sine_high
        ).astype(bfloat)
        kv = dot(latent_normed, latent_up_ref[:, head_lanes(head)]).astype(bfloat)
        key = jnp.where(lane < NOPE, kv, rope)
        store_rows(query_ref, head_lanes(head), query)
        store_rows(kv_ref, head_lanes(head), kv)
        scores = dot(query, key, 1, 1) * score_scale
        masked = jnp.where(allowed, scores, neg_large)
        top = jnp.max(masked, axis=-1, keepdims=True)
        exponent = jnp.exp(masked - top)
        weight = jnp.sum(exponent, axis=-1, keepdims=True)
        totals = jnp.where(lane == head, top + jnp.log(weight), totals)
        probs = (exponent * (1.0 / weight)).astype(bfloat)
        out = dot(probs, kv)
        if head % 2 == 0:
            held = pltpu.roll(out, VDIM, 1)
            if head == heads - 1:
                store_rows(attn_ref, pl.ds(head * VDIM, VDIM), held[:, :VDIM].astype(bfloat))
        else:
            pair = jnp.where(lane < VDIM, held, out).astype(bfloat)
            store_rows(attn_ref, pl.ds((head - 1) * VDIM, LANES), pair)
    store_rows(total_ref, pl.ds(0, LANES), totals)


def attend_back_kernel(
    heads, length_ref, query_ref, kv_ref, rope_ref, total_ref, grad_attn_ref, table_ref,
    grad_query_ref, grad_kv_ref, grad_rope_ref,
):
    rope = rows_of(rope_ref)
    total = rope.shape[0]
    totals = rows_of(total_ref)
    allowed = valid_pairs(total, length_ref[pl.program_id(0)])
    lane = lax.broadcasted_iota(jnp.int32, (total, LANES), 1)
    cosine, sine_low, sine_high = table_ref[0], table_ref[1], table_ref[2]
    grad_rope = jnp.zeros((total, LANES), single)
    queries, kvs, grads = rows_of(query_ref), rows_of(kv_ref), rows_of(grad_attn_ref)
    for head in range(heads):
        span = slice(head * LANES, (head + 1) * LANES)
        query, kv, grad_attn = queries[:, span], kvs[:, span], grads[:, span]
        key = jnp.where(lane < NOPE, kv, rope)
        scores = dot(query, key, 1, 1) * score_scale
        probs = jnp.where(allowed, jnp.exp(scores - totals[:, head : head + 1]), 0.0)
        grad_probs = dot(grad_attn, kv, 1, 1)
        delta = jnp.sum(probs * grad_probs, axis=-1, keepdims=True)
        grad_scores = (probs * (grad_probs - delta)).astype(bfloat)
        grad_query = (dot(grad_scores, key) * score_scale).astype(bfloat).astype(single)
        grad_full = (
            grad_query * cosine
            - pltpu.roll(grad_query, LANES - ROPE // 2, 1) * sine_low
            - pltpu.roll(grad_query, ROPE // 2, 1) * sine_high
        )
        store_rows(grad_query_ref, head_lanes(head), grad_full.astype(bfloat))
        grad_key = dot(grad_scores, query, 0, 0) * score_scale
        grad_value = dot(probs.astype(bfloat), grad_attn, 0, 0)
        store_rows(grad_kv_ref, head_lanes(head), jnp.where(lane < NOPE, grad_key, grad_value))
        grad_rope = grad_rope + jnp.where(lane < NOPE, 0.0, grad_key)
    store_rows(grad_rope_ref, pl.ds(0, LANES), grad_rope)


def slot_spec(ctx, span, width, block=0):
    return pl.BlockSpec((ctx, 1, span, width), lambda b: (0, b, 0, block))


def whole_spec(shape):
    return pl.BlockSpec(shape, lambda b: (0,) * len(shape))


def attend(lengths, latent, query_up, latent_up, table, heads):
    ctx, batch, span, _ = latent.shape
    wide = heads * LANES
    shapes = [
        ((ctx, batch, span, wide), bfloat),
        ((ctx, batch, span, wide), bfloat),
        ((ctx, batch, span, heads * VDIM), bfloat),
        ((ctx, batch, span, LANES), single),
    ]
    return pl.pallas_call(
        functools.partial(attend_kernel, heads),
        grid=(batch,),
        out_shape=[jax.ShapeDtypeStruct(*item) for item in shapes],
        in_specs=[
            pl.BlockSpec(memory_space=pltpu.SMEM),
            slot_spec(ctx, span, LATENT),
            whole_spec(query_up.shape),
            whole_spec(latent_up.shape),
            whole_spec(table.shape),
        ],
        out_specs=[slot_spec(ctx, span, item[0][-1]) for item in shapes],
        compiler_params=pltpu.CompilerParams(vmem_limit_bytes=56 << 20),
        name="attend",
    )(lengths, latent, query_up, latent_up, table)


def attend_back(lengths, query, kv, latent, totals, grad_attn, table, heads):
    ctx, batch, span, _ = latent.shape
    wide = heads * LANES
    shapes = [
        ((ctx, batch, span, wide), bfloat),
        ((ctx, batch, span, wide), single),
        ((ctx, batch, span, LANES), single),
    ]
    return pl.pallas_call(
        functools.partial(attend_back_kernel, heads),
        grid=(batch,),
        out_shape=[jax.ShapeDtypeStruct(*item) for item in shapes],
        in_specs=[
            pl.BlockSpec(memory_space=pltpu.SMEM),
            slot_spec(ctx, span, wide),
            slot_spec(ctx, span, wide),
            slot_spec(ctx, span, LANES, (QRANK + KVRANK) // LANES),
            slot_spec(ctx, span, LANES),
            slot_spec(ctx, span, wide),
            whole_spec(table.shape),
        ],
        out_specs=[slot_spec(ctx, span, item[0][-1]) for item in shapes],
        compiler_params=pltpu.CompilerParams(vmem_limit_bytes=56 << 20),
        name="attend_back",
    )(lengths, query, kv, latent, totals, grad_attn, table)


def angles_at(positions):
    freqs = 10000.0 ** (-(2.0 * jnp.arange(ROPE // 2, dtype=single)) / ROPE)
    angles = positions.astype(single)[:, None] * freqs[None, :]
    return (jnp.cos(angles), jnp.sin(angles))


def head_table(total):
    cosine, sine = angles_at(jnp.arange(total, dtype=jnp.int32))
    ones, none = jnp.ones((total, NOPE), single), jnp.zeros((total, NOPE), single)
    tail = jnp.zeros((total, LANES - NOPE - ROPE), single)
    zero = jnp.zeros_like(sine)
    return jnp.stack(
        [
            jnp.concatenate([ones, cosine, cosine, tail], axis=-1),
            jnp.concatenate([none, -sine, zero, tail], axis=-1),
            jnp.concatenate([none, zero, sine, tail], axis=-1),
        ]
    )


def pad_rope(values):
    return jnp.pad(values, ((0, 0), (NOPE, LANES - NOPE - ROPE)))


def on_device(
    dp,
    ctx,
    tokens,
    lengths,
    cotangent,
    input_gain,
    query_gain,
    latent_gain,
    post_gain,
    query_down,
    query_up,
    latent_down,
    latent_up,
    out_proj,
    gate_proj,
    up_proj,
    down_proj,
):
    batch, span, _ = tokens.shape
    own = batch * span
    group = ctx * own
    heads = -(-HEADS // ctx)
    spare = heads * ctx - HEADS
    d_rows, q_rows, l_rows, f_rows = (
        query_down.shape[0], query_up.shape[0], latent_up.shape[0], down_proj.shape[0],
    )
    d_part, f_part = dp * d_rows, dp * f_rows
    place = lax.axis_index("ctx")

    def slices(values):
        return values.reshape(own, dp, ctx, d_rows).transpose(2, 0, 1, 3).reshape(ctx, own, d_part)

    def unslices(values):
        return values.reshape(ctx, own, dp, d_rows).transpose(1, 2, 0, 3).reshape(own, D)

    def columns(values):
        split = values.reshape(d_rows, dp, ctx, f_rows).transpose(2, 0, 1, 3)
        return exchange_ctx(split.reshape(ctx, d_rows, f_part)).reshape(ctx * d_rows, f_part)

    gains = lax.all_gather(
        jnp.concatenate([input_gain, query_gain, latent_gain, post_gain]), ("dp", "ctx"), axis=0
    ).astype(single)
    cuts = (d_rows, d_rows + q_rows, d_rows + q_rows + l_rows)
    gain_in = gains[:, : cuts[0]].reshape(dp, ctx, d_rows)
    gain_in = lax.dynamic_index_in_dim(gain_in, place, 1, keepdims=False).reshape(1, d_part)
    gain_query = gains[:, cuts[0] : cuts[1]].reshape(1, QRANK)
    gain_latent = gains[:, cuts[1] : cuts[2]].reshape(1, KVRANK)
    gain_post = gains[:, cuts[2] :].reshape(1, D)

    down_rows = gather_dp(jnp.concatenate([query_down, latent_down[:, :KVRANK], pad_rope(latent_down[:, KVRANK:])], axis=1))
    up_query = query_up.reshape(q_rows, HEADS, NOPE + ROPE)
    up_query = jnp.pad(up_query, ((0, 0), (0, spare), (0, LANES - NOPE - ROPE)))
    up_latent = jnp.pad(latent_up.reshape(l_rows, HEADS, NOPE + VDIM), ((0, 0), (0, spare), (0, 0)))
    ups = jnp.concatenate([up_query, up_latent], axis=0)
    ups = ups.reshape(q_rows + l_rows, ctx, heads * LANES).transpose(1, 0, 2)
    ups = gather_dp(exchange_ctx(ups)).reshape(dp * ctx, q_rows + l_rows, heads * LANES)
    query_ups = ups[:, :q_rows].reshape(QRANK, heads * LANES)
    latent_ups = ups[:, q_rows:].reshape(KVRANK, heads * LANES)
    out_padded = jnp.pad(out_proj, ((0, 0), (0, spare * VDIM)))
    out_rows = gather_dp(out_padded)
    gate = gather_dp(columns(gate_proj))
    up = gather_dp(columns(up_proj))
    down = gather_dp(down_proj)
    out_heads = out_padded.reshape(d_rows, ctx, heads * VDIM).transpose(1, 0, 2)
    out_heads = gather_dp(exchange_ctx(out_heads).reshape(ctx * d_rows, heads * VDIM))
    out_heads = jnp.pad(out_heads.reshape(D, heads, VDIM), ((0, 0), (0, 0), (NOPE, 0)))
    out_heads = out_heads.reshape(D, heads * LANES)

    flat = tokens.reshape(own, D)
    inputs = flat.astype(single)
    normed_first, factor_first = normalize(inputs)
    factor_all = lax.all_gather(factor_first, "ctx", axis=0, tiled=True)
    token_slices = exchange_ctx(slices(flat)).reshape(group, d_part).astype(single)
    normed_slices = token_slices * factor_all
    normed_in = (normed_slices * gain_in).astype(bfloat)
    latents = scatter_ctx(dot(normed_in, down_rows).astype(bfloat)).astype(single)
    normed_query, factor_query = normalize(latents[:, :QRANK])
    query_normed = (normed_query * gain_query).astype(bfloat)
    normed_latent, factor_latent = normalize(latents[:, QRANK : QRANK + KVRANK])
    latent_normed = (normed_latent * gain_latent).astype(bfloat)
    cosine, sine = angles_at(place * span + jnp.arange(span, dtype=jnp.int32))
    cosine, sine = jnp.tile(cosine, (batch, 1)), jnp.tile(sine, (batch, 1))
    half = QRANK + KVRANK + NOPE + ROPE // 2
    leading, trailing = latents[:, half - ROPE // 2 : half], latents[:, half : half + ROPE // 2]
    key_rope = jnp.concatenate(
        [leading * cosine - trailing * sine, trailing * cosine + leading * sine], axis=-1
    ).astype(bfloat)
    latent_own = jnp.concatenate([query_normed, latent_normed, pad_rope(key_rope)], axis=-1)
    latent_all = gather_ctx(latent_own)

    table = head_table(ctx * span)
    latent_slots = latent_all.reshape(ctx, batch, span, LATENT)
    query, kv, attn, totals = attend(lengths, latent_slots, query_ups, latent_ups, table, heads)
    attn_all = gather_ctx(attn.reshape(1, group, heads * VDIM))
    attn_all = attn_all.transpose(1, 0, 2).reshape(group, ctx * heads * VDIM)
    branch = exchange_ctx(dot(attn_all, out_rows, 1, 1).astype(bfloat).reshape(ctx, own, d_part))
    middle = inputs + branch_scale * unslices(branch).astype(single)
    normed_post, factor_post = normalize(middle)
    normed_mid = gather_ctx((normed_post * gain_post).astype(bfloat))

    grad_out = cotangent.reshape(own, D).astype(single)
    grad_branch = gather_ctx((branch_scale * grad_out).astype(bfloat))
    gate_act = dot(normed_mid, gate)
    up_act = dot(normed_mid, up)
    sigma = jax.nn.sigmoid(gate_act)
    hidden = (gate_act * sigma * up_act).astype(bfloat)
    branch_out = scatter_ctx(dot(hidden, down).astype(bfloat)).astype(single)
    layer_out = (middle + branch_scale * branch_out).astype(bfloat)
    grad_hidden = dot(grad_branch, down, 1, 1)
    grad_gate = (grad_hidden * up_act * (sigma * (1.0 + gate_act * (1.0 - sigma)))).astype(bfloat)
    grad_up = (grad_hidden * (gate_act * sigma)).astype(bfloat)
    grad_normed_mid = dot(grad_gate, gate, 1, 1) + dot(grad_up, up, 1, 1)
    grad_normed_mid = scatter_ctx(grad_normed_mid.astype(bfloat)).astype(single)
    grad_middle = grad_out + norm_back(grad_normed_mid * gain_post, normed_post, factor_post)
    grad_attn_branch = gather_ctx((branch_scale * grad_middle).astype(bfloat))

    grad_attn = dot(grad_attn_branch, out_heads).astype(bfloat)
    grad_query, grad_kv, grad_rope = attend_back(
        lengths, query, kv, latent_slots, totals,
        grad_attn.reshape(ctx, batch, span, heads * LANES), table, heads,
    )
    grad_query = grad_query.reshape(group, heads * LANES)
    grad_kv = grad_kv.reshape(group, heads * LANES)
    grad_latents = jnp.concatenate(
        [
            dot(grad_query, query_ups, 1, 1),
            dot(grad_kv, latent_ups.astype(single), 1, 1, highest),
            grad_rope.reshape(group, LANES),
        ],
        axis=-1,
    )
    grad_latents = scatter_ctx(grad_latents.astype(bfloat)).astype(single)
    grad_query_normed = grad_latents[:, :QRANK]
    grad_latent_normed = grad_latents[:, QRANK : QRANK + KVRANK]
    leading, trailing = (
        grad_latents[:, half - ROPE // 2 : half], grad_latents[:, half : half + ROPE // 2],
    )
    grad_key_rope = jnp.concatenate(
        [leading * cosine + trailing * sine, trailing * cosine - leading * sine], axis=-1
    )
    grad_down = jnp.concatenate(
        [
            norm_back(grad_query_normed * gain_query, normed_query, factor_query),
            norm_back(grad_latent_normed * gain_latent, normed_latent, factor_latent),
            pad_rope(grad_key_rope),
        ],
        axis=-1,
    ).astype(bfloat)
    grad_down = gather_ctx(grad_down)
    grad_normed_in = dot(grad_down, down_rows, 1, 1)
    grad_scaled = exchange_ctx((grad_normed_in * gain_in).astype(bfloat).reshape(ctx, own, d_part))
    input_grad = grad_middle + norm_back(
        unslices(grad_scaled).astype(single), normed_first, factor_first
    )

    grad_down_proj = scatter_dp(dot(hidden, grad_branch, 0, 0).astype(bfloat)).astype(single)

    def owners(values):
        summed = scatter_dp(values.astype(bfloat)).reshape(ctx, d_rows, f_part)
        split = exchange_ctx(summed).reshape(ctx, d_rows, dp, f_rows).transpose(1, 2, 0, 3)
        return split.reshape(d_rows, FF).astype(single)

    grad_gate_proj = owners(dot(normed_mid, grad_gate, 0, 0))
    grad_up_proj = owners(dot(normed_mid, grad_up, 0, 0))
    row = lax.broadcasted_iota(jnp.int32, (D, d_part), 0)
    col = lax.broadcasted_iota(jnp.int32, (D, d_part), 1)
    chosen = (row == (col // d_rows) * (ctx * d_rows) + place * d_rows + col % d_rows).astype(bfloat)
    branch_slices = dot(grad_attn_branch, chosen).astype(bfloat)
    grad_out_proj = dot(branch_slices, attn_all[:, : HEADS * VDIM], 0, 0)
    grad_out_proj = scatter_dp(grad_out_proj.astype(bfloat)).astype(single)
    grad_query_ups = dot(latent_all[:, :QRANK], grad_query, 0, 0)
    grad_latent_ups = dot(
        latent_all[:, QRANK : QRANK + KVRANK].astype(single), grad_kv, 0, 0, highest
    )
    grad_ups = jnp.concatenate(
        [
            grad_query_ups.reshape(dp * ctx, q_rows, heads * LANES),
            grad_latent_ups.reshape(dp * ctx, l_rows, heads * LANES),
        ],
        axis=1,
    )
    grad_ups = exchange_ctx(scatter_dp(grad_ups.astype(bfloat))).transpose(1, 0, 2)
    grad_ups = grad_ups.reshape(q_rows + l_rows, ctx * heads, LANES)[:, :HEADS].astype(single)
    grad_query_up = grad_ups[:q_rows, :, : NOPE + ROPE].reshape(q_rows, HEADS * (NOPE + ROPE))
    grad_latent_up = grad_ups[q_rows:].reshape(l_rows, HEADS * (NOPE + VDIM))

    gain_sums = jnp.concatenate(
        [
            jnp.sum(grad_normed_mid * normed_post, axis=0).reshape(dp * ctx, d_rows),
            jnp.sum(grad_query_normed * normed_query, axis=0).reshape(dp * ctx, q_rows),
            jnp.sum(grad_latent_normed * normed_latent, axis=0).reshape(dp * ctx, l_rows),
        ],
        axis=1,
    )
    gain_sums = lax.psum_scatter(gain_sums, ("dp", "ctx"), scatter_dimension=0, tiled=True)[0]
    grad_rows = dot(normed_in, grad_down, 0, 0)
    last = jnp.sum(grad_normed_in * normed_slices, axis=0)[:, None]
    grad_rows = jnp.concatenate([grad_rows[:, : LATENT - 1], last], axis=1)
    grad_rows = scatter_dp(grad_rows)
    rope_start = QRANK + KVRANK + NOPE
    return (
        layer_out.reshape(batch, span, D),
        input_grad.reshape(batch, span, D),
        grad_rows[:, LATENT - 1],
        gain_sums[d_rows : d_rows + q_rows],
        gain_sums[d_rows + q_rows :],
        gain_sums[:d_rows],
        grad_rows[:, :QRANK],
        grad_query_up,
        jnp.concatenate(
            [grad_rows[:, QRANK : QRANK + KVRANK], grad_rows[:, rope_start : rope_start + ROPE]], axis=1
        ),
        grad_latent_up,
        grad_out_proj,
        grad_gate_proj,
        grad_up_proj,
        grad_down_proj,
    )


def solution(mesh):
    both = ("dp", "ctx")
    tokens, vector, matrix = P("dp", "ctx", None), P(both), P(both, None)
    return jax.shard_map(
        functools.partial(on_device, mesh.shape["dp"], mesh.shape["ctx"]),
        mesh=mesh,
        in_specs=(tokens, P("dp"), tokens) + (vector,) * 4 + (matrix,) * 8,
        out_specs=(tokens, tokens) + (vector,) * 4 + (matrix,) * 8,
        check_vma=False,
    )
```

```python
import functools

import jax
import jax.numpy as jnp
from jax import lax
from jax.experimental import pallas as pl
from jax.experimental.pallas import tpu as pltpu
from jax.sharding import PartitionSpec as P

D = 2560
FF = 6400
HEADS = 40
QRANK = 768
KVRANK = 256
NOPE = 64
ROPE = 32
VDIM = 64

LANES = 128
LATENT = QRANK + KVRANK + LANES

epsilon = 1e-05
branch_scale = 1.4 / 62**0.5
score_scale = 1.0 / (NOPE + ROPE) ** 0.5
neg_large = -1e30
bfloat = jnp.bfloat16
MESH = pl.DeviceIdType.MESH
single = jnp.float32
highest = lax.Precision.HIGHEST


def dot(left, right, left_dim=1, right_dim=0, precision=None):
    return lax.dot_general(
        left,
        right,
        (((left_dim,), (right_dim,)), ((), ())),
        precision=precision,
        preferred_element_type=single,
    )


def normalize(values):
    factor = lax.rsqrt(jnp.mean(values * values, axis=-1, keepdims=True) + epsilon)
    return (values * factor, factor)


def norm_back(grad_scaled, normed, factor):
    return factor * (grad_scaled - normed * jnp.mean(grad_scaled * normed, axis=-1, keepdims=True))


def gather_dp(values):
    return lax.all_gather(values, "dp", axis=0, tiled=True)


def scatter_dp(values):
    return lax.psum_scatter(values, "dp", scatter_dimension=0, tiled=True)


def gather_xla(values):
    return lax.all_gather(values, "ctx", axis=0, tiled=True)


def scatter_xla(values):
    return lax.psum_scatter(values, "ctx", scatter_dimension=0, tiled=True)


def exchange_xla(values):
    return lax.all_to_all(values, "ctx", 0, 0, tiled=True)


class Line:
    def __init__(self, ctx):
        self.pairs = ctx // 2
        self.place = lax.axis_index("ctx")
        self.pair, self.core = self.place // 2, self.place % 2
        self.has_left, self.has_right = self.pair > 0, self.pair < self.pairs - 1
        self.left = {"ctx": jnp.maximum(self.place - 2, 0)}
        self.right = {"ctx": jnp.minimum(self.place + 2, ctx - 1)}
        self.twin = {"ctx": self.place + 1 - 2 * self.core}


def remote(source, target, send, receive, device):
    return pltpu.make_async_remote_copy(
        src_ref=source, dst_ref=target, send_sem=send, recv_sem=receive,
        device_id=device, device_id_type=MESH,
    )


def gather_line(line, own_ref, all_ref, sems):
    send_left, send_right, send_twin, receive, receive_twin, local = sems
    pairs, pair, core = line.pairs, line.pair, line.core

    def to_side(source, slot, sem, device):
        return remote(source, all_ref.at[slot * 2 + core], sem.at[slot], receive.at[slot], device)

    def to_twin(source, slot):
        return remote(source, all_ref.at[slot * 2 + core], send_twin.at[slot], receive_twin.at[slot], line.twin)

    pl.when(line.has_right)(lambda: to_side(own_ref, pair, send_right, line.right).start())
    pl.when(line.has_left)(lambda: to_side(own_ref, pair, send_left, line.left).start())
    to_twin(own_ref, pair).start()
    keep = pltpu.make_async_copy(own_ref, all_ref.at[line.place], local)
    keep.start()
    for step in range(1, pairs):
        def from_left(slot=pair - step):
            block = all_ref.at[slot * 2 + core]
            to_side(block, slot, send_left, line.left).wait_recv()
            pl.when(line.has_right)(lambda: to_side(block, slot, send_right, line.right).start())
            to_twin(block, slot).start()

        def from_right(slot=pair + step):
            block = all_ref.at[slot * 2 + core]
            to_side(block, slot, send_right, line.right).wait_recv()
            pl.when(line.has_left)(lambda: to_side(block, slot, send_left, line.left).start())
            to_twin(block, slot).start()

        pl.when(pair - step >= 0)(from_left)
        pl.when(pair + step < pairs)(from_right)
    keep.wait()
    for slot in range(pairs):
        to_twin(own_ref, slot).wait()
        pl.when((slot <= pair) & line.has_right)(
            lambda slot=slot: to_side(own_ref, slot, send_right, line.right).wait_send())
        pl.when((slot >= pair) & line.has_left)(
            lambda slot=slot: to_side(own_ref, slot, send_left, line.left).wait_send())


def comm_params(collective_id, mebibytes):
    return pltpu.CompilerParams(
        collective_id=collective_id, has_side_effects=True, vmem_limit_bytes=mebibytes << 20
    )


def link_cost(size):
    return pl.CostEstimate(flops=0, transcendentals=0, bytes_accessed=size)


def scatter_line(line, parts_ref, twin_ref, left_ref, right_ref, send_ref, sems):
    send_twin, receive_twin, send_left, send_right, from_left_sem, from_right_sem = sems
    pairs, pair, core = line.pairs, line.pair, line.core

    def to_twin(slot):
        return remote(parts_ref.at[slot * 2 + 1 - core], twin_ref.at[slot], send_twin.at[slot], receive_twin.at[slot], line.twin)

    def to_right(slot):
        return remote(send_ref.at[slot], left_ref.at[slot], send_right.at[slot], from_left_sem.at[slot], line.right)

    def to_left(slot):
        return remote(send_ref.at[slot], right_ref.at[slot], send_left.at[slot], from_right_sem.at[slot], line.left)

    def both_cores(slot):
        return parts_ref[slot * 2 + core].astype(single) + twin_ref[slot].astype(single)

    for step in range(pairs - 1, 0, -1):
        pl.when(pair + step < pairs)(lambda slot=pair + step: to_twin(slot).start())
        pl.when(pair - step >= 0)(lambda slot=pair - step: to_twin(slot).start())
    to_twin(pair).start()
    for step in range(pairs - 1, 0, -1):
        def pass_right(slot=pair + step):
            to_twin(slot).wait_recv()
            send_ref[slot] = both_cores(slot).astype(send_ref.dtype)

            @pl.when(line.has_left)
            def _():
                to_right(slot).wait_recv()
                send_ref[slot] = (both_cores(slot) + left_ref[slot].astype(single)).astype(send_ref.dtype)
            to_right(slot).start()

        def pass_left(slot=pair - step):
            to_twin(slot).wait_recv()
            send_ref[slot] = both_cores(slot).astype(send_ref.dtype)

            @pl.when(line.has_right)
            def _():
                to_left(slot).wait_recv()
                send_ref[slot] = (both_cores(slot) + right_ref[slot].astype(single)).astype(send_ref.dtype)
            to_left(slot).start()

        pl.when(pair + step < pairs)(pass_right)
        pl.when(pair - step >= 0)(pass_left)
    to_twin(pair).wait_recv()


def scatter_total(line, parts_ref, twin_ref, left_ref, right_ref, send_ref, sems, out_ref):
    send_twin, receive_twin, send_left, send_right, from_left_sem, from_right_sem = sems
    pairs, pair, core = line.pairs, line.pair, line.core
    out_ref[...] = parts_ref[pair * 2 + core].astype(single) + twin_ref[pair].astype(single)

    @pl.when(line.has_left)
    def _():
        remote(send_ref.at[pair], left_ref.at[pair], send_right.at[pair], from_left_sem.at[pair], line.right).wait_recv()
        out_ref[...] += left_ref[pair].astype(single)

    @pl.when(line.has_right)
    def _():
        remote(send_ref.at[pair], right_ref.at[pair], send_left.at[pair], from_right_sem.at[pair], line.left).wait_recv()
        out_ref[...] += right_ref[pair].astype(single)

    for slot in range(pairs):
        remote(parts_ref.at[slot], twin_ref.at[slot], send_twin.at[slot], receive_twin.at[slot], line.twin).wait_send()
        pl.when(slot > pair)(lambda slot=slot: remote(
            send_ref.at[slot], left_ref.at[slot], send_right.at[slot], from_left_sem.at[slot], line.right).wait_send())
        pl.when(slot < pair)(lambda slot=slot: remote(
            send_ref.at[slot], right_ref.at[slot], send_left.at[slot], from_right_sem.at[slot], line.left).wait_send())


def gather_sems(ctx):
    return [pltpu.SemaphoreType.DMA((ctx // 2,))] * 5 + [pltpu.SemaphoreType.DMA]


def scatter_scratch(ctx, shape, dtype):
    return [pltpu.VMEM((ctx // 2,) + shape, dtype)] * 4 + [pltpu.SemaphoreType.DMA((ctx // 2,))] * 6


def pair_sems(count):
    return [pltpu.SemaphoreType.DMA((count,))] * 2 + [pltpu.SemaphoreType.DMA]


class ExchangeCtx:
    reach = "ctx"

    def __init__(self, dp, ctx, parts):
        self.count, self.parts = ctx, parts
        self.axis = len(parts.shape) - 3
        shape = parts.shape if not self.axis else (ctx, parts.shape[0]) + parts.shape[2:]
        self.result = jax.ShapeDtypeStruct(shape, parts.dtype)
        self.scratch = pair_sems(ctx)

    def copies(self, source, target, send, receive, local):
        place = lax.axis_index("ctx")

        def part(index):
            return source.at[:, index] if self.axis else source.at[index]

        out = [pltpu.make_async_copy(part(place), target.at[place], local)]
        for step in range(1, self.count):
            other = (place + step) % self.count
            out.append(
                remote(
                    part(other), target.at[place], send.at[step], receive.at[step], {"ctx": other}
                )
            )
        return out


class ExchangeDp:
    reach = "dp"
    whole = False

    def __init__(self, dp, ctx, parts):
        self.count, self.parts = dp, parts
        shape = (dp,) + parts.shape if self.whole else parts.shape
        self.result = jax.ShapeDtypeStruct(shape, parts.dtype)
        self.scratch = pair_sems(dp)

    def copies(self, source, target, send, receive, local):
        row = lax.axis_index("dp")

        def part(index):
            return source if self.whole else source.at[index]

        out = [pltpu.make_async_copy(part(row), target.at[row], local)]
        for step in range(1, self.count):
            other = (row + step) % self.count
            out.append(
                remote(part(other), target.at[row], send.at[step], receive.at[step], {"dp": other})
            )
        return out


class GatherDp(ExchangeDp):
    whole = True


class ExchangeAll:
    reach = "all"
    whole = False

    def __init__(self, dp, ctx, parts):
        self.dp, self.ctx, self.parts = dp, ctx, parts
        shape = (dp, ctx) + parts.shape if self.whole else parts.shape
        self.result = jax.ShapeDtypeStruct(shape, parts.dtype)
        self.scratch = pair_sems(dp * ctx)

    def copies(self, source, target, send, receive, local):
        row, place = lax.axis_index("dp"), lax.axis_index("ctx")

        def part(index):
            return source if self.whole else source.at[index[0], index[1]]

        out = [pltpu.make_async_copy(part((row, place)), target.at[row, place], local)]
        for index, other in enumerate(everyone(self.dp, self.ctx)):
            out.append(
                remote(
                    part(other), target.at[row, place], send.at[index], receive.at[index],
                    {"dp": other[0], "ctx": other[1]},
                )
            )
        return out


class GatherAll(ExchangeAll):
    whole = True


class GatherLine:
    reach = "ctx"

    def __init__(self, dp, ctx, parts):
        self.parts = parts
        self.result = jax.ShapeDtypeStruct((ctx,) + parts.shape, parts.dtype)
        self.scratch = gather_sems(ctx)

    def run(self, line, source, target, *sems):
        gather_line(line, source, target, sems)


class ScatterLine:
    reach = "ctx"

    def __init__(self, dp, ctx, parts):
        self.parts = parts
        self.result = jax.ShapeDtypeStruct(parts.shape[1:], single)
        self.scratch = scatter_scratch(ctx, parts.shape[1:], parts.dtype)

    def run(self, line, source, target, *scratch):
        scatter_line(line, source, *scratch[:4], scratch[4:])
        scatter_total(line, source, *scratch[:4], scratch[4:], target)


class LatentLine:
    reach = "ctx"

    def __init__(self, dp, ctx, parts):
        shape = parts.shape[1:]
        self.parts = parts
        self.result = [
            jax.ShapeDtypeStruct(shape, single), jax.ShapeDtypeStruct(parts.shape, bfloat)
        ]
        self.scratch = [pltpu.VMEM(shape, bfloat)] + scatter_scratch(ctx, shape, bfloat) + gather_sems(ctx)

    def finish_own(self, extra, sums_ref, own_ref):
        gain_ref, table_ref = extra
        for span in (QUERY_SPAN, LATENT_SPAN):
            normed, _ = normalize(sums_ref[:, span])
            own_ref[:, span] = (normed * gain_ref[:, span]).astype(bfloat)
        own_ref[:, ROPE_SPAN] = turn(sums_ref[:, ROPE_SPAN], table_ref, 1.0).astype(bfloat)

    def run(self, line, extra, source, sums_ref, all_ref, own_ref, *scratch):
        scatter_line(line, source, *scratch[:4], scratch[4:10])
        scatter_total(line, source, *scratch[:4], scratch[4:10], sums_ref)
        self.finish_own(extra, sums_ref, own_ref)
        gather_line(line, own_ref, all_ref, scratch[10:])


class LatentBackLine(LatentLine):
    def finish_own(self, extra, sums_ref, own_ref):
        gain_ref, table_ref, latents_ref = extra
        for span in (QUERY_SPAN, LATENT_SPAN):
            normed, factor = normalize(latents_ref[:, span])
            scaled = sums_ref[:, span] * gain_ref[:, span]
            own_ref[:, span] = norm_back(scaled, normed, factor).astype(bfloat)
        own_ref[:, ROPE_SPAN] = turn(sums_ref[:, ROPE_SPAN], table_ref, -1.0).astype(bfloat)


QUERY_SPAN = slice(0, QRANK)
LATENT_SPAN = slice(QRANK, QRANK + KVRANK)
ROPE_SPAN = slice(QRANK + KVRANK, LATENT)


def turn(values, table_ref, sign):
    return (
        values * table_ref[0]
        + sign * pltpu.roll(values, LANES - ROPE // 2, 1) * table_ref[1]
        + sign * pltpu.roll(values, ROPE // 2, 1) * table_ref[2]
    )


def everyone(dp, ctx):
    row, place = lax.axis_index("dp"), lax.axis_index("ctx")
    steps = [(a, b) for a in range(dp) for b in range(ctx) if a or b]
    return [((row + a) % dp, (place + b) % ctx) for a, b in steps]


def greet(dp, ctx, reach):
    row, place = lax.axis_index("dp"), lax.axis_index("ctx")
    if "all" in reach:
        targets = [{"dp": a, "ctx": b} for a, b in everyone(dp, ctx)]
    else:
        targets = []
        if "ctx" in reach:
            targets += [{"ctx": (place + step) % ctx} for step in range(1, ctx)]
        if "dp" in reach:
            targets += [{"dp": (row + step) % dp} for step in range(1, dp)]
    barrier = pltpu.get_barrier_semaphore()
    for target in targets:
        pl.semaphore_signal(barrier, inc=1, device_id=target, device_id_type=MESH)
    pl.semaphore_wait(barrier, len(targets))


def transfer_kernel(dp, ctx, line_piece, direct, extras, *refs):
    refs = list(refs)

    def take(count):
        taken = refs[:count]
        del refs[:count]
        return taken

    line_count = 1 if line_piece else 0
    sources = take(line_count + len(direct))
    extra = take(extras)
    results = [take(len(piece.result)) if isinstance(piece.result, list) else take(1)
               for piece in ([line_piece] if line_piece else []) + direct]
    greet(dp, ctx, [piece.reach for piece in direct] + (["ctx"] if line_piece else []))
    line_scratch = take(len(line_piece.scratch)) if line_piece else []
    copies = []
    for piece, source, result in zip(direct, sources[line_count:], results[line_count:]):
        copies += piece.copies(source, result[0], *take(len(piece.scratch)))
    for copy in copies:
        copy.start()
    if line_piece:
        before = (extra,) if extras else ()
        line_piece.run(Line(ctx), *before, sources[0], *results[0], *line_scratch)
    for copy in copies:
        copy.wait()


def transfer(dp, ctx, collective_id, name, line=None, direct=(), extra=()):
    line_piece = line[0](dp, ctx, line[1]) if line else None
    pieces = [item[0](dp, ctx, item[1]) for item in direct]
    everything = ([line_piece] if line else []) + pieces
    vmem, anywhere = pl.BlockSpec(memory_space=pltpu.VMEM), pl.BlockSpec(memory_space=pl.ANY)
    shapes, out_specs, in_specs, moved = [], [], [], 0
    for piece in everything:
        held = isinstance(piece, (ScatterLine, LatentLine))
        in_specs.append(vmem if held else anywhere)
        results = piece.result if isinstance(piece.result, list) else [piece.result]
        shapes += results
        out_specs += [vmem if held and index == 0 else anywhere for index in range(len(results))]
        moved += piece.parts.size * 2
    out = pl.pallas_call(
        functools.partial(transfer_kernel, dp, ctx, line_piece, pieces, len(extra)),
        out_shape=shapes,
        in_specs=in_specs + [vmem] * len(extra),
        out_specs=out_specs,
        scratch_shapes=[item for piece in everything for item in piece.scratch],
        compiler_params=comm_params(collective_id, 40 if line and line[0] is not GatherLine else 8),
        cost_estimate=link_cost(150 << 20),
        name=name,
    )(*[piece.parts for piece in everything], *extra)
    return out


def rows_of(ref):
    block = ref[...]
    return block.reshape(block.shape[0] * block.shape[2], block.shape[3])


def store_rows(ref, lanes, values):
    ref[:, :, :, lanes] = values.reshape(ref.shape[0], 1, ref.shape[2], values.shape[-1])


def head_lanes(head):
    return pl.ds(head * LANES, LANES)


def valid_pairs(total, length):
    row = lax.broadcasted_iota(jnp.int32, (total, total), 0)
    col = lax.broadcasted_iota(jnp.int32, (total, total), 1)
    return (col <= row) & (col < length)


def attend_kernel(
    heads, length_ref, latent_ref, query_up_ref, latent_up_ref, table_ref,
    query_ref, kv_ref, attn_ref, total_ref,
):
    latent = rows_of(latent_ref)
    total = latent.shape[0]
    query_normed = latent[:, :QRANK]
    latent_normed = latent[:, QRANK : QRANK + KVRANK]
    rope = latent[:, QRANK + KVRANK :]
    allowed = valid_pairs(total, length_ref[pl.program_id(0)])
    lane = lax.broadcasted_iota(jnp.int32, (total, LANES), 1)
    cosine, sine_low, sine_high = table_ref[0], table_ref[1], table_ref[2]
    totals = jnp.zeros((total, LANES), single)
    for head in range(heads):
        full = dot(query_normed, query_up_ref[:, head_lanes(head)])
        query = (
            full * cosine
            + pltpu.roll(full, LANES - ROPE // 2, 1) * sine_low
            + pltpu.roll(full, ROPE // 2, 1) * sine_high
        ).astype(bfloat)
        kv = dot(latent_normed, latent_up_ref[:, head_lanes(head)]).astype(bfloat)
        key = jnp.where(lane < NOPE, kv, rope)
        store_rows(query_ref, head_lanes(head), query)
        store_rows(kv_ref, head_lanes(head), kv)
        scores = dot(query, key, 1, 1) * score_scale
        masked = jnp.where(allowed, scores, neg_large)
        top = jnp.max(masked, axis=-1, keepdims=True)
        exponent = jnp.exp(masked - top)
        weight = jnp.sum(exponent, axis=-1, keepdims=True)
        totals = jnp.where(lane == head, top + jnp.log(weight), totals)
        probs = (exponent * (1.0 / weight)).astype(bfloat)
        out = dot(probs, kv).T[NOPE:]
        attn_ref[head * VDIM : (head + 1) * VDIM] = out.astype(bfloat)
    store_rows(total_ref, pl.ds(0, LANES), totals)


def attend_back_kernel(
    heads, length_ref, query_ref, kv_ref, rope_ref, total_ref, grad_attn_ref, table_ref,
    grad_query_ref, grad_kv_ref, grad_rope_ref,
):
    rope = rows_of(rope_ref)
    total = rope.shape[0]
    totals = rows_of(total_ref)
    allowed = valid_pairs(total, length_ref[pl.program_id(0)])
    lane = lax.broadcasted_iota(jnp.int32, (total, LANES), 1)
    cosine, sine_low, sine_high = table_ref[0], table_ref[1], table_ref[2]
    grad_rope = jnp.zeros((total, LANES), single)
    queries, kvs, grads = rows_of(query_ref), rows_of(kv_ref), rows_of(grad_attn_ref)
    for head in range(heads):
        span = slice(head * LANES, (head + 1) * LANES)
        query, kv, grad_attn = queries[:, span], kvs[:, span], grads[:, span]
        key = jnp.where(lane < NOPE, kv, rope)
        scores = dot(query, key, 1, 1) * score_scale
        probs = jnp.where(allowed, jnp.exp(scores - totals[:, head : head + 1]), 0.0)
        grad_probs = dot(grad_attn, kv, 1, 1)
        delta = jnp.sum(probs * grad_probs, axis=-1, keepdims=True)
        grad_scores = (probs * (grad_probs - delta)).astype(bfloat)
        grad_query = (dot(grad_scores, key) * score_scale).astype(bfloat).astype(single)
        grad_full = (
            grad_query * cosine
            - pltpu.roll(grad_query, LANES - ROPE // 2, 1) * sine_low
            - pltpu.roll(grad_query, ROPE // 2, 1) * sine_high
        )
        store_rows(grad_query_ref, head_lanes(head), grad_full.astype(bfloat))
        grad_key = dot(grad_scores, query, 0, 0) * score_scale
        grad_value = dot(probs.astype(bfloat), grad_attn, 0, 0)
        store_rows(grad_kv_ref, head_lanes(head), jnp.where(lane < NOPE, grad_key, grad_value))
        grad_rope = grad_rope + jnp.where(lane < NOPE, 0.0, grad_key)
    store_rows(grad_rope_ref, pl.ds(0, LANES), grad_rope)


def slot_spec(ctx, span, width, block=0):
    return pl.BlockSpec((ctx, 1, span, width), lambda b: (0, b, 0, block))


def whole_spec(shape):
    return pl.BlockSpec(shape, lambda b: (0,) * len(shape))


def attend(lengths, latent, query_up, latent_up, table, heads):
    ctx, batch, span, _ = latent.shape
    wide = heads * LANES
    shapes = [
        ((ctx, batch, span, wide), bfloat),
        ((ctx, batch, span, wide), bfloat),
        ((heads * VDIM, batch * ctx * span), bfloat),
        ((ctx, batch, span, LANES), single),
    ]
    return pl.pallas_call(
        functools.partial(attend_kernel, heads),
        grid=(batch,),
        out_shape=[jax.ShapeDtypeStruct(*item) for item in shapes],
        in_specs=[
            pl.BlockSpec(memory_space=pltpu.SMEM),
            slot_spec(ctx, span, LATENT),
            whole_spec(query_up.shape),
            whole_spec(latent_up.shape),
            whole_spec(table.shape),
        ],
        out_specs=[
            slot_spec(ctx, span, wide),
            slot_spec(ctx, span, wide),
            pl.BlockSpec((heads * VDIM, ctx * span), lambda b: (0, b)),
            slot_spec(ctx, span, LANES),
        ],
        compiler_params=pltpu.CompilerParams(vmem_limit_bytes=56 << 20),
        name="attend",
    )(lengths, latent, query_up, latent_up, table)


def attend_back(lengths, query, kv, latent, totals, grad_attn, table, heads):
    ctx, batch, span, _ = latent.shape
    wide = heads * LANES
    shapes = [
        ((ctx, batch, span, wide), bfloat),
        ((ctx, batch, span, wide), single),
        ((ctx, batch, span, LANES), single),
    ]
    return pl.pallas_call(
        functools.partial(attend_back_kernel, heads),
        grid=(batch,),
        out_shape=[jax.ShapeDtypeStruct(*item) for item in shapes],
        in_specs=[
            pl.BlockSpec(memory_space=pltpu.SMEM),
            slot_spec(ctx, span, wide),
            slot_spec(ctx, span, wide),
            slot_spec(ctx, span, LANES, (QRANK + KVRANK) // LANES),
            slot_spec(ctx, span, LANES),
            slot_spec(ctx, span, wide),
            whole_spec(table.shape),
        ],
        out_specs=[slot_spec(ctx, span, item[0][-1]) for item in shapes],
        compiler_params=pltpu.CompilerParams(vmem_limit_bytes=56 << 20),
        name="attend_back",
    )(lengths, query, kv, latent, totals, grad_attn, table)


def angles_at(positions):
    freqs = 10000.0 ** (-(2.0 * jnp.arange(ROPE // 2, dtype=single)) / ROPE)
    angles = positions.astype(single)[:, None] * freqs[None, :]
    return (jnp.cos(angles), jnp.sin(angles))


def head_table(positions):
    total = positions.shape[0]
    cosine, sine = angles_at(positions)
    ones, none = jnp.ones((total, NOPE), single), jnp.zeros((total, NOPE), single)
    tail = jnp.zeros((total, LANES - NOPE - ROPE), single)
    zero = jnp.zeros_like(sine)
    return jnp.stack(
        [
            jnp.concatenate([ones, cosine, cosine, tail], axis=-1),
            jnp.concatenate([none, -sine, zero, tail], axis=-1),
            jnp.concatenate([none, zero, sine, tail], axis=-1),
        ]
    )


def pad_rope(values):
    return jnp.pad(values, ((0, 0), (NOPE, LANES - NOPE - ROPE)))


def on_device(
    dp,
    ctx,
    tokens,
    lengths,
    cotangent,
    input_gain,
    query_gain,
    latent_gain,
    post_gain,
    query_down,
    query_up,
    latent_down,
    latent_up,
    out_proj,
    gate_proj,
    up_proj,
    down_proj,
):
    batch, span, _ = tokens.shape
    own = batch * span
    group = ctx * own
    heads = -(-HEADS // ctx)
    spare = heads * ctx - HEADS
    d_rows, q_rows, l_rows, f_rows = (
        query_down.shape[0], query_up.shape[0], latent_up.shape[0], down_proj.shape[0],
    )
    d_part, f_part = dp * d_rows, dp * f_rows
    place = lax.axis_index("ctx")

    def slices(values):
        return values.reshape(own, dp, ctx, d_rows).transpose(2, 0, 1, 3).reshape(ctx, own, d_part)

    def unslices(values):
        return values.reshape(ctx, own, dp, d_rows).transpose(1, 2, 0, 3).reshape(own, D)

    def columns(values):
        split = values.reshape(d_rows, dp, ctx, f_rows).transpose(2, 0, 1, 3)
        return split.reshape(ctx, d_rows, f_part)

    def from_columns(values):
        split = values.reshape(ctx, d_rows, dp, f_rows).transpose(1, 2, 0, 3)
        return split.reshape(d_rows, FF).astype(single)

    def row_sums(values):
        return jnp.sum(values.astype(single), axis=0)

    wide = heads * LANES
    up_rows = q_rows + l_rows
    run = functools.partial(transfer, dp, ctx)

    flat = tokens.reshape(own, D)
    inputs = flat.astype(single)
    normed_first, factor_first = normalize(inputs)
    gains = jnp.concatenate([input_gain, query_gain, latent_gain, post_gain]).astype(single)
    tile = 8 * LANES
    small = jnp.concatenate(
        [jnp.pad(gains, (0, tile - gains.shape[0])), jnp.pad(factor_first[:, 0], (0, tile - own))]
    )
    down_own = jnp.concatenate(
        [query_down, latent_down[:, :KVRANK], pad_rope(latent_down[:, KVRANK:])], axis=1
    )
    up_query = query_up.reshape(q_rows, HEADS, NOPE + ROPE)
    up_query = jnp.pad(up_query, ((0, 0), (0, spare), (0, LANES - NOPE - ROPE)))
    up_latent = jnp.pad(latent_up.reshape(l_rows, HEADS, NOPE + VDIM), ((0, 0), (0, spare), (0, 0)))
    ups = jnp.concatenate([up_query, up_latent], axis=0)
    ups = ups.reshape(up_rows, ctx, wide).transpose(1, 0, 2)
    token_slices, ups, down_rows, smalls = run(
        1, "open",
        direct=[
            (ExchangeCtx, slices(flat)), (ExchangeCtx, ups), (GatherDp, down_own),
            (GatherAll, small.reshape(16, LANES)),
        ],
    )
    gate_proj, up_proj, out_proj, smalls = lax.optimization_barrier(
        (gate_proj, up_proj, out_proj, smalls)
    )
    down_rows = down_rows.reshape(d_part, LATENT)
    smalls = smalls.reshape(dp, ctx, 2 * tile)
    factor_all = smalls[lax.axis_index("dp"), :, tile : tile + own].reshape(group, 1)
    cuts = (d_rows, d_rows + q_rows, d_rows + up_rows, d_rows + up_rows + d_rows)
    gain_in = lax.dynamic_index_in_dim(smalls[:, :, : cuts[0]], place, 1, keepdims=False)
    gain_in = gain_in.reshape(1, d_part)
    gain_query = smalls[:, :, cuts[0] : cuts[1]].reshape(1, QRANK)
    gain_latent = smalls[:, :, cuts[1] : cuts[2]].reshape(1, KVRANK)
    gain_post = smalls[:, :, cuts[2] : cuts[3]].reshape(1, D)
    gain_down = jnp.concatenate([gain_query, gain_latent, jnp.zeros((1, LANES), single)], axis=1)

    out_padded = jnp.pad(out_proj, ((0, 0), (0, spare * VDIM)))
    out_rows = gather_dp(out_padded)
    down = gather_dp(down_proj)
    grad_out = cotangent.reshape(own, D).astype(single)
    grad_branch = gather_xla((branch_scale * grad_out).astype(bfloat))

    normed_slices = token_slices.reshape(group, d_part).astype(single) * factor_all
    normed_in = (normed_slices * gain_in).astype(bfloat)
    own_table = head_table(place * span + jnp.arange(own, dtype=jnp.int32) % span)
    parts = dot(normed_in, down_rows).astype(bfloat).reshape(ctx, own, LATENT)
    out_heads = out_padded.reshape(d_rows, ctx, heads * VDIM).transpose(1, 0, 2)
    latents, latent_all, ups, gate, up, out_heads = run(
        2, "latent_sum", (LatentLine, parts),
        [
            (GatherDp, ups.reshape(ctx * up_rows, wide)), (ExchangeCtx, columns(gate_proj)),
            (ExchangeCtx, columns(up_proj)), (ExchangeCtx, out_heads),
        ],
        (gain_down, own_table),
    )
    ups = ups.reshape(dp * ctx, up_rows, wide)
    query_ups = ups[:, :q_rows].reshape(QRANK, wide)
    latent_ups = ups[:, q_rows:].reshape(KVRANK, wide)

    table = head_table(jnp.arange(ctx * span, dtype=jnp.int32))
    latent_slots = latent_all.reshape(ctx, batch, span, LATENT)
    latent_all = latent_all.reshape(group, LATENT)
    query, kv, attn, totals = attend(lengths, latent_slots, query_ups, latent_ups, table, heads)
    attn_all, gate = run(
        3, "attn_gather", (GatherLine, attn), [(GatherDp, gate.reshape(ctx * d_rows, f_part))]
    )
    attn_all = attn_all.reshape(ctx * heads * VDIM, group)
    gate = gate.reshape(D, f_part)
    branch = dot(attn_all, out_rows, 0, 1).astype(bfloat).reshape(batch, ctx, span, d_part)
    branch, out_heads = run(
        4, "branch_exchange",
        direct=[(ExchangeCtx, branch), (GatherDp, out_heads.reshape(ctx * d_rows, heads * VDIM))],
    )
    out_heads = jnp.pad(out_heads.reshape(D, heads, VDIM), ((0, 0), (0, 0), (NOPE, 0)))
    out_heads = out_heads.reshape(D, wide)
    middle = inputs + branch_scale * unslices(branch.reshape(ctx, own, d_part)).astype(single)
    normed_post, factor_post = normalize(middle)
    normed_mid, up = run(
        5, "mid_gather", (GatherLine, (normed_post * gain_post).astype(bfloat)),
        [(GatherDp, up.reshape(ctx * d_rows, f_part))],
    )
    normed_mid = normed_mid.reshape(group, D)
    up = up.reshape(D, f_part)

    gate_act = dot(normed_mid, gate)
    up_act = dot(normed_mid, up)
    sigma = jax.nn.sigmoid(gate_act)
    hidden = (gate_act * sigma * up_act).astype(bfloat)
    branch_out = scatter_xla(dot(hidden, down).astype(bfloat)).astype(single)
    layer_out = (middle + branch_scale * branch_out).astype(bfloat)
    grad_hidden = dot(grad_branch, down, 1, 1)
    grad_gate = (grad_hidden * up_act * (sigma * (1.0 + gate_act * (1.0 - sigma)))).astype(bfloat)
    grad_up = (grad_hidden * (gate_act * sigma)).astype(bfloat)
    grad_normed_mid = dot(grad_gate, gate, 1, 1) + dot(grad_up, up, 1, 1)
    rows = (dp, ctx * d_rows, f_part)
    grad_normed_mid, grad_gate_proj = run(
        6, "mid_scatter", (ScatterLine, grad_normed_mid.astype(bfloat).reshape(ctx, own, D)),
        [(ExchangeDp, dot(normed_mid, grad_gate, 0, 0).astype(bfloat).reshape(rows))],
    )
    grad_middle = grad_out + norm_back(grad_normed_mid * gain_post, normed_post, factor_post)
    grad_attn_branch, grad_up_proj = run(
        7, "branch_gather", (GatherLine, (branch_scale * grad_middle).astype(bfloat)),
        [(ExchangeDp, dot(normed_mid, grad_up, 0, 0).astype(bfloat).reshape(rows))],
    )
    grad_attn_branch = grad_attn_branch.reshape(group, D)

    grad_attn = dot(grad_attn_branch, out_heads).astype(bfloat)
    grad_query, grad_kv, grad_rope = attend_back(
        lengths, query, kv, latent_slots, totals,
        grad_attn.reshape(ctx, batch, span, wide), table, heads,
    )
    grad_query = grad_query.reshape(group, wide)
    grad_kv = grad_kv.reshape(group, wide)
    grad_latents = jnp.concatenate(
        [
            dot(grad_query, query_ups, 1, 1),
            dot(grad_kv, latent_ups.astype(single), 1, 1, highest),
            grad_rope.reshape(group, LANES),
        ],
        axis=-1,
    ).astype(bfloat)
    grad_query_ups = dot(latent_all[:, :QRANK], grad_query, 0, 0)
    grad_latent_ups = dot(
        latent_all[:, QRANK : QRANK + KVRANK].astype(single), grad_kv, 0, 0, highest
    )
    grad_ups = jnp.concatenate(
        [
            grad_query_ups.reshape(dp * ctx, q_rows, wide),
            grad_latent_ups.reshape(dp * ctx, l_rows, wide),
        ],
        axis=1,
    ).astype(bfloat)
    grad_down_proj = dot(hidden, grad_branch, 0, 0).astype(bfloat).reshape(dp, f_rows, D)
    columns_shape = (ctx, d_rows, f_part)
    grad_latents, grad_down, grad_ups, grad_down_proj, grad_gate_proj, grad_up_proj = run(
        8, "latent_sum_back", (LatentBackLine, grad_latents.reshape(ctx, own, LATENT)),
        [
            (ExchangeDp, grad_ups.reshape(dp, ctx * up_rows, wide)),
            (ExchangeDp, grad_down_proj),
            (ExchangeCtx, row_sums(grad_gate_proj).astype(bfloat).reshape(columns_shape)),
            (ExchangeCtx, row_sums(grad_up_proj).astype(bfloat).reshape(columns_shape)),
        ],
        (gain_down, own_table, latents),
    )
    grad_down = grad_down.reshape(group, LATENT)
    grad_normed_in = dot(grad_down, down_rows, 1, 1)
    grad_scaled = (grad_normed_in * gain_in).astype(bfloat).reshape(ctx, own, d_part)
    grad_rows = dot(normed_in, grad_down, 0, 0)
    last = jnp.sum(grad_normed_in * normed_slices, axis=0)[:, None]
    grad_rows = jnp.concatenate([grad_rows[:, : LATENT - 1], last], axis=1)
    normed_query, _ = normalize(latents[:, :QRANK])
    normed_latent, _ = normalize(latents[:, QRANK : QRANK + KVRANK])
    grad_query_normed = grad_latents[:, :QRANK]
    grad_latent_normed = grad_latents[:, QRANK : QRANK + KVRANK]
    gain_sums = jnp.concatenate(
        [
            jnp.sum(grad_normed_mid * normed_post, axis=0).reshape(dp, ctx, d_rows),
            jnp.sum(grad_query_normed * normed_query, axis=0).reshape(dp, ctx, q_rows),
            jnp.sum(grad_latent_normed * normed_latent, axis=0).reshape(dp, ctx, l_rows),
        ],
        axis=2,
    )
    gain_sums = jnp.pad(gain_sums, ((0, 0), (0, 0), (0, tile - gain_sums.shape[2])))
    row = lax.broadcasted_iota(jnp.int32, (D, d_part), 0)
    col = lax.broadcasted_iota(jnp.int32, (D, d_part), 1)
    chosen = (row == (col // d_rows) * (ctx * d_rows) + place * d_rows + col % d_rows).astype(bfloat)
    branch_slices = dot(grad_attn_branch, chosen).astype(bfloat).reshape(ctx, batch, span, d_part)
    branch_slices = branch_slices.transpose(1, 0, 2, 3).reshape(group, d_part)
    grad_out_proj = dot(branch_slices, attn_all[: HEADS * VDIM], 0, 1).astype(bfloat)
    grad_scaled, grad_rows, grad_out_proj, grad_ups, gain_sums = run(
        9, "close",
        direct=[
            (ExchangeCtx, grad_scaled), (ExchangeDp, grad_rows.reshape(dp, d_rows, LATENT)),
            (ExchangeDp, grad_out_proj.reshape(dp, d_rows, HEADS * VDIM)),
            (ExchangeCtx, row_sums(grad_ups).astype(bfloat).reshape(ctx, up_rows, wide)),
            (ExchangeAll, gain_sums.reshape(dp, ctx, 8, LANES)),
        ],
    )
    input_grad = grad_middle + norm_back(
        unslices(grad_scaled).astype(single), normed_first, factor_first
    )
    grad_rows = jnp.sum(grad_rows, axis=0)
    gain_sums = jnp.sum(gain_sums.reshape(dp * ctx, tile), axis=0)
    grad_ups = grad_ups.transpose(1, 0, 2).reshape(up_rows, ctx * heads, LANES)
    grad_ups = grad_ups[:, :HEADS].astype(single)
    grad_query_up = grad_ups[:q_rows, :, : NOPE + ROPE].reshape(q_rows, HEADS * (NOPE + ROPE))
    grad_latent_up = grad_ups[q_rows:].reshape(l_rows, HEADS * (NOPE + VDIM))
    rope_start = QRANK + KVRANK + NOPE
    return (
        layer_out.reshape(batch, span, D),
        input_grad.reshape(batch, span, D),
        grad_rows[:, LATENT - 1],
        gain_sums[d_rows : d_rows + q_rows],
        gain_sums[d_rows + q_rows : d_rows + up_rows],
        gain_sums[:d_rows],
        grad_rows[:, :QRANK],
        grad_query_up,
        jnp.concatenate(
            [grad_rows[:, QRANK : QRANK + KVRANK], grad_rows[:, rope_start : rope_start + ROPE]], axis=1
        ),
        grad_latent_up,
        row_sums(grad_out_proj),
        from_columns(grad_gate_proj),
        from_columns(grad_up_proj),
        row_sums(grad_down_proj),
    )


def solution(mesh):
    both = ("dp", "ctx")
    tokens, vector, matrix = P("dp", "ctx", None), P(both), P(both, None)
    return jax.shard_map(
        functools.partial(on_device, mesh.shape["dp"], mesh.shape["ctx"]),
        mesh=mesh,
        in_specs=(tokens, P("dp"), tokens) + (vector,) * 4 + (matrix,) * 8,
        out_specs=(tokens, tokens) + (vector,) * 4 + (matrix,) * 8,
        check_vma=False,
    )
```

```python
import functools

import jax
import jax.numpy as jnp
from jax import lax
from jax.experimental import pallas as pl
from jax.experimental.pallas import tpu as pltpu
from jax.sharding import PartitionSpec as P

D = 2560
FF = 6400
HEADS = 40
QRANK = 768
KVRANK = 256
NOPE = 64
ROPE = 32
VDIM = 64

LANES = 128
LATENT = QRANK + KVRANK + LANES

epsilon = 1e-05
branch_scale = 1.4 / 62**0.5
score_scale = 1.0 / (NOPE + ROPE) ** 0.5
neg_large = -1e30
bfloat = jnp.bfloat16
MESH = pl.DeviceIdType.MESH
single = jnp.float32
highest = lax.Precision.HIGHEST


def dot(left, right, left_dim=1, right_dim=0, precision=None):
    return lax.dot_general(
        left,
        right,
        (((left_dim,), (right_dim,)), ((), ())),
        precision=precision,
        preferred_element_type=single,
    )


def normalize(values):
    factor = lax.rsqrt(jnp.mean(values * values, axis=-1, keepdims=True) + epsilon)
    return (values * factor, factor)


def norm_back(grad_scaled, normed, factor):
    return factor * (grad_scaled - normed * jnp.mean(grad_scaled * normed, axis=-1, keepdims=True))


def gather_dp(values):
    return lax.all_gather(values, "dp", axis=0, tiled=True)


def scatter_dp(values):
    return lax.psum_scatter(values, "dp", scatter_dimension=0, tiled=True)


def gather_xla(values):
    return lax.all_gather(values, "ctx", axis=0, tiled=True)


def scatter_xla(values):
    return lax.psum_scatter(values, "ctx", scatter_dimension=0, tiled=True)


def exchange_xla(values):
    return lax.all_to_all(values, "ctx", 0, 0, tiled=True)


class Line:
    def __init__(self, ctx):
        self.pairs = ctx // 2
        self.place = lax.axis_index("ctx")
        self.pair, self.core = self.place // 2, self.place % 2
        self.has_left, self.has_right = self.pair > 0, self.pair < self.pairs - 1
        self.left = {"ctx": jnp.maximum(self.place - 2, 0)}
        self.right = {"ctx": jnp.minimum(self.place + 2, ctx - 1)}
        self.twin = {"ctx": self.place + 1 - 2 * self.core}


def remote(source, target, send, receive, device):
    return pltpu.make_async_remote_copy(
        src_ref=source, dst_ref=target, send_sem=send, recv_sem=receive,
        device_id=device, device_id_type=MESH,
    )


def nothing():
    pass


def gather_line(line, own_ref, all_ref, sems, idle=nothing):
    send_left, send_right, send_twin, receive, receive_twin, local = sems
    pairs, pair, core = line.pairs, line.pair, line.core

    def to_side(source, slot, sem, device):
        return remote(source, all_ref.at[slot * 2 + core], sem.at[slot], receive.at[slot], device)

    def to_twin(source, slot):
        return remote(source, all_ref.at[slot * 2 + core], send_twin.at[slot], receive_twin.at[slot], line.twin)

    pl.when(line.has_right)(lambda: to_side(own_ref, pair, send_right, line.right).start())
    pl.when(line.has_left)(lambda: to_side(own_ref, pair, send_left, line.left).start())
    to_twin(own_ref, pair).start()
    keep = pltpu.make_async_copy(own_ref, all_ref.at[line.place], local)
    keep.start()
    for step in range(1, pairs):
        idle()

        def from_left(slot=pair - step):
            block = all_ref.at[slot * 2 + core]
            to_side(block, slot, send_left, line.left).wait_recv()
            pl.when(line.has_right)(lambda: to_side(block, slot, send_right, line.right).start())
            to_twin(block, slot).start()

        def from_right(slot=pair + step):
            block = all_ref.at[slot * 2 + core]
            to_side(block, slot, send_right, line.right).wait_recv()
            pl.when(line.has_left)(lambda: to_side(block, slot, send_left, line.left).start())
            to_twin(block, slot).start()

        pl.when(pair - step >= 0)(from_left)
        pl.when(pair + step < pairs)(from_right)
    keep.wait()
    for slot in range(pairs):
        to_twin(own_ref, slot).wait()
        pl.when((slot <= pair) & line.has_right)(
            lambda slot=slot: to_side(own_ref, slot, send_right, line.right).wait_send())
        pl.when((slot >= pair) & line.has_left)(
            lambda slot=slot: to_side(own_ref, slot, send_left, line.left).wait_send())


def comm_params(collective_id, mebibytes):
    return pltpu.CompilerParams(
        collective_id=collective_id, has_side_effects=True, vmem_limit_bytes=mebibytes << 20
    )


def link_cost(size):
    return pl.CostEstimate(flops=0, transcendentals=0, bytes_accessed=size)


def scatter_line(line, parts_ref, twin_ref, landed_ref, sems, idle=nothing, make=None):
    send_twin, receive_twin, send_left, send_right, from_left, from_right = sems
    pairs, pair = line.pairs, line.pair
    to_twin, to_right, to_left = travels(line, parts_ref, twin_ref, landed_ref, sems)

    def both_cores(slot):
        return parts_ref[slot * 2 + line.core].astype(single) + twin_ref[slot].astype(single)

    def prepare(order):
        ahead = (pair + pairs - 1 - order) % pairs
        slot = jnp.where(pair < pairs // 2, ahead, (pair + 1 + order) % pairs)
        if make:
            make(slot)
        to_twin(slot).start()

    todo = list(range(pairs))
    for _ in range(2 if make else pairs):
        prepare(todo.pop(0))
    for step in range(pairs - 1, 0, -1):
        idle()

        def pass_on(slot, arrives, travel):
            to_twin(slot).wait_recv()

            @pl.when(arrives)
            def _():
                travel(slot).wait_recv()
                total = both_cores(slot) + landed_ref[slot].astype(single)
                twin_ref[slot] = total.astype(twin_ref.dtype)

            @pl.when(jnp.logical_not(arrives))
            def _():
                twin_ref[slot] = both_cores(slot).astype(twin_ref.dtype)

            travel(slot).start()

        pl.when(pair + step < pairs)(lambda slot=pair + step: pass_on(slot, line.has_left, to_right))
        pl.when(pair - step >= 0)(lambda slot=pair - step: pass_on(slot, line.has_right, to_left))
        if todo:
            prepare(todo.pop(0))
    to_twin(pair).wait_recv()


def travels(line, parts_ref, twin_ref, landed_ref, sems):
    send_twin, receive_twin, send_left, send_right, from_left, from_right = sems
    pairs = line.pairs

    def to_twin(slot):
        source = parts_ref.at[slot * 2 + 1 - line.core]
        return remote(source, twin_ref.at[slot], send_twin.at[slot], receive_twin.at[slot], line.twin)

    def to_right(slot):
        return remote(
            twin_ref.at[slot], landed_ref.at[slot], send_right.at[slot], from_left.at[slot], line.right
        )

    def to_left(slot):
        goal = jnp.where(slot == line.pair - 1, pairs, slot)
        return remote(
            twin_ref.at[slot], landed_ref.at[goal], send_left.at[slot], from_right.at[slot], line.left
        )

    return (to_twin, to_right, to_left)


def scatter_total(line, parts_ref, twin_ref, landed_ref, sems, out_ref):
    pairs, pair = line.pairs, line.pair
    to_twin, to_right, to_left = travels(line, parts_ref, twin_ref, landed_ref, sems)
    out_ref[...] = parts_ref[pair * 2 + line.core].astype(single) + twin_ref[pair].astype(single)

    @pl.when(line.has_left)
    def _():
        to_right(pair).wait_recv()
        out_ref[...] += landed_ref[pair].astype(single)

    @pl.when(line.has_right)
    def _():
        to_left(pair).wait_recv()
        out_ref[...] += landed_ref[pairs].astype(single)

    for slot in range(pairs):
        to_twin(slot).wait_send()
        pl.when(slot > pair)(lambda slot=slot: to_right(slot).wait_send())
        pl.when(slot < pair)(lambda slot=slot: to_left(slot).wait_send())


def gather_sems(ctx):
    return [pltpu.SemaphoreType.DMA((ctx // 2,))] * 5 + [pltpu.SemaphoreType.DMA]


def scatter_scratch(ctx, shape, dtype):
    pairs = ctx // 2
    slots = [pltpu.VMEM((count,) + shape, dtype) for count in (pairs, pairs + 1)]
    return slots + [pltpu.SemaphoreType.DMA((pairs,))] * 6


def pair_sems(count):
    return [pltpu.SemaphoreType.DMA((count,))] * 2 + [pltpu.SemaphoreType.DMA]


class ExchangeCtx:
    reach = "ctx"

    def __init__(self, dp, ctx, parts):
        self.count, self.parts = ctx, parts
        self.axis = len(parts.shape) - 3
        shape = parts.shape if not self.axis else (ctx, parts.shape[0]) + parts.shape[2:]
        self.result = jax.ShapeDtypeStruct(shape, parts.dtype)
        self.scratch = pair_sems(ctx)

    def copies(self, source, target, send, receive, local):
        place = lax.axis_index("ctx")

        def part(index):
            return source.at[:, index] if self.axis else source.at[index]

        out = [pltpu.make_async_copy(part(place), target.at[place], local)]
        for step in range(1, self.count):
            other = (place + step) % self.count
            out.append(
                remote(
                    part(other), target.at[place], send.at[step], receive.at[step], {"ctx": other}
                )
            )
        return out


class ExchangeDp:
    reach = "dp"
    whole = False

    def __init__(self, dp, ctx, parts):
        self.count, self.parts = dp, parts
        shape = (dp,) + parts.shape if self.whole else parts.shape
        self.result = jax.ShapeDtypeStruct(shape, parts.dtype)
        self.scratch = pair_sems(dp)

    def copies(self, source, target, send, receive, local):
        row = lax.axis_index("dp")

        def part(index):
            return source if self.whole else source.at[index]

        out = [pltpu.make_async_copy(part(row), target.at[row], local)]
        for step in range(1, self.count):
            other = (row + step) % self.count
            out.append(
                remote(part(other), target.at[row], send.at[step], receive.at[step], {"dp": other})
            )
        return out


class GatherDp(ExchangeDp):
    whole = True


class ExchangeAll:
    reach = "all"
    whole = False

    def __init__(self, dp, ctx, parts):
        self.dp, self.ctx, self.parts = dp, ctx, parts
        shape = (dp, ctx) + parts.shape if self.whole else parts.shape
        self.result = jax.ShapeDtypeStruct(shape, parts.dtype)
        self.scratch = pair_sems(dp * ctx)

    def copies(self, source, target, send, receive, local):
        row, place = lax.axis_index("dp"), lax.axis_index("ctx")

        def part(index):
            return source if self.whole else source.at[index[0], index[1]]

        out = [pltpu.make_async_copy(part((row, place)), target.at[row, place], local)]
        for index, other in enumerate(everyone(self.dp, self.ctx)):
            out.append(
                remote(
                    part(other), target.at[row, place], send.at[index], receive.at[index],
                    {"dp": other[0], "ctx": other[1]},
                )
            )
        return out


class GatherAll(ExchangeAll):
    whole = True


class GatherLine:
    reach = "ctx"
    held = False
    extra_held = True

    def __init__(self, dp, ctx, parts):
        self.parts = parts
        self.result = [jax.ShapeDtypeStruct((ctx,) + parts.shape, parts.dtype)]
        self.in_vmem = [False]
        self.scratch = gather_sems(ctx)

    def run(self, line, extra, source, results, sems):
        gather_line(line, source, results[0], sems)


class LatentLine:
    reach = "ctx"
    held = True

    def __init__(self, dp, ctx, parts):
        shape = parts.shape[1:]
        self.parts = parts
        self.result = [
            jax.ShapeDtypeStruct(shape, single), jax.ShapeDtypeStruct(parts.shape, bfloat)
        ]
        self.in_vmem = [True, False]
        self.scratch = [pltpu.VMEM(shape, bfloat)] + scatter_scratch(ctx, shape, bfloat) + gather_sems(ctx)

    def finish_own(self, extra, sums_ref, own_ref):
        gain_ref, table_ref = extra
        for span in (QUERY_SPAN, LATENT_SPAN):
            normed, _ = normalize(sums_ref[:, span])
            own_ref[:, span] = (normed * gain_ref[:, span]).astype(bfloat)
        own_ref[:, ROPE_SPAN] = turn(sums_ref[:, ROPE_SPAN], table_ref, 1.0).astype(bfloat)

    def run(self, line, extra, source, results, scratch):
        sums_ref, all_ref = results
        own_ref = scratch[0]
        scatter_line(line, source, *scratch[1:3], scratch[3:9])
        scatter_total(line, source, *scratch[1:3], scratch[3:9], sums_ref)
        self.finish_own(extra, sums_ref, own_ref)
        gather_line(line, own_ref, all_ref, scratch[9:])


class ForwardLine(LatentLine):
    reach = "both"

    def __init__(self, dp, ctx, parts, heads, batch, matrices, ups, out_own, out_heads):
        super().__init__(dp, ctx, parts)
        own = parts.shape[1]
        rows, width = matrices[0].shape
        group, wide = ctx * own, heads * LANES
        self.dp, self.ctx, self.heads, self.batch = dp, ctx, heads, batch
        self.cut = (ctx, rows, width // ctx)
        self.pieces = {
            "gate": ExchangeCtx(dp, ctx, jax.ShapeDtypeStruct(self.cut, bfloat)),
            "up": ExchangeCtx(dp, ctx, jax.ShapeDtypeStruct(self.cut, bfloat)),
            "heads": ExchangeCtx(dp, ctx, out_heads),
            "queries": GatherDp(dp, ctx, ups[0]),
            "latents": GatherDp(dp, ctx, ups[1]),
            "rows": GatherDp(dp, ctx, out_own),
            "gates": GatherDp(dp, ctx, jax.ShapeDtypeStruct(self.cut, bfloat)),
        }
        self.result += [
            jax.ShapeDtypeStruct((ctx, own, wide), bfloat),
            jax.ShapeDtypeStruct((ctx, own, wide), bfloat),
            jax.ShapeDtypeStruct((ctx, own, LANES), single),
            jax.ShapeDtypeStruct((ctx, heads * VDIM, group), bfloat),
        ]
        self.result += [
            self.pieces[name].result for name in ("queries", "latents", "rows", "gates", "up", "heads")
        ]
        self.in_vmem = [True, True, True, True, True, False, True, True] + [False] * 4
        self.base = len(self.scratch)
        self.scratch = self.scratch + [
            pltpu.VMEM((2,) + self.cut, bfloat), pltpu.VMEM(self.cut, bfloat),
            pltpu.VMEM((heads * VDIM, group), bfloat),
        ]
        for piece in self.pieces.values():
            self.scratch = self.scratch + piece.scratch
        self.scratch = self.scratch + gather_sems(ctx)

    def run(self, line, extra, source, results, scratch):
        gain_ref, table_ref, length_ref, slot_table_ref = extra[:4]
        matrices, ups, out_own_ref, out_heads_ref = extra[4:6], extra[6:8], extra[8], extra[9]
        sums_ref, all_ref, query_ref, kv_ref, total_ref, attn_all_ref = results[:6]
        query_ups_ref, latent_ups_ref, rows_ref, gates_ref, up_ref, heads_ref = results[6:]
        cut_ref, gate_ref, attn_ref = scratch[self.base : self.base + 3]
        later = list(scratch[self.base + 3 :])
        ends = {
            "gate": (cut_ref.at[0], gate_ref), "up": (cut_ref.at[1], up_ref),
            "heads": (out_heads_ref, heads_ref), "queries": (ups[0], query_ups_ref),
            "latents": (ups[1], latent_ups_ref), "rows": (out_own_ref, rows_ref),
            "gates": (gate_ref, gates_ref),
        }
        copies = {}
        for name, piece in self.pieces.items():
            copies[name] = piece.copies(*ends[name], *later[: len(piece.scratch)])
            del later[: len(piece.scratch)]

        def start(*names):
            for name in names:
                for copy in copies[name]:
                    copy.start()

        def wait(*names):
            for name in names:
                for copy in copies[name]:
                    copy.wait()

        todo = ["gate", "up"]

        def idle():
            while todo:
                name = todo.pop(0)
                index = 1 - len(todo)
                regroup(matrices[index], cut_ref.at[index], self.dp, self.ctx, True)
                start(name)

        start("queries", "latents", "rows")
        scatter_line(line, source, *scratch[1:3], scratch[3:9], idle)
        scatter_total(line, source, *scratch[1:3], scratch[3:9], sums_ref)
        self.finish_own((gain_ref, table_ref), sums_ref, scratch[0])
        gather_line(line, scratch[0], all_ref, scratch[9 : self.base])
        wait("queries", "latents")
        start("heads")

        def slot(index, carry):
            attend_slot(
                self.heads, index, self.batch, length_ref, all_ref, query_ups_ref, latent_ups_ref,
                slot_table_ref, query_ref, kv_ref, attn_ref, total_ref,
            )
            return carry

        lax.fori_loop(0, self.batch, slot, 0)
        wait("gate")
        start("gates")
        gather_line(line, attn_ref, attn_all_ref, later)
        wait("up", "heads", "rows", "gates")


class BackwardLine(LatentLine):
    reach = "both"

    def __init__(self, dp, ctx, branch, heads, batch, columns):
        own = branch.shape[1]
        parts = jax.ShapeDtypeStruct((ctx, own, LATENT), bfloat)
        super().__init__(dp, ctx, parts)
        self.parts = branch
        self.dp, self.ctx, self.heads, self.batch = dp, ctx, heads, batch
        rows, wide = D // (dp * ctx), heads * LANES
        self.ups = [
            ExchangeDp(dp, ctx, jax.ShapeDtypeStruct((dp, rank // dp, wide), bfloat))
            for rank in (QRANK, KVRANK)
        ]
        self.result += [jax.ShapeDtypeStruct((dp, rows, columns), bfloat)]
        self.result += [piece.result for piece in self.ups]
        self.in_vmem += [True, False, False]
        self.base = len(self.scratch)
        total = ctx * own // batch
        self.scratch = self.scratch + [
            pltpu.VMEM((ctx * own, rows), bfloat), pltpu.VMEM(parts.shape, bfloat),
        ]
        self.scratch = self.scratch + [pltpu.VMEM((total, wide), bfloat)] * 3
        self.scratch = self.scratch + [pltpu.VMEM((rank, wide), single) for rank in (QRANK, KVRANK)]
        self.scratch = self.scratch + [pltpu.VMEM(piece.parts.shape, bfloat) for piece in self.ups]
        for piece in self.ups:
            self.scratch = self.scratch + piece.scratch

    def run(self, line, extra, source, results, scratch):
        branch_ref, attn_ref = source, extra[3]
        parts_ref = scratch[self.base + 1]
        work_refs = scratch[self.base + 2 : self.base + 5]
        sum_refs = scratch[self.base + 5 : self.base + 7]
        send_refs = scratch[self.base + 7 : self.base + 9]
        sems = scratch[self.base + 9 :]
        for ref in sum_refs:
            ref[...] = jnp.zeros_like(ref)

        def slot(index, carry):
            attend_back_slot(
                self.heads, index, self.batch, extra[4], extra[5], extra[6], extra[7], extra[8],
                branch_ref, *extra[9:13], parts_ref, *work_refs, *sum_refs,
            )
            return carry

        lax.fori_loop(0, self.batch, slot, 0)
        copies = []
        for index, piece in enumerate(self.ups):
            send_refs[index][...] = sum_refs[index][...].astype(bfloat).reshape(piece.parts.shape)
            copies += piece.copies(
                send_refs[index], results[3 + index], *sems[3 * index : 3 * index + 3]
            )
        for copy in copies:
            copy.start()
        out_ref, slice_ref = results[2], scratch[self.base]
        rows = D // (self.dp * self.ctx)
        height = D // self.dp
        own = branch_ref.shape[1]
        span = own // self.batch

        def work(index):
            row = lax.broadcasted_iota(jnp.int32, (height, rows), 0)
            col = lax.broadcasted_iota(jnp.int32, (height, rows), 1)
            chosen = (row == line.place * rows + col).astype(single).astype(bfloat)
            block = branch_ref[:, :, index * height : (index + 1) * height]
            picked = dot(block.reshape(self.ctx * own, height), chosen).astype(bfloat)
            for place in range(self.ctx):
                for slot in range(self.batch):
                    start = (place * self.batch + slot) * span
                    goal = (slot * self.ctx + place) * span
                    slice_ref[goal : goal + span] = picked[start : start + span]
            columns = out_ref.shape[2]
            out_ref[index] = dot(slice_ref[...].T, attn_ref[:columns], 1, 1).astype(bfloat)

        todo = list(range(self.dp))

        def idle():
            if todo:
                work(todo.pop(0))

        sums_ref, all_ref = results[:2]
        own_ref = scratch[0]
        scatter_line(line, parts_ref, *scratch[1:3], scratch[3:9], idle)
        scatter_total(line, parts_ref, *scratch[1:3], scratch[3:9], sums_ref)
        self.finish_own(extra[:3], sums_ref, own_ref)
        gather_line(line, own_ref, all_ref, scratch[9 : self.base], idle)
        while todo:
            idle()
        for copy in copies:
            copy.wait()

    def finish_own(self, extra, sums_ref, own_ref):
        gain_ref, table_ref, latents_ref = extra
        for span in (QUERY_SPAN, LATENT_SPAN):
            normed, factor = normalize(latents_ref[:, span])
            scaled = sums_ref[:, span] * gain_ref[:, span]
            own_ref[:, span] = norm_back(scaled, normed, factor).astype(bfloat)
        own_ref[:, ROPE_SPAN] = turn(sums_ref[:, ROPE_SPAN], table_ref, -1.0).astype(bfloat)


class MiddleLine:
    reach = "ctx"
    held = False

    def __init__(self, dp, ctx, parts):
        self.dp, self.ctx, self.parts = dp, ctx, parts
        own, cut = parts.shape[0] * parts.shape[2], parts.shape[3]
        self.result = [
            jax.ShapeDtypeStruct((own, D), single), jax.ShapeDtypeStruct((ctx, own, D), bfloat)
        ]
        self.in_vmem = [True, False]
        self.scratch = (
            [pltpu.VMEM((ctx, parts.shape[0], parts.shape[2], cut), bfloat), pltpu.VMEM((own, D), bfloat)]
            + pair_sems(ctx) + gather_sems(ctx)
        )

    def run(self, line, extra, source, results, scratch):
        tokens_ref, gain_ref = extra
        middle_ref, all_ref = results
        landed_ref, own_ref = scratch[:2]
        copies = ExchangeCtx(self.dp, self.ctx, self.parts).copies(source, landed_ref, *scratch[2:5])
        for copy in copies:
            copy.start()
        for copy in copies:
            copy.wait()
        ungroup(landed_ref, middle_ref, self.dp, self.ctx)

        def chunk(rows):
            middle = tokens_ref[rows].astype(single) + branch_scale * middle_ref[rows]
            middle_ref[rows] = middle
            normed, _ = normalize(middle)
            own_ref[rows] = (normed * gain_ref[...]).astype(bfloat)

        by_chunks(own_ref.shape[0], chunk)
        gather_line(line, own_ref, all_ref, scratch[5:])


class MiddleBackLine:
    reach = "both"
    held = True

    def __init__(self, dp, ctx, parts, shape, f_part, fused):
        self.dp, self.ctx, self.parts, self.fused = dp, ctx, parts, fused
        own = shape[0]
        self.cut = (dp, D // dp, f_part)
        self.f_part = f_part
        self.result = [
            jax.ShapeDtypeStruct(shape, single),
            jax.ShapeDtypeStruct((1, D), single),
            jax.ShapeDtypeStruct((ctx, own, D), bfloat),
            jax.ShapeDtypeStruct((f_part, D), bfloat),
            jax.ShapeDtypeStruct(self.cut, bfloat),
            jax.ShapeDtypeStruct(self.cut, bfloat),
        ]
        self.in_vmem = [True, True, False, True, False, False]
        self.scratch = (
            [pltpu.VMEM(shape, bfloat), pltpu.VMEM((2,) + self.cut, bfloat)]
            + scatter_scratch(ctx, shape, bfloat) + gather_sems(ctx)
            + [pltpu.SemaphoreType.DMA((dp,))] * 4
            + ([pltpu.VMEM((ctx,) + shape, bfloat)] if fused else [])
        )

    def run(self, line, extra, source, results, scratch):
        middle_ref, cotangent_ref, gain_ref, normed_mid_ref, grads, hidden_ref, branch_ref = (
            extra[0], extra[1], extra[2], extra[3], extra[4:6], extra[6], extra[7],
        )
        grad_middle_ref, gain_sum_ref, all_ref, down_ref = results[:4]
        landed = results[4:]
        own_ref, cut_ref = scratch[:2]
        travel, sems = scratch[2:4], scratch[4:10]
        pushes = scratch[16:20]
        row = lax.axis_index("dp")
        height = D // self.dp

        def push(index, target):
            return remote(
                cut_ref.at[index, target], landed[index].at[row],
                pushes[2 * index].at[target], pushes[2 * index + 1].at[row], {"dp": target},
            )

        def keep(index):
            return pltpu.make_async_copy(
                cut_ref.at[index, row], landed[index].at[row], pushes[2 * index].at[row]
            )

        def rows_work(target):
            left = normed_mid_ref[:, target * height : (target + 1) * height].T
            for index in range(2):
                cut_ref[index, target] = dot(left, grads[index][...]).astype(bfloat)

        def send_rows():
            for index in range(2):
                for step in range(1, self.dp):
                    push(index, (row + step) % self.dp).start()
                keep(index).start()

        def down_work(part):
            width = D // 4
            span = slice(part * width, (part + 1) * width)
            down_ref[:, span] = dot(hidden_ref[...].T, branch_ref[:, span]).astype(bfloat)

        todo = [functools.partial(rows_work, target) for target in range(self.dp)]
        todo += [send_rows] + [functools.partial(down_work, part) for part in range(4)]

        def idle(count=2):
            for _ in range(min(count, len(todo))):
                todo.pop(0)()

        parts_ref = scratch[20] if self.fused else source

        def make(slot):
            pair_rows = 2 * own_ref.shape[0]
            rows = pl.ds(pl.multiple_of(slot * pair_rows, pair_rows), pair_rows)
            total = dot(grads[0][rows], source[...], 1, 1) + dot(grads[1][rows], extra[8][...], 1, 1)
            parts_ref[pl.ds(slot * 2, 2)] = total.astype(bfloat).reshape((2,) + own_ref.shape)

        scatter_line(line, parts_ref, *travel, sems, idle, make if self.fused else None)
        scatter_total(line, parts_ref, *travel, sems, grad_middle_ref)
        gain_sum_ref[...] = jnp.zeros_like(gain_sum_ref)

        def chunk(rows):
            normed, factor = normalize(middle_ref[rows])
            gradient = grad_middle_ref[rows]
            gain_sum_ref[...] += jnp.sum(gradient * normed, axis=0, keepdims=True)
            back = cotangent_ref[rows].astype(single) + norm_back(gradient * gain_ref[...], normed, factor)
            grad_middle_ref[rows] = back
            own_ref[rows] = (branch_scale * back).astype(bfloat)

        by_chunks(own_ref.shape[0], chunk)
        gather_line(line, own_ref, all_ref, scratch[10:16], lambda: idle(2))
        idle(len(todo))
        for index in range(2):
            for other in range(self.dp):
                @pl.when(row != other)
                def _():
                    push(index, other).wait_send()
                    remote(
                        cut_ref.at[index, other], landed[index].at[other],
                        pushes[2 * index].at[other], pushes[2 * index + 1].at[other], {"dp": other},
                    ).wait_recv()
            keep(index).wait()


class CloseLine:
    reach = "ctx"
    held = False

    def __init__(self, dp, ctx, parts):
        self.dp, self.ctx, self.parts = dp, ctx, parts
        own = parts.shape[1]
        self.result = [jax.ShapeDtypeStruct((own, D), single)]
        self.in_vmem = [True]
        self.scratch = [pltpu.VMEM(parts.shape, bfloat)] + pair_sems(ctx)

    def lay_out(self, rows, width):
        self.result += [jax.ShapeDtypeStruct((rows, width), single)] * 2
        self.in_vmem += [True] * 2
        return self

    def run(self, line, extra, source, results, scratch):
        tokens_ref, grad_middle_ref = extra[:2]
        out_ref, landed_ref = results[0], scratch[0]
        copies = ExchangeCtx(self.dp, self.ctx, self.parts).copies(source, landed_ref, *scratch[1:4])
        for copy in copies:
            copy.start()
        for index in range(2):
            regroup(extra[2 + index], results[1 + index], self.dp, self.ctx, False)
        for copy in copies:
            copy.wait()
        ungroup(landed_ref, out_ref, self.dp, self.ctx)

        def chunk(rows):
            normed, factor = normalize(tokens_ref[rows].astype(single))
            out_ref[rows] = grad_middle_ref[rows] + norm_back(out_ref[rows], normed, factor)

        by_chunks(out_ref.shape[0], chunk)


def by_chunks(total, work):
    def step(index, carry):
        work(pl.ds(pl.multiple_of(index * 16, 16), 16))
        return carry

    lax.fori_loop(0, total // 16, step, 0)


def regroup(source, target, dp, ctx, forward):
    whole, parts = (source, target) if forward else (target, source)
    width = whole.shape[1] // (dp * ctx)
    for place in range(ctx):
        for row in range(dp):
            start = (row * ctx + place) * width
            wide, narrow = slice(start, start + width), slice(row * width, (row + 1) * width)
            if forward:
                target[place, :, narrow] = source[:, wide]
            else:
                target[:, wide] = source[place, :, narrow].astype(single)


def ungroup(landed_ref, out_ref, dp, ctx):
    width = D // (dp * ctx)
    for place in range(ctx):
        block = landed_ref[place]
        block = block.reshape(out_ref.shape[0], dp * width).astype(single)
        for row in range(dp):
            start = (row * ctx + place) * width
            out_ref[:, start : start + width] = block[:, row * width : (row + 1) * width]


QUERY_SPAN = slice(0, QRANK)
LATENT_SPAN = slice(QRANK, QRANK + KVRANK)
ROPE_SPAN = slice(QRANK + KVRANK, LATENT)


def turn(values, table_ref, sign):
    return (
        values * table_ref[0]
        + sign * pltpu.roll(values, LANES - ROPE // 2, 1) * table_ref[1]
        + sign * pltpu.roll(values, ROPE // 2, 1) * table_ref[2]
    )


def everyone(dp, ctx):
    row, place = lax.axis_index("dp"), lax.axis_index("ctx")
    steps = [(a, b) for a in range(dp) for b in range(ctx) if a or b]
    return [((row + a) % dp, (place + b) % ctx) for a, b in steps]


def greet(dp, ctx, reach):
    row, place = lax.axis_index("dp"), lax.axis_index("ctx")
    if "all" in reach:
        targets = [{"dp": a, "ctx": b} for a, b in everyone(dp, ctx)]
    else:
        targets = []
        if "ctx" in reach:
            targets += [{"ctx": (place + step) % ctx} for step in range(1, ctx)]
        if "dp" in reach:
            targets += [{"dp": (row + step) % dp} for step in range(1, dp)]
    barrier = pltpu.get_barrier_semaphore()
    for target in targets:
        pl.semaphore_signal(barrier, inc=1, device_id=target, device_id_type=MESH)
    pl.semaphore_wait(barrier, len(targets))


def transfer_kernel(dp, ctx, line_piece, direct, extras, *refs):
    refs = list(refs)

    def take(count):
        taken = refs[:count]
        del refs[:count]
        return taken

    line_source = take(1) if line_piece else []
    sources = take(len(direct))
    extra = take(extras)
    line_results = take(len(line_piece.result)) if line_piece else []
    results = take(len(direct))
    line_scratch = take(len(line_piece.scratch)) if line_piece else []
    greet(dp, ctx, [piece.reach for piece in direct] + line_reach(line_piece))
    copies = []
    for piece, source, result in zip(direct, sources, results):
        copies += piece.copies(source, result, *take(len(piece.scratch)))
    for copy in copies:
        copy.start()
    if line_piece:
        line_piece.run(Line(ctx), extra, line_source[0], line_results, line_scratch)
    for copy in copies:
        copy.wait()


def line_reach(line_piece):
    if line_piece is None:
        return []
    return ["ctx", "dp"] if line_piece.reach == "both" else ["ctx"]


def transfer(dp, ctx, collective_id, name, line=None, direct=(), extra=(), mebibytes=8):
    pieces = [item[0](dp, ctx, item[1]) for item in direct]
    vmem, anywhere = pl.BlockSpec(memory_space=pltpu.VMEM), pl.BlockSpec(memory_space=pl.ANY)
    operands, in_specs, shapes, out_specs, scratch = [], [], [], [], []
    if line:
        operands.append(line.parts)
        in_specs.append(vmem if line.held else anywhere)
        shapes += line.result
        out_specs += [vmem if held else anywhere for held in line.in_vmem]
        scratch += line.scratch
    for piece in pieces:
        operands.append(piece.parts)
        in_specs.append(anywhere)
        shapes.append(piece.result)
        out_specs.append(anywhere)
        scratch += piece.scratch
    return pl.pallas_call(
        functools.partial(transfer_kernel, dp, ctx, line, pieces, len(extra)),
        out_shape=shapes,
        in_specs=in_specs + [
            pl.BlockSpec(memory_space=pltpu.SMEM) if item.dtype == jnp.int32 else vmem for item in extra
        ],
        out_specs=out_specs,
        scratch_shapes=scratch,
        compiler_params=comm_params(collective_id, mebibytes),
        cost_estimate=link_cost(150 << 20),
        name=name,
    )(*operands, *extra)


def valid_pairs(total, length):
    row = lax.broadcasted_iota(jnp.int32, (total, total), 0)
    col = lax.broadcasted_iota(jnp.int32, (total, total), 1)
    return (col <= row) & (col < length)


def slot_rows(ref, index, batch):
    span = ref.shape[1] // batch
    block = ref[:, pl.ds(pl.multiple_of(index * span, span), span), :]
    return block.reshape(ref.shape[0] * span, ref.shape[2])


def store_slot(ref, index, batch, lanes, values):
    span = ref.shape[1] // batch
    rows = pl.ds(pl.multiple_of(index * span, span), span)
    ref[:, rows, lanes] = values.reshape(ref.shape[0], span, values.shape[-1])


def attend_slot(
    heads, index, batch, length_ref, latent_ref, query_up_ref, latent_up_ref, table_ref,
    query_ref, kv_ref, attn_ref, total_ref,
):
    wide = heads * LANES
    latent = slot_rows(latent_ref, index, batch)
    total = latent.shape[0]
    query_normed, latent_normed, rope = latent[:, QUERY_SPAN], latent[:, LATENT_SPAN], latent[:, ROPE_SPAN]
    allowed = valid_pairs(total, length_ref[index])
    lane = lax.broadcasted_iota(jnp.int32, (total, LANES), 1)
    totals = jnp.zeros((total, LANES), single)
    query_up = query_up_ref[...].reshape(QRANK, wide)
    latent_up = latent_up_ref[...].reshape(KVRANK, wide)
    columns = pl.ds(pl.multiple_of(index * total, LANES), total)
    for head in range(heads):
        span = slice(head * LANES, (head + 1) * LANES)
        query = turn(dot(query_normed, query_up[:, span]), table_ref, 1.0).astype(bfloat)
        kv = dot(latent_normed, latent_up[:, span]).astype(bfloat)
        key = jnp.where(lane < NOPE, kv, rope)
        store_slot(query_ref, index, batch, span, query)
        store_slot(kv_ref, index, batch, span, kv)
        scores = dot(query, key, 1, 1) * score_scale
        masked = jnp.where(allowed, scores, neg_large)
        top = jnp.max(masked, axis=-1, keepdims=True)
        exponent = jnp.exp(masked - top)
        weight = jnp.sum(exponent, axis=-1, keepdims=True)
        totals = jnp.where(lane == head, top + jnp.log(weight), totals)
        probs = (exponent * (1.0 / weight)).astype(bfloat)
        out = dot(probs, kv).T[NOPE:]
        attn_ref[head * VDIM : (head + 1) * VDIM, columns] = out.astype(bfloat)
    store_slot(total_ref, index, batch, slice(0, LANES), totals)


def attend_back_slot(
    heads, index, batch, length_ref, query_ref, kv_ref, latent_ref, total_ref, branch_ref,
    out_heads_ref, query_up_ref, latent_up_ref, table_ref, parts_ref,
    grad_query_ref, grad_high_ref, grad_low_ref, query_sum_ref, latent_sum_ref,
):
    wide = heads * LANES
    latent = slot_rows(latent_ref, index, batch)
    rope = latent[:, ROPE_SPAN]
    total = rope.shape[0]
    totals = slot_rows(total_ref, index, batch)
    allowed = valid_pairs(total, length_ref[index])
    lane = lax.broadcasted_iota(jnp.int32, (total, LANES), 1)
    grad_rope = jnp.zeros((total, LANES), single)
    queries, kvs = slot_rows(query_ref, index, batch), slot_rows(kv_ref, index, batch)
    grads = dot(slot_rows(branch_ref, index, batch), out_heads_ref[...].reshape(D, heads * VDIM))
    grads = grads.astype(bfloat)
    blank = jnp.zeros((total, NOPE), bfloat)
    for head in range(heads):
        span = slice(head * LANES, (head + 1) * LANES)
        query, kv = queries[:, span], kvs[:, span]
        grad_attn = jnp.concatenate([blank, grads[:, head * VDIM : (head + 1) * VDIM]], axis=1)
        key = jnp.where(lane < NOPE, kv, rope)
        scores = dot(query, key, 1, 1) * score_scale
        probs = jnp.where(allowed, jnp.exp(scores - totals[:, head : head + 1]), 0.0)
        grad_probs = dot(grad_attn, kv, 1, 1)
        delta = jnp.sum(probs * grad_probs, axis=-1, keepdims=True)
        grad_scores = (probs * (grad_probs - delta)).astype(bfloat)
        grad_query = (dot(grad_scores, key) * score_scale).astype(bfloat).astype(single)
        grad_query_ref[:, span] = turn(grad_query, table_ref, -1.0).astype(bfloat)
        grad_key = dot(grad_scores, query, 0, 0) * score_scale
        grad_value = dot(probs.astype(bfloat), grad_attn, 0, 0)
        grad_kv = jnp.where(lane < NOPE, grad_key, grad_value)
        high = grad_kv.astype(bfloat)
        grad_high_ref[:, span] = high
        grad_low_ref[:, span] = (grad_kv - high.astype(single)).astype(bfloat)
        grad_rope = grad_rope + jnp.where(lane < NOPE, 0.0, grad_key)
    grad_query, high, low = grad_query_ref[...], grad_high_ref[...], grad_low_ref[...]
    query_up = query_up_ref[...].reshape(QRANK, wide)
    latent_up = latent_up_ref[...].reshape(KVRANK, wide)
    grad_latent = dot(high, latent_up, 1, 1) + dot(low, latent_up, 1, 1)
    for span, values in (
        (QUERY_SPAN, dot(grad_query, query_up, 1, 1)), (LATENT_SPAN, grad_latent), (ROPE_SPAN, grad_rope),
    ):
        store_slot(parts_ref, index, batch, span, values.astype(bfloat))
    latent_normed = latent[:, LATENT_SPAN]
    query_sum_ref[...] += dot(latent[:, QUERY_SPAN], grad_query, 0, 0)
    latent_sum_ref[...] += dot(latent_normed, high, 0, 0) + dot(latent_normed, low, 0, 0)


def angles_at(positions):
    freqs = 10000.0 ** (-(2.0 * jnp.arange(ROPE // 2, dtype=single)) / ROPE)
    angles = positions.astype(single)[:, None] * freqs[None, :]
    return (jnp.cos(angles), jnp.sin(angles))


def head_table(positions):
    total = positions.shape[0]
    cosine, sine = angles_at(positions)
    ones, none = jnp.ones((total, NOPE), single), jnp.zeros((total, NOPE), single)
    tail = jnp.zeros((total, LANES - NOPE - ROPE), single)
    zero = jnp.zeros_like(sine)
    return jnp.stack(
        [
            jnp.concatenate([ones, cosine, cosine, tail], axis=-1),
            jnp.concatenate([none, -sine, zero, tail], axis=-1),
            jnp.concatenate([none, zero, sine, tail], axis=-1),
        ]
    )


def pad_rope(values):
    return jnp.pad(values, ((0, 0), (NOPE, LANES - NOPE - ROPE)))


def on_device(
    dp,
    ctx,
    tokens,
    lengths,
    cotangent,
    input_gain,
    query_gain,
    latent_gain,
    post_gain,
    query_down,
    query_up,
    latent_down,
    latent_up,
    out_proj,
    gate_proj,
    up_proj,
    down_proj,
):
    batch, span, _ = tokens.shape
    own = batch * span
    group = ctx * own
    heads = -(-HEADS // ctx)
    spare = heads * ctx - HEADS
    d_rows, q_rows, l_rows, f_rows = (
        query_down.shape[0], query_up.shape[0], latent_up.shape[0], down_proj.shape[0],
    )
    d_part, f_part = dp * d_rows, dp * f_rows
    place = lax.axis_index("ctx")

    def slices(values):
        return values.reshape(own, dp, ctx, d_rows).transpose(2, 0, 1, 3).reshape(ctx, own, d_part)

    def row_sums(values):
        return jnp.sum(values.astype(single), axis=0)

    wide = heads * LANES
    up_rows = q_rows + l_rows
    run = functools.partial(transfer, dp, ctx)

    grad_out = cotangent.reshape(own, D).astype(single)
    grad_branch = gather_xla((branch_scale * grad_out).astype(bfloat))

    flat = tokens.reshape(own, D)
    inputs = flat.astype(single)
    normed_first, factor_first = normalize(inputs)
    gains = jnp.concatenate([input_gain, query_gain, latent_gain, post_gain]).astype(single)
    tile = 8 * LANES
    small = jnp.concatenate(
        [jnp.pad(gains, (0, tile - gains.shape[0])), jnp.pad(factor_first[:, 0], (0, tile - own))]
    )
    down_own = jnp.concatenate(
        [query_down, latent_down[:, :KVRANK], pad_rope(latent_down[:, KVRANK:])], axis=1
    )
    up_query = query_up.reshape(q_rows, HEADS, NOPE + ROPE)
    up_query = jnp.pad(up_query, ((0, 0), (0, spare), (0, LANES - NOPE - ROPE)))
    up_latent = jnp.pad(latent_up.reshape(l_rows, HEADS, NOPE + VDIM), ((0, 0), (0, spare), (0, 0)))
    up_query = up_query.reshape(q_rows, ctx, wide).transpose(1, 0, 2)
    up_latent = up_latent.reshape(l_rows, ctx, wide).transpose(1, 0, 2)
    token_slices, up_query, up_latent, down_rows, smalls = run(
        1, "open", None,
        [
            (ExchangeCtx, slices(flat)), (ExchangeCtx, up_query), (ExchangeCtx, up_latent),
            (GatherDp, down_own),
            (GatherAll, small.reshape(16, LANES)),
        ],
    )
    smalls, down_proj = lax.optimization_barrier((smalls, down_proj))
    down_rows = down_rows.reshape(d_part, LATENT)
    smalls = smalls.reshape(dp, ctx, 2 * tile)
    factor_all = smalls[lax.axis_index("dp"), :, tile : tile + own].reshape(group, 1)
    cuts = (d_rows, d_rows + q_rows, d_rows + up_rows, d_rows + up_rows + d_rows)
    gain_in = lax.dynamic_index_in_dim(smalls[:, :, : cuts[0]], place, 1, keepdims=False)
    gain_in = gain_in.reshape(1, d_part)
    gain_query = smalls[:, :, cuts[0] : cuts[1]].reshape(1, QRANK)
    gain_latent = smalls[:, :, cuts[1] : cuts[2]].reshape(1, KVRANK)
    gain_post = smalls[:, :, cuts[2] : cuts[3]].reshape(1, D)
    gain_down = jnp.concatenate([gain_query, gain_latent, jnp.zeros((1, LANES), single)], axis=1)

    out_padded = jnp.pad(out_proj, ((0, 0), (0, spare * VDIM)))
    down = gather_dp(down_proj)

    normed_slices = token_slices.reshape(group, d_part).astype(single) * factor_all
    normed_in = (normed_slices * gain_in).astype(bfloat)
    own_table = head_table(place * span + jnp.arange(own, dtype=jnp.int32) % span)
    parts = dot(normed_in, down_rows).astype(bfloat).reshape(ctx, own, LATENT)
    out_heads = out_padded.reshape(d_rows, ctx, heads * VDIM).transpose(1, 0, 2)
    ups = (up_query.reshape(ctx * q_rows, wide), up_latent.reshape(ctx * l_rows, wide))
    table = head_table(jnp.arange(ctx * span, dtype=jnp.int32))
    outs = run(
        2, "forward",
        ForwardLine(dp, ctx, parts, heads, batch, (gate_proj, up_proj), ups, out_padded, out_heads),
        (),
        (gain_down, own_table, lengths, table, gate_proj, up_proj) + ups + (out_padded, out_heads),
        56,
    )
    latents, latent_all, query, kv, totals, attn_all = outs[:6]
    query_ups, latent_ups, out_rows, gate, up, out_heads = outs[6:]
    attn_all = attn_all.reshape(ctx * heads * VDIM, group)
    gate = gate.reshape(D, f_part)
    branch = dot(attn_all, out_rows.reshape(d_part, ctx * heads * VDIM), 0, 1).astype(bfloat).reshape(batch, ctx, span, d_part)
    middle, normed_mid, out_heads, up = run(
        4, "middle", MiddleLine(dp, ctx, branch),
        [
            (GatherDp, out_heads.reshape(ctx * d_rows, heads * VDIM)),
            (GatherDp, up.reshape(ctx * d_rows, f_part)),
        ],
        (flat, gain_post), 24,
    )
    normed_mid = normed_mid.reshape(group, D)
    up = up.reshape(D, f_part)

    gate_act = dot(normed_mid, gate)
    up_act = dot(normed_mid, up)
    sigma = jax.nn.sigmoid(gate_act)
    hidden = (gate_act * sigma * up_act).astype(bfloat)
    grad_hidden = dot(grad_branch, down, 1, 1)
    grad_gate = (grad_hidden * up_act * (sigma * (1.0 + gate_act * (1.0 - sigma)))).astype(bfloat)
    grad_up = (grad_hidden * (gate_act * sigma)).astype(bfloat)
    fused = group <= 1024
    if fused:
        parts, last = gate, (up,)
    else:
        parts = dot(grad_gate, gate, 1, 1) + dot(grad_up, up, 1, 1)
        parts, last = parts.astype(bfloat).reshape(ctx, own, D), ()
    grad_middle, post_sum, grad_attn_branch, grad_down_proj, grad_gate_proj, grad_up_proj = run(
        5, "middle_back",
        MiddleBackLine(dp, ctx, parts, (own, D), f_part, fused),
        (),
        (
            middle, cotangent.reshape(own, D), gain_post, normed_mid, grad_gate, grad_up, hidden,
            grad_branch,
        ) + last,
        60,
    )
    columns_shape = (ctx, d_rows, f_part)
    grad_gate_proj = row_sums(grad_gate_proj).astype(bfloat).reshape(columns_shape)
    grad_up_proj = row_sums(grad_up_proj).astype(bfloat).reshape(columns_shape)
    branch_out = dot(hidden, down).astype(bfloat)
    branch_out, grad_attn_branch = lax.optimization_barrier((branch_out, grad_attn_branch))
    branch_out = scatter_xla(branch_out).astype(single)
    layer_out = (middle + branch_scale * branch_out).astype(bfloat)

    outs = run(
        8, "backward", BackwardLine(dp, ctx, grad_attn_branch, heads, batch, HEADS * VDIM),
        [
            (ExchangeDp, grad_down_proj.reshape(dp, f_rows, D)), (ExchangeCtx, grad_gate_proj),
            (ExchangeCtx, grad_up_proj),
        ],
        (
            gain_down, own_table, latents, attn_all, lengths, query, kv, latent_all, totals, out_heads,
            query_ups, latent_ups, table,
        ),
        62,
    )
    grad_latents, grad_down, grad_out_proj, grad_query_ups, grad_latent_ups = outs[:5]
    grad_down_proj, grad_gate_proj, grad_up_proj = outs[5:]
    grad_down = grad_down.reshape(group, LATENT)
    grad_normed_in = dot(grad_down, down_rows, 1, 1)
    grad_scaled = (grad_normed_in * gain_in).astype(bfloat).reshape(ctx, own, d_part)
    grad_rows = dot(normed_in, grad_down, 0, 0)
    last = jnp.sum(grad_normed_in * normed_slices, axis=0)[:, None]
    grad_rows = jnp.concatenate([grad_rows[:, : LATENT - 1], last], axis=1)
    normed_query, _ = normalize(latents[:, :QRANK])
    normed_latent, _ = normalize(latents[:, QRANK : QRANK + KVRANK])
    grad_query_normed = grad_latents[:, :QRANK]
    grad_latent_normed = grad_latents[:, QRANK : QRANK + KVRANK]
    gain_sums = jnp.concatenate(
        [
            post_sum.reshape(dp, ctx, d_rows),
            jnp.sum(grad_query_normed * normed_query, axis=0).reshape(dp, ctx, q_rows),
            jnp.sum(grad_latent_normed * normed_latent, axis=0).reshape(dp, ctx, l_rows),
        ],
        axis=2,
    )
    gain_sums = jnp.pad(gain_sums, ((0, 0), (0, 0), (0, tile - gain_sums.shape[2])))
    outs = run(
        9, "close", CloseLine(dp, ctx, grad_scaled).lay_out(d_rows, FF),
        [
            (ExchangeDp, grad_rows.reshape(dp, d_rows, LATENT)),
            (ExchangeDp, grad_out_proj),
            (ExchangeCtx, row_sums(grad_query_ups).astype(bfloat).reshape(ctx, q_rows, wide)),
            (ExchangeCtx, row_sums(grad_latent_ups).astype(bfloat).reshape(ctx, l_rows, wide)),
            (ExchangeAll, gain_sums.reshape(dp, ctx, 8, LANES)),
        ],
        (flat, grad_middle, grad_gate_proj, grad_up_proj),
        32,
    )
    input_grad, grad_gate_proj, grad_up_proj, grad_rows, grad_out_proj = outs[:5]
    grad_query_ups, grad_latent_ups, gain_sums = outs[5:]
    grad_rows = jnp.sum(grad_rows, axis=0)
    gain_sums = jnp.sum(gain_sums.reshape(dp * ctx, tile), axis=0)

    def by_heads(values, rows):
        return values.transpose(1, 0, 2).reshape(rows, ctx * heads, LANES)[:, :HEADS].astype(single)

    grad_query_up = by_heads(grad_query_ups, q_rows)[:, :, : NOPE + ROPE]
    grad_query_up = grad_query_up.reshape(q_rows, HEADS * (NOPE + ROPE))
    grad_latent_up = by_heads(grad_latent_ups, l_rows).reshape(l_rows, HEADS * (NOPE + VDIM))
    rope_start = QRANK + KVRANK + NOPE
    return (
        layer_out.reshape(batch, span, D),
        input_grad.reshape(batch, span, D),
        grad_rows[:, LATENT - 1],
        gain_sums[d_rows : d_rows + q_rows],
        gain_sums[d_rows + q_rows : d_rows + up_rows],
        gain_sums[:d_rows],
        grad_rows[:, :QRANK],
        grad_query_up,
        jnp.concatenate(
            [grad_rows[:, QRANK : QRANK + KVRANK], grad_rows[:, rope_start : rope_start + ROPE]], axis=1
        ),
        grad_latent_up,
        row_sums(grad_out_proj),
        grad_gate_proj,
        grad_up_proj,
        row_sums(grad_down_proj),
    )


def solution(mesh):
    both = ("dp", "ctx")
    tokens, vector, matrix = P("dp", "ctx", None), P(both), P(both, None)
    return jax.shard_map(
        functools.partial(on_device, mesh.shape["dp"], mesh.shape["ctx"]),
        mesh=mesh,
        in_specs=(tokens, P("dp"), tokens) + (vector,) * 4 + (matrix,) * 8,
        out_specs=(tokens, tokens) + (vector,) * 4 + (matrix,) * 8,
        check_vma=False,
    )
```

```python
import functools

import jax
import jax.numpy as jnp
import numpy as np
from jax import lax
from jax.experimental import pallas as pl
from jax.experimental.pallas import tpu as pltpu
from jax.sharding import PartitionSpec as P

D = 2560
FF = 6400
HEADS = 40
QRANK = 768
KVRANK = 256
NOPE = 64
ROPE = 32
VDIM = 64

LANES = 128
LATENT = QRANK + KVRANK + LANES

epsilon = 1e-05
branch_scale = 1.4 / 62**0.5
score_scale = 1.0 / (NOPE + ROPE) ** 0.5
neg_large = -1e30
bfloat = jnp.bfloat16
MESH = pl.DeviceIdType.MESH
single = jnp.float32
highest = lax.Precision.HIGHEST


def dot(left, right, left_dim=1, right_dim=0, precision=None):
    return lax.dot_general(
        left,
        right,
        (((left_dim,), (right_dim,)), ((), ())),
        precision=precision,
        preferred_element_type=single,
    )


def normalize(values):
    factor = lax.rsqrt(jnp.mean(values * values, axis=-1, keepdims=True) + epsilon)
    return (values * factor, factor)


def norm_back(grad_scaled, normed, factor):
    return factor * (grad_scaled - normed * jnp.mean(grad_scaled * normed, axis=-1, keepdims=True))


def gather_xla(values):
    return lax.all_gather(values, "ctx", axis=0, tiled=True)


def scatter_xla(values):
    return lax.psum_scatter(values, "ctx", scatter_dimension=0, tiled=True)


def exchange_xla(values):
    return lax.all_to_all(values, "ctx", 0, 0, tiled=True)


class Line:
    def __init__(self, ctx):
        self.pairs = ctx // 2
        self.place = lax.axis_index("ctx")
        self.pair, self.core = self.place // 2, self.place % 2
        self.has_left, self.has_right = self.pair > 0, self.pair < self.pairs - 1
        self.left = {"ctx": jnp.maximum(self.place - 2, 0)}
        self.right = {"ctx": jnp.minimum(self.place + 2, ctx - 1)}
        self.twin = {"ctx": self.place + 1 - 2 * self.core}


def remote(source, target, send, receive, device):
    return pltpu.make_async_remote_copy(
        src_ref=source, dst_ref=target, send_sem=send, recv_sem=receive,
        device_id=device, device_id_type=MESH,
    )


def nothing():
    pass


def gather_line(line, own_ref, all_ref, sems, idle=nothing, arrived=None):
    send_left, send_right, send_twin, receive, receive_twin, local = sems
    pairs, pair, core = line.pairs, line.pair, line.core

    def to_side(source, slot, sem, device):
        return remote(source, all_ref.at[slot * 2 + core], sem.at[slot], receive.at[slot], device)

    def to_twin(source, slot):
        return remote(source, all_ref.at[slot * 2 + core], send_twin.at[slot], receive_twin.at[slot], line.twin)

    pl.when(line.has_right)(lambda: to_side(own_ref, pair, send_right, line.right).start())
    pl.when(line.has_left)(lambda: to_side(own_ref, pair, send_left, line.left).start())
    to_twin(own_ref, pair).start()
    keep = pltpu.make_async_copy(own_ref, all_ref.at[line.place], local)
    keep.start()
    if arrived:
        keep.wait()
        to_twin(own_ref, pair).wait_recv()
        arrived(pair)
    for step in range(1, pairs):
        idle()

        def from_left(slot=pair - step):
            block = all_ref.at[slot * 2 + core]
            to_side(block, slot, send_left, line.left).wait_recv()
            pl.when(line.has_right)(lambda: to_side(block, slot, send_right, line.right).start())
            to_twin(block, slot).start()

        def from_right(slot=pair + step):
            block = all_ref.at[slot * 2 + core]
            to_side(block, slot, send_right, line.right).wait_recv()
            pl.when(line.has_left)(lambda: to_side(block, slot, send_left, line.left).start())
            to_twin(block, slot).start()

        pl.when(pair - step >= 0)(from_left)
        pl.when(pair + step < pairs)(from_right)
        if arrived:
            slot = nearest(line, step)
            to_twin(own_ref, slot).wait_recv()
            arrived(slot)
    if not arrived:
        keep.wait()
    for slot in range(pairs):
        if arrived:
            to_twin(own_ref, slot).wait_send()
        else:
            to_twin(own_ref, slot).wait()
        pl.when((slot <= pair) & line.has_right)(
            lambda slot=slot: to_side(own_ref, slot, send_right, line.right).wait_send())
        pl.when((slot >= pair) & line.has_left)(
            lambda slot=slot: to_side(own_ref, slot, send_left, line.left).wait_send())


def nearest(line, order):
    shorter = jnp.minimum(line.pair, line.pairs - 1 - line.pair)
    distance = (order + 1) // 2
    both = line.pair + (distance if order % 2 == 0 else -distance)
    ahead = jnp.where(line.pair < line.pairs - 1 - line.pair, order - shorter, shorter - order)
    return jnp.where(order <= 2 * shorter, both, line.pair + ahead)


def comm_params(collective_id, mebibytes):
    return pltpu.CompilerParams(
        collective_id=collective_id, has_side_effects=True, vmem_limit_bytes=mebibytes << 20
    )


def link_cost(size):
    return pl.CostEstimate(flops=0, transcendentals=0, bytes_accessed=size)


def scatter_line(line, parts_ref, twin_ref, landed_ref, sems, idle=nothing, make=None):
    send_twin, receive_twin, send_left, send_right, from_left, from_right = sems
    pairs, pair = line.pairs, line.pair
    to_twin, to_right, to_left = travels(line, parts_ref, twin_ref, landed_ref, sems)

    def both_cores(slot):
        return parts_ref[slot * 2 + line.core].astype(single) + twin_ref[slot].astype(single)

    def prepare(order):
        ahead = (pair + pairs - 1 - order) % pairs
        slot = jnp.where(pair < pairs // 2, ahead, (pair + 1 + order) % pairs)
        if make:
            make(slot)
        to_twin(slot).start()

    todo = list(range(pairs))
    for _ in range(2 if make else pairs):
        prepare(todo.pop(0))
    for step in range(pairs - 1, 0, -1):
        idle()

        def pass_on(slot, arrives, travel):
            to_twin(slot).wait_recv()

            @pl.when(arrives)
            def _():
                travel(slot).wait_recv()
                total = both_cores(slot) + landed_ref[slot].astype(single)
                twin_ref[slot] = total.astype(twin_ref.dtype)

            @pl.when(jnp.logical_not(arrives))
            def _():
                twin_ref[slot] = both_cores(slot).astype(twin_ref.dtype)

            travel(slot).start()

        pl.when(pair + step < pairs)(lambda slot=pair + step: pass_on(slot, line.has_left, to_right))
        pl.when(pair - step >= 0)(lambda slot=pair - step: pass_on(slot, line.has_right, to_left))
        if todo:
            prepare(todo.pop(0))
    to_twin(pair).wait_recv()


def travels(line, parts_ref, twin_ref, landed_ref, sems):
    send_twin, receive_twin, send_left, send_right, from_left, from_right = sems
    pairs = line.pairs

    def to_twin(slot):
        source = parts_ref.at[slot * 2 + 1 - line.core]
        return remote(source, twin_ref.at[slot], send_twin.at[slot], receive_twin.at[slot], line.twin)

    def to_right(slot):
        return remote(
            twin_ref.at[slot], landed_ref.at[slot], send_right.at[slot], from_left.at[slot], line.right
        )

    def to_left(slot):
        goal = jnp.where(slot == line.pair - 1, pairs, slot)
        return remote(
            twin_ref.at[slot], landed_ref.at[goal], send_left.at[slot], from_right.at[slot], line.left
        )

    return (to_twin, to_right, to_left)


def scatter_total(line, parts_ref, twin_ref, landed_ref, sems, out_ref):
    pairs, pair = line.pairs, line.pair
    to_twin, to_right, to_left = travels(line, parts_ref, twin_ref, landed_ref, sems)
    out_ref[...] = parts_ref[pair * 2 + line.core].astype(single) + twin_ref[pair].astype(single)

    @pl.when(line.has_left)
    def _():
        to_right(pair).wait_recv()
        out_ref[...] += landed_ref[pair].astype(single)

    @pl.when(line.has_right)
    def _():
        to_left(pair).wait_recv()
        out_ref[...] += landed_ref[pairs].astype(single)

    for slot in range(pairs):
        to_twin(slot).wait_send()
        pl.when(slot > pair)(lambda slot=slot: to_right(slot).wait_send())
        pl.when(slot < pair)(lambda slot=slot: to_left(slot).wait_send())


def gather_sems(ctx):
    return [pltpu.SemaphoreType.DMA((ctx // 2,))] * 5 + [pltpu.SemaphoreType.DMA]


def scatter_scratch(ctx, shape, dtype):
    pairs = ctx // 2
    slots = [pltpu.VMEM((count,) + shape, dtype) for count in (pairs, pairs + 1)]
    return slots + [pltpu.SemaphoreType.DMA((pairs,))] * 6


def pair_sems(count):
    return [pltpu.SemaphoreType.DMA((count,))] * 2 + [pltpu.SemaphoreType.DMA]


class ExchangeCtx:
    reach = "ctx"

    def __init__(self, dp, ctx, parts):
        self.count, self.parts = ctx, parts
        self.axis = len(parts.shape) - 3
        shape = parts.shape if not self.axis else (ctx, parts.shape[0]) + parts.shape[2:]
        self.result = jax.ShapeDtypeStruct(shape, parts.dtype)
        self.scratch = pair_sems(ctx)

    def copies(self, source, target, send, receive, local):
        place = lax.axis_index("ctx")

        def part(index):
            return source.at[:, index] if self.axis else source.at[index]

        out = [pltpu.make_async_copy(part(place), target.at[place], local)]
        for step in range(1, self.count):
            other = (place + step) % self.count
            out.append(
                remote(
                    part(other), target.at[place], send.at[step], receive.at[step], {"ctx": other}
                )
            )
        return out


class ExchangeDp:
    reach = "dp"
    whole = False

    def __init__(self, dp, ctx, parts):
        self.count, self.parts = dp, parts
        shape = (dp,) + parts.shape if self.whole else parts.shape
        self.result = jax.ShapeDtypeStruct(shape, parts.dtype)
        self.scratch = pair_sems(dp)

    def copies(self, source, target, send, receive, local):
        row = lax.axis_index("dp")

        def part(index):
            return source if self.whole else source.at[index]

        out = [pltpu.make_async_copy(part(row), target.at[row], local)]
        for step in range(1, self.count):
            other = (row + step) % self.count
            out.append(
                remote(part(other), target.at[row], send.at[step], receive.at[step], {"dp": other})
            )
        return out


class GatherDp(ExchangeDp):
    whole = True


class ExchangeAll:
    reach = "all"
    whole = False

    def __init__(self, dp, ctx, parts):
        self.dp, self.ctx, self.parts = dp, ctx, parts
        shape = (dp, ctx) + parts.shape if self.whole else parts.shape
        self.result = jax.ShapeDtypeStruct(shape, parts.dtype)
        self.scratch = pair_sems(dp * ctx)

    def copies(self, source, target, send, receive, local):
        row, place = lax.axis_index("dp"), lax.axis_index("ctx")

        def part(index):
            return source if self.whole else source.at[index[0], index[1]]

        out = [pltpu.make_async_copy(part((row, place)), target.at[row, place], local)]
        for index, other in enumerate(everyone(self.dp, self.ctx)):
            out.append(
                remote(
                    part(other), target.at[row, place], send.at[index], receive.at[index],
                    {"dp": other[0], "ctx": other[1]},
                )
            )
        return out


class GatherAll(ExchangeAll):
    whole = True


class GatherLine:
    reach = "ctx"
    held = False
    extra_held = True

    def __init__(self, dp, ctx, parts):
        self.parts = parts
        self.result = [jax.ShapeDtypeStruct((ctx,) + parts.shape, parts.dtype)]
        self.in_vmem = [False]
        self.scratch = gather_sems(ctx)

    def run(self, line, extra, source, results, sems):
        gather_line(line, source, results[0], sems)


class LatentLine:
    reach = "ctx"
    held = True

    def __init__(self, dp, ctx, parts):
        shape = parts.shape[1:]
        self.parts = parts
        self.result = [
            jax.ShapeDtypeStruct(shape, single), jax.ShapeDtypeStruct(parts.shape, bfloat)
        ]
        self.in_vmem = [True, False]
        self.scratch = [pltpu.VMEM(shape, bfloat)] + scatter_scratch(ctx, shape, bfloat) + gather_sems(ctx)

    def finish_own(self, extra, sums_ref, own_ref):
        gain_ref, table_ref = extra
        for span in (QUERY_SPAN, LATENT_SPAN):
            normed, _ = normalize(sums_ref[:, span])
            own_ref[:, span] = (normed * gain_ref[:, span]).astype(bfloat)
        own_ref[:, ROPE_SPAN] = turn(sums_ref[:, ROPE_SPAN], table_ref, 1.0).astype(bfloat)

    def run(self, line, extra, source, results, scratch):
        sums_ref, all_ref = results
        own_ref = scratch[0]
        scatter_line(line, source, *scratch[1:3], scratch[3:9])
        scatter_total(line, source, *scratch[1:3], scratch[3:9], sums_ref)
        self.finish_own(extra, sums_ref, own_ref)
        gather_line(line, own_ref, all_ref, scratch[9:])


class OpenLine:
    reach = "ctx"
    held = True

    def __init__(self, dp, ctx, parts):
        self.dp, self.ctx, self.parts = dp, ctx, parts
        rows, width = parts.shape
        self.cut = jax.ShapeDtypeStruct((ctx, rows, width // ctx), bfloat)
        self.result = [self.cut] * 2
        self.in_vmem = [False] * 2
        self.scratch = [pltpu.VMEM((2,) + self.cut.shape, bfloat)] + pair_sems(ctx) * 2

    def run(self, line, extra, source, results, scratch):
        cut_ref, copies = scratch[0], []
        for index, matrix in enumerate((source, extra[0])):
            regroup(matrix, cut_ref.at[index], self.dp, self.ctx, True)
            sems = scratch[1 + 3 * index : 4 + 3 * index]
            pieces = ExchangeCtx(self.dp, self.ctx, self.cut).copies(cut_ref.at[index], results[index], *sems)
            for copy in pieces:
                copy.start()
            copies += pieces
        for copy in copies:
            copy.wait()


class ForwardLine(LatentLine):
    reach = "both"

    def __init__(self, dp, ctx, parts, heads, batch, matrices, ups, out_heads):
        super().__init__(dp, ctx, parts)
        own = parts.shape[1]
        group, wide = ctx * own, heads * LANES
        self.dp, self.ctx, self.heads, self.batch = dp, ctx, heads, batch
        self.pieces = {
            "heads": ExchangeCtx(dp, ctx, out_heads),
            "queries": GatherDp(dp, ctx, ups[0]),
            "latents": GatherDp(dp, ctx, ups[1]),
            "gates": GatherDp(dp, ctx, matrices[0]),
            "ups": GatherDp(dp, ctx, matrices[1]),
        }
        self.elsewhere = (4, 5)
        self.result += [
            jax.ShapeDtypeStruct((ctx, own, wide), bfloat),
            jax.ShapeDtypeStruct((ctx, own, wide), bfloat),
            jax.ShapeDtypeStruct((ctx, own, LANES), single),
            jax.ShapeDtypeStruct((ctx, heads * VDIM, group), bfloat),
        ]
        self.result += [
            self.pieces[name].result for name in ("queries", "latents", "gates", "ups", "heads")
        ]
        self.in_vmem = [True, True, True, True, True, False, True, True] + [False] * 3
        self.base = len(self.scratch)
        self.scratch = self.scratch + [pltpu.VMEM((heads * VDIM, group), bfloat)]
        for piece in self.pieces.values():
            self.scratch = self.scratch + piece.scratch
        self.scratch = self.scratch + gather_sems(ctx)

    def run(self, line, extra, source, results, scratch):
        gain_ref, table_ref, length_ref, slot_table_ref = extra[:4]
        matrices, ups, out_heads_ref = extra[4:6], extra[6:8], extra[8]
        sums_ref, all_ref, query_ref, kv_ref, total_ref, attn_all_ref = results[:6]
        query_ups_ref, latent_ups_ref, gates_ref, ups_ref, heads_ref = results[6:]
        attn_ref = scratch[self.base]
        later = list(scratch[self.base + 1 :])
        ends = {
            "heads": (out_heads_ref, heads_ref), "queries": (ups[0], query_ups_ref),
            "latents": (ups[1], latent_ups_ref),
            "gates": (matrices[0], gates_ref), "ups": (matrices[1], ups_ref),
        }
        copies = {}
        for name, piece in self.pieces.items():
            copies[name] = piece.copies(*ends[name], *later[: len(piece.scratch)])
            del later[: len(piece.scratch)]

        def start(*names):
            for name in names:
                for copy in copies[name]:
                    copy.start()

        def wait(*names):
            for name in names:
                for copy in copies[name]:
                    copy.wait()

        start("queries", "latents", "gates", "ups")
        scatter_line(line, source, *scratch[1:3], scratch[3:9])
        scatter_total(line, source, *scratch[1:3], scratch[3:9], sums_ref)
        self.finish_own((gain_ref, table_ref), sums_ref, scratch[0])
        gather_line(line, scratch[0], all_ref, scratch[9 : self.base])
        wait("queries", "latents")
        start("heads")

        def slot(index, carry):
            attend_slot(
                self.heads, index, self.batch, length_ref, all_ref, query_ups_ref, latent_ups_ref,
                slot_table_ref, query_ref, kv_ref, attn_ref, total_ref,
            )
            return carry

        lax.fori_loop(0, self.batch, slot, 0)
        gather_line(line, attn_ref, attn_all_ref, later)
        wait("heads", "gates", "ups")


class BackwardLine(LatentLine):
    reach = "both"

    def __init__(self, dp, ctx, branch, heads, batch, columns):
        own = branch.shape[1]
        parts = jax.ShapeDtypeStruct((ctx, own, LATENT), bfloat)
        super().__init__(dp, ctx, parts)
        self.parts = branch
        self.dp, self.ctx, self.heads, self.batch = dp, ctx, heads, batch
        rows, wide = D // (dp * ctx), heads * LANES
        self.ups = [
            ExchangeDp(dp, ctx, jax.ShapeDtypeStruct((dp, rank // dp, wide), bfloat))
            for rank in (QRANK, KVRANK)
        ]
        self.out = ExchangeDp(dp, ctx, jax.ShapeDtypeStruct((dp, rows, columns), bfloat))
        self.result += [self.out.result]
        self.result += [piece.result for piece in self.ups]
        self.in_vmem += [False, False, False]
        self.base = len(self.scratch)
        total = ctx * own // batch
        self.scratch = self.scratch + [
            pltpu.VMEM((ctx * own, rows), bfloat), pltpu.VMEM(parts.shape, bfloat),
        ]
        self.scratch = self.scratch + [pltpu.VMEM((total, wide), bfloat)] * 3
        self.scratch = self.scratch + [pltpu.VMEM((rank, wide), single) for rank in (QRANK, KVRANK)]
        self.scratch = self.scratch + [pltpu.VMEM(piece.parts.shape, bfloat) for piece in self.ups]
        for piece in self.ups + [self.out]:
            self.scratch = self.scratch + piece.scratch
        self.scratch = self.scratch + [pltpu.VMEM(self.out.parts.shape, bfloat)]

    def run(self, line, extra, source, results, scratch):
        branch_ref, attn_ref = source, extra[3]
        parts_ref = scratch[self.base + 1]
        work_refs = scratch[self.base + 2 : self.base + 5]
        sum_refs = scratch[self.base + 5 : self.base + 7]
        send_refs = scratch[self.base + 7 : self.base + 9]
        sems = scratch[self.base + 9 :]
        for ref in sum_refs:
            ref[...] = jnp.zeros_like(ref)

        def slot(index, carry):
            attend_back_slot(
                self.heads, index, self.batch, extra[4], extra[5], extra[6], extra[7], extra[8],
                branch_ref, *extra[9:13], parts_ref, *work_refs, *sum_refs,
            )
            return carry

        lax.fori_loop(0, self.batch, slot, 0)
        copies = []
        for index, piece in enumerate(self.ups):
            send_refs[index][...] = sum_refs[index][...].astype(bfloat).reshape(piece.parts.shape)
            copies += piece.copies(
                send_refs[index], results[3 + index], *sems[3 * index : 3 * index + 3]
            )
        for copy in copies:
            copy.start()
        out_ref, slice_ref = scratch[-1], scratch[self.base]
        out_copies = self.out.copies(out_ref, results[2], *scratch[-4:-1])
        rows = D // (self.dp * self.ctx)
        height = D // self.dp
        own = branch_ref.shape[1]
        span = own // self.batch

        def work(index):
            row = lax.broadcasted_iota(jnp.int32, (height, rows), 0)
            col = lax.broadcasted_iota(jnp.int32, (height, rows), 1)
            chosen = (row == line.place * rows + col).astype(single).astype(bfloat)
            block = branch_ref[:, :, index * height : (index + 1) * height]
            picked = dot(block.reshape(self.ctx * own, height), chosen).astype(bfloat)
            for place in range(self.ctx):
                for slot in range(self.batch):
                    start = (place * self.batch + slot) * span
                    goal = (slot * self.ctx + place) * span
                    slice_ref[goal : goal + span] = picked[start : start + span]
            columns = out_ref.shape[2]
            out_ref[index] = dot(slice_ref[...].T, attn_ref[:columns], 1, 1).astype(bfloat)

        todo = list(range(self.dp))

        def idle():
            if todo:
                work(todo.pop(0))
                if not todo:
                    for copy in out_copies:
                        copy.start()

        sums_ref, all_ref = results[:2]
        own_ref = scratch[0]
        scatter_line(line, parts_ref, *scratch[1:3], scratch[3:9], idle)
        scatter_total(line, parts_ref, *scratch[1:3], scratch[3:9], sums_ref)
        self.finish_own(extra[:3], sums_ref, own_ref)
        gather_line(line, own_ref, all_ref, scratch[9 : self.base], idle)
        while todo:
            idle()
        for copy in copies + out_copies:
            copy.wait()

    def finish_own(self, extra, sums_ref, own_ref):
        gain_ref, table_ref, latents_ref = extra
        for span in (QUERY_SPAN, LATENT_SPAN):
            normed, factor = normalize(latents_ref[:, span])
            scaled = sums_ref[:, span] * gain_ref[:, span]
            own_ref[:, span] = norm_back(scaled, normed, factor).astype(bfloat)
        own_ref[:, ROPE_SPAN] = turn(sums_ref[:, ROPE_SPAN], table_ref, -1.0).astype(bfloat)


class MiddleLine:
    reach = "ctx"
    held = False

    def __init__(self, dp, ctx, parts, f_part):
        self.dp, self.ctx, self.parts = dp, ctx, parts
        own, cut = parts.shape[0] * parts.shape[2], parts.shape[3]
        group = ctx * own
        self.result = [
            jax.ShapeDtypeStruct((own, D), single), jax.ShapeDtypeStruct((ctx, own, D), bfloat),
            jax.ShapeDtypeStruct((ctx, own, D), bfloat),
        ]
        self.result += [jax.ShapeDtypeStruct((group, f_part), bfloat)] * 3
        self.in_vmem = [True] + [False] * 5
        self.scratch = (
            [pltpu.VMEM((ctx, parts.shape[0], parts.shape[2], cut), bfloat), pltpu.VMEM((own, D), bfloat)]
            + pair_sems(ctx) + gather_sems(ctx)
        )
        self.base = len(self.scratch)
        self.scratch = self.scratch + [pltpu.VMEM((ctx, own, D), bfloat)] * 2
        self.scratch = self.scratch + [pltpu.VMEM((group, f_part), bfloat)] * 3
        self.scratch = self.scratch + [pltpu.SemaphoreType.DMA((ctx // 2,))] * 5
        shapes = [(D, f_part), (D, f_part), (f_part, D), (group, D)]
        self.scratch = self.scratch + [pltpu.VMEM(shape, bfloat) for shape in shapes]
        self.scratch = self.scratch + [pltpu.SemaphoreType.DMA] * 4
        self.elsewhere = (2, 3, 4, 5)

    def run(self, line, extra, source, results, scratch):
        tokens_ref, gain_ref = extra[:2]
        middle_ref = results[0]
        landed_ref, own_ref = scratch[:2]
        kept = scratch[self.base : self.base + 5]
        kept_sems = scratch[self.base + 5 : self.base + 10]
        weights = scratch[self.base + 10 : self.base + 14]
        all_ref, branch_out_ref, hidden_ref, grad_gate_ref, grad_up_ref = kept
        gate_ref, up_ref, down_ref, branch_ref = weights
        loads = [
            pltpu.make_async_copy(extra[2 + index], ref, scratch[self.base + 14 + index])
            for index, ref in enumerate(weights)
        ]
        copies = ExchangeCtx(self.dp, self.ctx, self.parts).copies(source, landed_ref, *scratch[2:5])
        for copy in copies + loads:
            copy.start()
        for copy in copies:
            copy.wait()
        ungroup(landed_ref, middle_ref, self.dp, self.ctx)

        def chunk(rows):
            middle = tokens_ref[rows].astype(single) + branch_scale * middle_ref[rows]
            middle_ref[rows] = middle
            normed, _ = normalize(middle)
            own_ref[rows] = (normed * gain_ref[...]).astype(bfloat)

        by_chunks(own_ref.shape[0], chunk)
        todo = list(loads)

        def out_copies(slot):
            height = 2 * own_ref.shape[0]
            for index, (ref, sem) in enumerate(zip(kept, kept_sems)):
                rows = pl.ds(slot * 2, 2) if index < 2 else pl.ds(slot * height, height)
                yield pltpu.make_async_copy(ref.at[rows], results[1 + index].at[rows], sem.at[slot])

        def arrived(slot):
            while todo:
                todo.pop(0).wait()
            height = 2 * own_ref.shape[0]
            rows = pl.ds(pl.multiple_of(slot * height, height), height)
            normed = all_ref[pl.ds(slot * 2, 2)].reshape(height, D)
            gate_act = dot(normed, gate_ref[...])
            up_act = dot(normed, up_ref[...])
            grad_hidden = dot(branch_ref[rows], down_ref[...], 1, 1)
            sigma = jax.nn.sigmoid(gate_act)
            silu = gate_act * sigma
            hidden = (silu * up_act).astype(bfloat)
            hidden_ref[rows] = hidden
            slope = sigma * (1.0 + gate_act * (1.0 - sigma))
            grad_gate_ref[rows] = (grad_hidden * up_act * slope).astype(bfloat)
            grad_up_ref[rows] = (grad_hidden * silu).astype(bfloat)
            out = dot(hidden, down_ref[...]).astype(bfloat)
            branch_out_ref[pl.ds(slot * 2, 2)] = out.reshape((2,) + own_ref.shape)
            for copy in out_copies(slot):
                copy.start()

        gather_line(line, own_ref, all_ref, scratch[5:self.base], arrived=arrived)
        for slot in range(line.pairs):
            for copy in out_copies(slot):
                copy.wait()


class MiddleBackLine:
    reach = "both"
    held = True

    def __init__(self, dp, ctx, parts, shape, f_part, fused):
        self.dp, self.ctx, self.parts, self.fused = dp, ctx, parts, fused
        own = shape[0]
        self.cut = (dp, D // dp, f_part)
        self.f_part = f_part
        self.result = [
            jax.ShapeDtypeStruct(shape, single),
            jax.ShapeDtypeStruct((1, D), single),
            jax.ShapeDtypeStruct((ctx, own, D), bfloat),
            jax.ShapeDtypeStruct((f_part, D), bfloat),
            jax.ShapeDtypeStruct(self.cut, bfloat),
            jax.ShapeDtypeStruct(self.cut, bfloat),
        ]
        self.in_vmem = [True, True, False, True, False, False]
        self.scratch = (
            [pltpu.VMEM(shape, bfloat), pltpu.VMEM((2,) + self.cut, bfloat)]
            + scatter_scratch(ctx, shape, bfloat) + gather_sems(ctx)
            + [pltpu.SemaphoreType.DMA((dp,))] * 4
            + ([pltpu.VMEM((ctx,) + shape, bfloat)] if fused else [])
        )
        self.base = len(self.scratch)
        group = ctx * own
        for size in (D, f_part, D):
            self.scratch = self.scratch + [pltpu.VMEM((group, size), bfloat), pltpu.SemaphoreType.DMA]
        self.elsewhere = (3, 6, 7)

    def run(self, line, extra, source, results, scratch):
        middle_ref, cotangent_ref, gain_ref, grads = extra[0], extra[1], extra[2], extra[4:6]
        normed_mid_ref, hidden_ref, branch_ref = scratch[self.base :: 2]
        loads = [
            pltpu.make_async_copy(extra[place], scratch[self.base + 2 * index], scratch[self.base + 2 * index + 1])
            for index, place in enumerate(self.elsewhere)
        ]
        for load in loads:
            load.start()
        grad_middle_ref, gain_sum_ref, all_ref, down_ref = results[:4]
        landed = results[4:]
        own_ref, cut_ref = scratch[:2]
        travel, sems = scratch[2:4], scratch[4:10]
        pushes = scratch[16:20]
        row = lax.axis_index("dp")
        height = D // self.dp

        def push(index, target):
            return remote(
                cut_ref.at[index, target], landed[index].at[row],
                pushes[2 * index].at[target], pushes[2 * index + 1].at[row], {"dp": target},
            )

        def keep(index):
            return pltpu.make_async_copy(
                cut_ref.at[index, row], landed[index].at[row], pushes[2 * index].at[row]
            )

        def rows_work(step):
            if step == 1:
                loads[0].wait()
            if height % LANES == 0:
                target = (row + step) % self.dp
                columns = pl.ds(pl.multiple_of(target * height, LANES), height)
            else:
                target = step % self.dp
                columns = slice(target * height, (target + 1) * height)
            left = normed_mid_ref[:, columns].T
            for index in range(2):
                cut_ref[index, target] = dot(left, grads[index][...]).astype(bfloat)
                if height % LANES == 0 and step < self.dp:
                    push(index, target).start()
            if step == self.dp:
                last_rows()

        def last_rows():
            for index in range(2):
                for step in range(1, self.dp):
                    if height % LANES:
                        push(index, (row + step) % self.dp).start()
                keep(index).start()

        def down_work(part):
            width = D // 4
            if part == 0:
                loads[1].wait()
                loads[2].wait()
            span = slice(part * width, (part + 1) * width)
            down_ref[:, span] = dot(hidden_ref[...].T, branch_ref[:, span]).astype(bfloat)

        todo = [functools.partial(rows_work, step) for step in range(1, self.dp + 1)]
        todo += [functools.partial(down_work, part) for part in range(4)]

        def idle(count=2):
            for _ in range(min(count, len(todo))):
                todo.pop(0)()

        parts_ref = scratch[20] if self.fused else source

        def make(slot):
            pair_rows = 2 * own_ref.shape[0]
            rows = pl.ds(pl.multiple_of(slot * pair_rows, pair_rows), pair_rows)
            total = dot(grads[0][rows], source[...], 1, 1) + dot(grads[1][rows], extra[8][...], 1, 1)
            parts_ref[pl.ds(slot * 2, 2)] = total.astype(bfloat).reshape((2,) + own_ref.shape)

        scatter_line(line, parts_ref, *travel, sems, idle, make if self.fused else None)
        scatter_total(line, parts_ref, *travel, sems, grad_middle_ref)
        gain_sum_ref[...] = jnp.zeros_like(gain_sum_ref)

        def chunk(rows):
            normed, factor = normalize(middle_ref[rows])
            gradient = grad_middle_ref[rows]
            gain_sum_ref[...] += jnp.sum(gradient * normed, axis=0, keepdims=True)
            back = cotangent_ref[rows].astype(single) + norm_back(gradient * gain_ref[...], normed, factor)
            grad_middle_ref[rows] = back
            own_ref[rows] = (branch_scale * back).astype(bfloat)

        by_chunks(own_ref.shape[0], chunk)
        gather_line(line, own_ref, all_ref, scratch[10:16], lambda: idle(2))
        idle(len(todo))
        for index in range(2):
            for other in range(self.dp):
                @pl.when(row != other)
                def _():
                    push(index, other).wait_send()
                    remote(
                        cut_ref.at[index, other], landed[index].at[other],
                        pushes[2 * index].at[other], pushes[2 * index + 1].at[other], {"dp": other},
                    ).wait_recv()
            keep(index).wait()


class CloseLine:
    reach = "ctx"
    held = False

    def __init__(self, dp, ctx, parts):
        self.dp, self.ctx, self.parts = dp, ctx, parts
        own = parts.shape[1]
        self.result = [jax.ShapeDtypeStruct((own, D), single)]
        self.in_vmem = [True]
        self.scratch = [pltpu.VMEM(parts.shape, bfloat)] + pair_sems(ctx)

    def lay_out(self, rows, width):
        self.result += [jax.ShapeDtypeStruct((rows, width), single)] * 2
        self.in_vmem += [True] * 2
        return self

    def run(self, line, extra, source, results, scratch):
        tokens_ref, grad_middle_ref = extra[:2]
        out_ref, landed_ref = results[0], scratch[0]
        copies = ExchangeCtx(self.dp, self.ctx, self.parts).copies(source, landed_ref, *scratch[1:4])
        for copy in copies:
            copy.start()
        for index in range(2):
            regroup(extra[2 + index], results[1 + index], self.dp, self.ctx, False)
        for copy in copies:
            copy.wait()
        ungroup(landed_ref, out_ref, self.dp, self.ctx)

        def chunk(rows):
            normed, factor = normalize(tokens_ref[rows].astype(single))
            out_ref[rows] = grad_middle_ref[rows] + norm_back(out_ref[rows], normed, factor)

        by_chunks(out_ref.shape[0], chunk)


def by_chunks(total, work):
    def step(index, carry):
        work(pl.ds(pl.multiple_of(index * 16, 16), 16))
        return carry

    lax.fori_loop(0, total // 16, step, 0)


def regroup(source, target, dp, ctx, forward):
    whole, parts = (source, target) if forward else (target, source)
    width = whole.shape[1] // (dp * ctx)
    for place in range(ctx):
        for row in range(dp):
            start = (row * ctx + place) * width
            wide, narrow = slice(start, start + width), slice(row * width, (row + 1) * width)
            if forward:
                target[place, :, narrow] = source[:, wide]
            else:
                target[:, wide] = source[place, :, narrow].astype(single)


def ungroup(landed_ref, out_ref, dp, ctx):
    width = D // (dp * ctx)
    for place in range(ctx):
        block = landed_ref[place]
        block = block.reshape(out_ref.shape[0], dp * width).astype(single)
        for row in range(dp):
            start = (row * ctx + place) * width
            out_ref[:, start : start + width] = block[:, row * width : (row + 1) * width]


QUERY_SPAN = slice(0, QRANK)
LATENT_SPAN = slice(QRANK, QRANK + KVRANK)
ROPE_SPAN = slice(QRANK + KVRANK, LATENT)


def turn(values, table_ref, sign):
    return (
        values * table_ref[0]
        + sign * pltpu.roll(values, LANES - ROPE // 2, 1) * table_ref[1]
        + sign * pltpu.roll(values, ROPE // 2, 1) * table_ref[2]
    )


def everyone(dp, ctx):
    row, place = lax.axis_index("dp"), lax.axis_index("ctx")
    steps = [(a, b) for a in range(dp) for b in range(ctx) if a or b]
    return [((row + a) % dp, (place + b) % ctx) for a, b in steps]


def greet(dp, ctx, reach):
    row, place = lax.axis_index("dp"), lax.axis_index("ctx")
    if "all" in reach:
        targets = [{"dp": a, "ctx": b} for a, b in everyone(dp, ctx)]
    else:
        targets = []
        if "ctx" in reach:
            targets += [{"ctx": (place + step) % ctx} for step in range(1, ctx)]
        if "dp" in reach:
            targets += [{"dp": (row + step) % dp} for step in range(1, dp)]
    barrier = pltpu.get_barrier_semaphore()
    for target in targets:
        pl.semaphore_signal(barrier, inc=1, device_id=target, device_id_type=MESH)
    pl.semaphore_wait(barrier, len(targets))


def transfer_kernel(dp, ctx, line_piece, direct, extras, *refs):
    refs = list(refs)

    def take(count):
        taken = refs[:count]
        del refs[:count]
        return taken

    line_source = take(1) if line_piece else []
    sources = take(len(direct))
    extra = take(extras)
    line_results = take(len(line_piece.result)) if line_piece else []
    results = take(len(direct))
    line_scratch = take(len(line_piece.scratch)) if line_piece else []
    greet(dp, ctx, [piece.reach for piece in direct] + line_reach(line_piece))
    copies = []
    for piece, source, result in zip(direct, sources, results):
        copies += piece.copies(source, result, *take(len(piece.scratch)))
    for copy in copies:
        copy.start()
    if line_piece:
        line_piece.run(Line(ctx), extra, line_source[0], line_results, line_scratch)
    for copy in copies:
        copy.wait()


def line_reach(line_piece):
    if line_piece is None:
        return []
    return ["ctx", "dp"] if line_piece.reach == "both" else ["ctx"]


def transfer(dp, ctx, collective_id, name, line=None, direct=(), extra=(), mebibytes=8):
    pieces = [item[0](dp, ctx, item[1]) for item in direct]
    vmem, anywhere = pl.BlockSpec(memory_space=pltpu.VMEM), pl.BlockSpec(memory_space=pl.ANY)
    operands, in_specs, shapes, out_specs, scratch = [], [], [], [], []
    if line:
        operands.append(line.parts)
        in_specs.append(vmem if line.held else anywhere)
        shapes += line.result
        out_specs += [vmem if held else anywhere for held in line.in_vmem]
        scratch += line.scratch
    for piece in pieces:
        operands.append(piece.parts)
        in_specs.append(anywhere)
        shapes.append(piece.result)
        out_specs.append(anywhere)
        scratch += piece.scratch
    return pl.pallas_call(
        functools.partial(transfer_kernel, dp, ctx, line, pieces, len(extra)),
        out_shape=shapes,
        in_specs=in_specs + [
            pl.BlockSpec(memory_space=pltpu.SMEM) if item.dtype == jnp.int32
            else anywhere if index in getattr(line, "elsewhere", ()) else vmem
            for index, item in enumerate(extra)
        ],
        out_specs=out_specs,
        scratch_shapes=scratch,
        compiler_params=comm_params(collective_id, mebibytes),
        cost_estimate=link_cost(150 << 20),
        name=name,
    )(*operands, *extra)


def valid_pairs(total, length):
    row = lax.broadcasted_iota(jnp.int32, (total, total), 0)
    col = lax.broadcasted_iota(jnp.int32, (total, total), 1)
    return (col <= row) & (col < length)


def slot_rows(ref, index, batch):
    span = ref.shape[1] // batch
    block = ref[:, pl.ds(pl.multiple_of(index * span, span), span), :]
    return block.reshape(ref.shape[0] * span, ref.shape[2])


def store_slot(ref, index, batch, lanes, values):
    span = ref.shape[1] // batch
    rows = pl.ds(pl.multiple_of(index * span, span), span)
    ref[:, rows, lanes] = values.reshape(ref.shape[0], span, values.shape[-1])


def attend_slot(
    heads, index, batch, length_ref, latent_ref, query_up_ref, latent_up_ref, table_ref,
    query_ref, kv_ref, attn_ref, total_ref,
):
    wide = heads * LANES
    latent = slot_rows(latent_ref, index, batch)
    total = latent.shape[0]
    query_normed, latent_normed, rope = latent[:, QUERY_SPAN], latent[:, LATENT_SPAN], latent[:, ROPE_SPAN]
    allowed = valid_pairs(total, length_ref[index])
    lane = lax.broadcasted_iota(jnp.int32, (total, LANES), 1)
    totals = jnp.zeros((total, LANES), single)
    query_up = query_up_ref[...].reshape(QRANK, wide)
    latent_up = latent_up_ref[...].reshape(KVRANK, wide)
    columns = pl.ds(pl.multiple_of(index * total, LANES), total)
    for head in range(heads):
        span = slice(head * LANES, (head + 1) * LANES)
        query = turn(dot(query_normed, query_up[:, span]), table_ref, 1.0).astype(bfloat)
        kv = dot(latent_normed, latent_up[:, span]).astype(bfloat)
        key = jnp.where(lane < NOPE, kv, rope)
        store_slot(query_ref, index, batch, span, query)
        store_slot(kv_ref, index, batch, span, kv)
        scores = dot(query, key, 1, 1) * score_scale
        masked = jnp.where(allowed, scores, neg_large)
        top = jnp.max(masked, axis=-1, keepdims=True)
        exponent = jnp.exp(masked - top)
        weight = jnp.sum(exponent, axis=-1, keepdims=True)
        totals = jnp.where(lane == head, top + jnp.log(weight), totals)
        probs = (exponent * (1.0 / weight)).astype(bfloat)
        out = dot(probs, kv).T[NOPE:]
        attn_ref[head * VDIM : (head + 1) * VDIM, columns] = out.astype(bfloat)
    store_slot(total_ref, index, batch, slice(0, LANES), totals)


def attend_back_slot(
    heads, index, batch, length_ref, query_ref, kv_ref, latent_ref, total_ref, branch_ref,
    out_heads_ref, query_up_ref, latent_up_ref, table_ref, parts_ref,
    grad_query_ref, grad_high_ref, grad_low_ref, query_sum_ref, latent_sum_ref,
):
    wide = heads * LANES
    latent = slot_rows(latent_ref, index, batch)
    rope = latent[:, ROPE_SPAN]
    total = rope.shape[0]
    totals = slot_rows(total_ref, index, batch)
    allowed = valid_pairs(total, length_ref[index])
    lane = lax.broadcasted_iota(jnp.int32, (total, LANES), 1)
    grad_rope = jnp.zeros((total, LANES), single)
    queries, kvs = slot_rows(query_ref, index, batch), slot_rows(kv_ref, index, batch)
    grads = dot(slot_rows(branch_ref, index, batch), out_heads_ref[...].reshape(D, heads * VDIM))
    grads = grads.astype(bfloat)
    blank = jnp.zeros((total, NOPE), bfloat)
    for head in range(heads):
        span = slice(head * LANES, (head + 1) * LANES)
        query, kv = queries[:, span], kvs[:, span]
        grad_attn = jnp.concatenate([blank, grads[:, head * VDIM : (head + 1) * VDIM]], axis=1)
        key = jnp.where(lane < NOPE, kv, rope)
        scores = dot(query, key, 1, 1) * score_scale
        probs = jnp.where(allowed, jnp.exp(scores - totals[:, head : head + 1]), 0.0)
        grad_probs = dot(grad_attn, kv, 1, 1)
        delta = jnp.sum(probs * grad_probs, axis=-1, keepdims=True)
        grad_scores = (probs * (grad_probs - delta)).astype(bfloat)
        grad_query = (dot(grad_scores, key) * score_scale).astype(bfloat).astype(single)
        grad_query_ref[:, span] = turn(grad_query, table_ref, -1.0).astype(bfloat)
        grad_key = dot(grad_scores, query, 0, 0) * score_scale
        grad_value = dot(probs.astype(bfloat), grad_attn, 0, 0)
        grad_kv = jnp.where(lane < NOPE, grad_key, grad_value)
        high = grad_kv.astype(bfloat)
        grad_high_ref[:, span] = high
        grad_low_ref[:, span] = (grad_kv - high.astype(single)).astype(bfloat)
        grad_rope = grad_rope + jnp.where(lane < NOPE, 0.0, grad_key)
    grad_query, high, low = grad_query_ref[...], grad_high_ref[...], grad_low_ref[...]
    query_up = query_up_ref[...].reshape(QRANK, wide)
    latent_up = latent_up_ref[...].reshape(KVRANK, wide)
    grad_latent = dot(high, latent_up, 1, 1) + dot(low, latent_up, 1, 1)
    for span, values in (
        (QUERY_SPAN, dot(grad_query, query_up, 1, 1)), (LATENT_SPAN, grad_latent), (ROPE_SPAN, grad_rope),
    ):
        store_slot(parts_ref, index, batch, span, values.astype(bfloat))
    latent_normed = latent[:, LATENT_SPAN]
    query_sum_ref[...] += dot(latent[:, QUERY_SPAN], grad_query, 0, 0)
    latent_sum_ref[...] += dot(latent_normed, high, 0, 0) + dot(latent_normed, low, 0, 0)


def head_table(total):
    freqs = np.float32(10000.0) ** (-(2.0 * np.arange(ROPE // 2, dtype=np.float32)) / ROPE)
    angles = np.arange(total, dtype=np.float32)[:, None] * freqs.astype(np.float32)[None, :]
    cosine, sine = np.cos(angles), np.sin(angles)
    table = np.zeros((3, total, LANES), np.float32)
    half, end = NOPE + ROPE // 2, NOPE + ROPE
    table[0, :, :NOPE] = 1.0
    table[0, :, NOPE:half] = table[0, :, half:end] = cosine
    table[1, :, NOPE:half] = -sine
    table[2, :, half:end] = sine
    return jnp.asarray(table)


def pad_rope(values):
    return jnp.pad(values, ((0, 0), (NOPE, LANES - NOPE - ROPE)))


def on_device(
    dp,
    ctx,
    tokens,
    lengths,
    cotangent,
    input_gain,
    query_gain,
    latent_gain,
    post_gain,
    query_down,
    query_up,
    latent_down,
    latent_up,
    out_proj,
    gate_proj,
    up_proj,
    down_proj,
):
    batch, span, _ = tokens.shape
    own = batch * span
    group = ctx * own
    heads = -(-HEADS // ctx)
    spare = heads * ctx - HEADS
    d_rows, q_rows, l_rows, f_rows = (
        query_down.shape[0], query_up.shape[0], latent_up.shape[0], down_proj.shape[0],
    )
    d_part, f_part = dp * d_rows, dp * f_rows
    place = lax.axis_index("ctx")

    def slices(values):
        return values.reshape(own, dp, ctx, d_rows).transpose(2, 0, 1, 3).reshape(ctx, own, d_part)

    def row_sums(values):
        return jnp.sum(values.astype(single), axis=0)

    wide = heads * LANES
    up_rows = q_rows + l_rows
    run = functools.partial(transfer, dp, ctx)

    grad_out = cotangent.reshape(own, D).astype(single)
    grad_branch = (branch_scale * grad_out).astype(bfloat)

    flat = tokens.reshape(own, D)
    inputs = flat.astype(single)
    normed_first, factor_first = normalize(inputs)
    gains = jnp.concatenate([input_gain, query_gain, latent_gain, post_gain]).astype(single)
    tile = 8 * LANES
    small = jnp.concatenate(
        [jnp.pad(gains, (0, tile - gains.shape[0])), jnp.pad(factor_first[:, 0], (0, tile - own))]
    )
    down_own = jnp.concatenate(
        [query_down, latent_down[:, :KVRANK], pad_rope(latent_down[:, KVRANK:])], axis=1
    )
    up_query = query_up.reshape(q_rows, HEADS, NOPE + ROPE)
    up_query = jnp.pad(up_query, ((0, 0), (0, spare), (0, LANES - NOPE - ROPE)))
    up_latent = jnp.pad(latent_up.reshape(l_rows, HEADS, NOPE + VDIM), ((0, 0), (0, spare), (0, 0)))
    up_query = up_query.reshape(q_rows, ctx, wide).transpose(1, 0, 2)
    up_latent = up_latent.reshape(l_rows, ctx, wide).transpose(1, 0, 2)
    out_padded = jnp.pad(out_proj, ((0, 0), (0, spare * VDIM)))
    gate, up, token_slices, up_query, up_latent, down_rows, smalls, out_rows, down = run(
        1, "open", OpenLine(dp, ctx, gate_proj),
        [
            (ExchangeCtx, slices(flat)), (ExchangeCtx, up_query), (ExchangeCtx, up_latent),
            (GatherDp, down_own),
            (GatherAll, small.reshape(16, LANES)), (GatherDp, out_padded), (GatherDp, down_proj),
        ],
        (up_proj,), 16,
    )
    smalls, grad_branch = lax.optimization_barrier((smalls, grad_branch))
    grad_branch = gather_xla(grad_branch)
    down = down.reshape(f_part, D)
    down_rows = down_rows.reshape(d_part, LATENT)
    smalls = smalls.reshape(dp, ctx, 2 * tile)
    factor_all = smalls[lax.axis_index("dp"), :, tile : tile + own].reshape(group, 1)
    cuts = (d_rows, d_rows + q_rows, d_rows + up_rows, d_rows + up_rows + d_rows)
    gain_in = lax.dynamic_index_in_dim(smalls[:, :, : cuts[0]], place, 1, keepdims=False)
    gain_in = gain_in.reshape(1, d_part)
    gain_query = smalls[:, :, cuts[0] : cuts[1]].reshape(1, QRANK)
    gain_latent = smalls[:, :, cuts[1] : cuts[2]].reshape(1, KVRANK)
    gain_post = smalls[:, :, cuts[2] : cuts[3]].reshape(1, D)
    gain_down = jnp.concatenate([gain_query, gain_latent, jnp.zeros((1, LANES), single)], axis=1)

    normed_slices = token_slices.reshape(group, d_part).astype(single) * factor_all
    normed_in = (normed_slices * gain_in).astype(bfloat)
    table = head_table(ctx * span)
    own_table = lax.dynamic_slice_in_dim(table, place * span, span, 1)
    own_table = jnp.tile(own_table, (1, batch, 1))
    parts = dot(normed_in, down_rows).astype(bfloat).reshape(ctx, own, LATENT)
    out_heads = out_padded.reshape(d_rows, ctx, heads * VDIM).transpose(1, 0, 2)
    ups = (up_query.reshape(ctx * q_rows, wide), up_latent.reshape(ctx * l_rows, wide))
    outs = run(
        2, "forward",
        ForwardLine(dp, ctx, parts, heads, batch, (gate, up), ups, out_heads),
        (),
        (gain_down, own_table, lengths, table, gate, up) + ups + (out_heads,),
        56,
    )
    latents, latent_all, query, kv, totals, attn_all = outs[:6]
    query_ups, latent_ups, gate, up, out_heads = outs[6:]
    attn_all = attn_all.reshape(ctx * heads * VDIM, group)
    branch = dot(attn_all, out_rows.reshape(d_part, ctx * heads * VDIM), 0, 1).astype(bfloat).reshape(batch, ctx, span, d_part)
    gate, up = gate.reshape(D, f_part), up.reshape(D, f_part)
    middle, normed_mid, branch_out, hidden, grad_gate, grad_up, out_heads = run(
        4, "middle", MiddleLine(dp, ctx, branch, f_part),
        [(GatherDp, out_heads.reshape(ctx * d_rows, heads * VDIM))],
        (flat, gain_post, gate, up, down, grad_branch), 60,
    )
    normed_mid = normed_mid.reshape(group, D)
    fused = group <= 1024
    if fused:
        parts, last = gate, (up,)
    else:
        parts = dot(grad_gate, gate, 1, 1) + dot(grad_up, up, 1, 1)
        parts, last = parts.astype(bfloat).reshape(ctx, own, D), ()
    grad_middle, post_sum, grad_attn_branch, grad_down_proj, grad_gate_proj, grad_up_proj = run(
        5, "middle_back",
        MiddleBackLine(dp, ctx, parts, (own, D), f_part, fused),
        (),
        (
            middle, cotangent.reshape(own, D), gain_post, normed_mid, grad_gate, grad_up, hidden,
            grad_branch,
        ) + last,
        60,
    )
    columns_shape = (ctx, d_rows, f_part)
    grad_gate_proj = row_sums(grad_gate_proj).astype(bfloat).reshape(columns_shape)
    grad_up_proj = row_sums(grad_up_proj).astype(bfloat).reshape(columns_shape)

    outs = run(
        8, "backward", BackwardLine(dp, ctx, grad_attn_branch, heads, batch, HEADS * VDIM),
        [
            (ExchangeDp, grad_down_proj.reshape(dp, f_rows, D)), (ExchangeCtx, grad_gate_proj),
            (ExchangeCtx, grad_up_proj),
        ],
        (
            gain_down, own_table, latents, attn_all, lengths, query, kv, latent_all, totals, out_heads,
            query_ups, latent_ups, table,
        ),
        62,
    )
    grad_latents, grad_down, grad_out_proj, grad_query_ups, grad_latent_ups = outs[:5]
    grad_down_proj, grad_gate_proj, grad_up_proj = outs[5:]
    branch_out, grad_down = lax.optimization_barrier((branch_out, grad_down))
    branch_out = scatter_xla(branch_out.reshape(group, D)).astype(single)
    layer_out = (middle + branch_scale * branch_out).astype(bfloat)
    grad_down = grad_down.reshape(group, LATENT)
    grad_normed_in = dot(grad_down, down_rows, 1, 1)
    grad_scaled = (grad_normed_in * gain_in).astype(bfloat).reshape(ctx, own, d_part)
    grad_rows = dot(normed_in, grad_down, 0, 0)
    last = jnp.sum(grad_normed_in * normed_slices, axis=0)[:, None]
    grad_rows = jnp.concatenate([grad_rows[:, : LATENT - 1], last], axis=1)
    normed_query, _ = normalize(latents[:, :QRANK])
    normed_latent, _ = normalize(latents[:, QRANK : QRANK + KVRANK])
    grad_query_normed = grad_latents[:, :QRANK]
    grad_latent_normed = grad_latents[:, QRANK : QRANK + KVRANK]
    gain_sums = jnp.concatenate(
        [
            post_sum.reshape(dp, ctx, d_rows),
            jnp.sum(grad_query_normed * normed_query, axis=0).reshape(dp, ctx, q_rows),
            jnp.sum(grad_latent_normed * normed_latent, axis=0).reshape(dp, ctx, l_rows),
        ],
        axis=2,
    )
    gain_sums = jnp.pad(gain_sums, ((0, 0), (0, 0), (0, tile - gain_sums.shape[2])))
    outs = run(
        9, "close", CloseLine(dp, ctx, grad_scaled).lay_out(d_rows, FF),
        [
            (ExchangeDp, grad_rows.reshape(dp, d_rows, LATENT)),
            (ExchangeCtx, row_sums(grad_query_ups).astype(bfloat).reshape(ctx, q_rows, wide)),
            (ExchangeCtx, row_sums(grad_latent_ups).astype(bfloat).reshape(ctx, l_rows, wide)),
            (ExchangeAll, gain_sums.reshape(dp, ctx, 8, LANES)),
        ],
        (flat, grad_middle, grad_gate_proj, grad_up_proj),
        32,
    )
    input_grad, grad_gate_proj, grad_up_proj, grad_rows = outs[:4]
    grad_query_ups, grad_latent_ups, gain_sums = outs[4:]
    grad_rows = jnp.sum(grad_rows, axis=0)
    gain_sums = jnp.sum(gain_sums.reshape(dp * ctx, tile), axis=0)

    def by_heads(values, rows):
        return values.transpose(1, 0, 2).reshape(rows, ctx * heads, LANES)[:, :HEADS].astype(single)

    grad_query_up = by_heads(grad_query_ups, q_rows)[:, :, : NOPE + ROPE]
    grad_query_up = grad_query_up.reshape(q_rows, HEADS * (NOPE + ROPE))
    grad_latent_up = by_heads(grad_latent_ups, l_rows).reshape(l_rows, HEADS * (NOPE + VDIM))
    rope_start = QRANK + KVRANK + NOPE
    return (
        layer_out.reshape(batch, span, D),
        input_grad.reshape(batch, span, D),
        grad_rows[:, LATENT - 1],
        gain_sums[d_rows : d_rows + q_rows],
        gain_sums[d_rows + q_rows : d_rows + up_rows],
        gain_sums[:d_rows],
        grad_rows[:, :QRANK],
        grad_query_up,
        jnp.concatenate(
            [grad_rows[:, QRANK : QRANK + KVRANK], grad_rows[:, rope_start : rope_start + ROPE]], axis=1
        ),
        grad_latent_up,
        row_sums(grad_out_proj),
        grad_gate_proj,
        grad_up_proj,
        row_sums(grad_down_proj),
    )


def solution(mesh):
    both = ("dp", "ctx")
    tokens, vector, matrix = P("dp", "ctx", None), P(both), P(both, None)
    return jax.shard_map(
        functools.partial(on_device, mesh.shape["dp"], mesh.shape["ctx"]),
        mesh=mesh,
        in_specs=(tokens, P("dp"), tokens) + (vector,) * 4 + (matrix,) * 8,
        out_specs=(tokens, tokens) + (vector,) * 4 + (matrix,) * 8,
        check_vma=False,
    )
```

```python
import functools

import jax
import jax.numpy as jnp
import numpy as np
from jax import lax
from jax.experimental import pallas as pl
from jax.experimental.pallas import tpu as pltpu
from jax.sharding import PartitionSpec as P

D = 2560
FF = 6400
HEADS = 40
QRANK = 768
KVRANK = 256
NOPE = 64
ROPE = 32
VDIM = 64

LANES = 128
LATENT = QRANK + KVRANK + LANES

epsilon = 1e-05
branch_scale = 1.4 / 62**0.5
score_scale = 1.0 / (NOPE + ROPE) ** 0.5
neg_large = -1e30
bfloat = jnp.bfloat16
MESH = pl.DeviceIdType.MESH
single = jnp.float32
highest = lax.Precision.HIGHEST


def dot(left, right, left_dim=1, right_dim=0, precision=None):
    return lax.dot_general(
        left,
        right,
        (((left_dim,), (right_dim,)), ((), ())),
        precision=precision,
        preferred_element_type=single,
    )


def normalize(values):
    factor = lax.rsqrt(jnp.mean(values * values, axis=-1, keepdims=True) + epsilon)
    return (values * factor, factor)


def norm_back(grad_scaled, normed, factor):
    return factor * (grad_scaled - normed * jnp.mean(grad_scaled * normed, axis=-1, keepdims=True))


def gather_xla(values):
    return lax.all_gather(values, "ctx", axis=0, tiled=True)


def scatter_xla(values):
    return lax.psum_scatter(values, "ctx", scatter_dimension=0, tiled=True)


def exchange_xla(values):
    return lax.all_to_all(values, "ctx", 0, 0, tiled=True)


class Line:
    def __init__(self, ctx):
        self.pairs = ctx // 2
        self.place = lax.axis_index("ctx")
        self.pair, self.core = self.place // 2, self.place % 2
        self.has_left, self.has_right = self.pair > 0, self.pair < self.pairs - 1
        self.left = {"ctx": jnp.maximum(self.place - 2, 0)}
        self.right = {"ctx": jnp.minimum(self.place + 2, ctx - 1)}
        self.twin = {"ctx": self.place + 1 - 2 * self.core}


def remote(source, target, send, receive, device):
    return pltpu.make_async_remote_copy(
        src_ref=source, dst_ref=target, send_sem=send, recv_sem=receive,
        device_id=device, device_id_type=MESH,
    )


def nothing():
    pass


def gather_line(line, own_ref, all_ref, sems, idle=nothing, arrived=None):
    steps = gather_steps(line, own_ref, all_ref, sems, arrived)
    for step, _ in enumerate(steps):
        if step < line.pairs - 1:
            idle()


def gather_steps(line, own_ref, all_ref, sems, arrived=None):
    send_left, send_right, send_twin, receive, receive_twin, local = sems
    pairs, pair, core = line.pairs, line.pair, line.core

    def to_side(source, slot, sem, device):
        return remote(source, all_ref.at[slot * 2 + core], sem.at[slot], receive.at[slot], device)

    def to_twin(source, slot):
        return remote(source, all_ref.at[slot * 2 + core], send_twin.at[slot], receive_twin.at[slot], line.twin)

    pl.when(line.has_right)(lambda: to_side(own_ref, pair, send_right, line.right).start())
    pl.when(line.has_left)(lambda: to_side(own_ref, pair, send_left, line.left).start())
    to_twin(own_ref, pair).start()
    keep = pltpu.make_async_copy(own_ref, all_ref.at[line.place], local)
    keep.start()
    if arrived:
        keep.wait()
        to_twin(own_ref, pair).wait_recv()
        arrived(pair)
    for step in range(1, pairs):
        yield

        def from_left(slot=pair - step):
            block = all_ref.at[slot * 2 + core]
            to_side(block, slot, send_left, line.left).wait_recv()
            pl.when(line.has_right)(lambda: to_side(block, slot, send_right, line.right).start())
            to_twin(block, slot).start()

        def from_right(slot=pair + step):
            block = all_ref.at[slot * 2 + core]
            to_side(block, slot, send_right, line.right).wait_recv()
            pl.when(line.has_left)(lambda: to_side(block, slot, send_left, line.left).start())
            to_twin(block, slot).start()

        pl.when(pair - step >= 0)(from_left)
        pl.when(pair + step < pairs)(from_right)
        if arrived:
            slot = nearest(line, step)
            to_twin(own_ref, slot).wait_recv()
            arrived(slot)
    yield
    if not arrived:
        keep.wait()
    for slot in range(pairs):
        if arrived:
            to_twin(own_ref, slot).wait_send()
        else:
            to_twin(own_ref, slot).wait()
        pl.when((slot <= pair) & line.has_right)(
            lambda slot=slot: to_side(own_ref, slot, send_right, line.right).wait_send())
        pl.when((slot >= pair) & line.has_left)(
            lambda slot=slot: to_side(own_ref, slot, send_left, line.left).wait_send())


def nearest(line, order):
    shorter = jnp.minimum(line.pair, line.pairs - 1 - line.pair)
    distance = (order + 1) // 2
    both = line.pair + (distance if order % 2 == 0 else -distance)
    ahead = jnp.where(line.pair < line.pairs - 1 - line.pair, order - shorter, shorter - order)
    return jnp.where(order <= 2 * shorter, both, line.pair + ahead)


def comm_params(collective_id, mebibytes):
    return pltpu.CompilerParams(
        collective_id=collective_id, has_side_effects=True, vmem_limit_bytes=mebibytes << 20
    )


def link_cost(size):
    return pl.CostEstimate(flops=0, transcendentals=0, bytes_accessed=size)


def scatter_line(line, parts_ref, twin_ref, landed_ref, sems, idle=nothing):
    for _ in scatter_steps(line, parts_ref, twin_ref, landed_ref, sems):
        idle()


def scatter_steps(line, parts_ref, twin_ref, landed_ref, sems, make=None, begun=False):
    send_twin, receive_twin, send_left, send_right, from_left, from_right = sems
    pairs, pair = line.pairs, line.pair
    to_twin, to_right, to_left = travels(line, parts_ref, twin_ref, landed_ref, sems)

    def both_cores(slot):
        return parts_ref[slot * 2 + line.core].astype(single) + twin_ref[slot].astype(single)

    def prepare(order):
        ahead = (pair + pairs - 1 - order) % pairs
        slot = jnp.where(pair < pairs // 2, ahead, (pair + 1 + order) % pairs)
        if make:
            make(slot)
        to_twin(slot).start()

    todo = [] if begun else list(range(pairs))
    for _ in range(2 if make else len(todo)):
        prepare(todo.pop(0))
    for step in range(pairs - 1, 0, -1):
        yield

        def pass_on(slot, arrives, travel):
            to_twin(slot).wait_recv()

            @pl.when(arrives)
            def _():
                travel(slot).wait_recv()
                total = both_cores(slot) + landed_ref[slot].astype(single)
                twin_ref[slot] = total.astype(twin_ref.dtype)

            @pl.when(jnp.logical_not(arrives))
            def _():
                twin_ref[slot] = both_cores(slot).astype(twin_ref.dtype)

            travel(slot).start()

        pl.when(pair + step < pairs)(lambda slot=pair + step: pass_on(slot, line.has_left, to_right))
        pl.when(pair - step >= 0)(lambda slot=pair - step: pass_on(slot, line.has_right, to_left))
        if todo:
            prepare(todo.pop(0))
    to_twin(pair).wait_recv()


def travels(line, parts_ref, twin_ref, landed_ref, sems):
    send_twin, receive_twin, send_left, send_right, from_left, from_right = sems
    pairs = line.pairs

    def to_twin(slot):
        source = parts_ref.at[slot * 2 + 1 - line.core]
        return remote(source, twin_ref.at[slot], send_twin.at[slot], receive_twin.at[slot], line.twin)

    def to_right(slot):
        return remote(
            twin_ref.at[slot], landed_ref.at[slot], send_right.at[slot], from_left.at[slot], line.right
        )

    def to_left(slot):
        goal = jnp.where(slot == line.pair - 1, pairs, slot)
        return remote(
            twin_ref.at[slot], landed_ref.at[goal], send_left.at[slot], from_right.at[slot], line.left
        )

    return (to_twin, to_right, to_left)


def scatter_total(line, parts_ref, twin_ref, landed_ref, sems, out_ref):
    pairs, pair = line.pairs, line.pair
    to_twin, to_right, to_left = travels(line, parts_ref, twin_ref, landed_ref, sems)
    out_ref[...] = parts_ref[pair * 2 + line.core].astype(single) + twin_ref[pair].astype(single)

    @pl.when(line.has_left)
    def _():
        to_right(pair).wait_recv()
        out_ref[...] += landed_ref[pair].astype(single)

    @pl.when(line.has_right)
    def _():
        to_left(pair).wait_recv()
        out_ref[...] += landed_ref[pairs].astype(single)

    for slot in range(pairs):
        to_twin(slot).wait_send()
        pl.when(slot > pair)(lambda slot=slot: to_right(slot).wait_send())
        pl.when(slot < pair)(lambda slot=slot: to_left(slot).wait_send())


def gather_sems(ctx):
    return [pltpu.SemaphoreType.DMA((ctx // 2,))] * 5 + [pltpu.SemaphoreType.DMA]


def scatter_scratch(ctx, shape, dtype):
    pairs = ctx // 2
    slots = [pltpu.VMEM((count,) + shape, dtype) for count in (pairs, pairs + 1)]
    return slots + [pltpu.SemaphoreType.DMA((pairs,))] * 6


def pair_sems(count):
    return [pltpu.SemaphoreType.DMA((count,))] * 2 + [pltpu.SemaphoreType.DMA]


class ExchangeCtx:
    reach = "ctx"

    def __init__(self, dp, ctx, parts):
        self.count, self.parts = ctx, parts
        self.axis = len(parts.shape) - 3
        shape = parts.shape if not self.axis else (ctx, parts.shape[0]) + parts.shape[2:]
        self.result = jax.ShapeDtypeStruct(shape, parts.dtype)
        self.scratch = pair_sems(ctx)

    def copies(self, source, target, send, receive, local):
        place = lax.axis_index("ctx")

        def part(index):
            return source.at[:, index] if self.axis else source.at[index]

        out = [pltpu.make_async_copy(part(place), target.at[place], local)]
        for step in range(1, self.count):
            other = (place + step) % self.count
            out.append(
                remote(
                    part(other), target.at[place], send.at[step], receive.at[step], {"ctx": other}
                )
            )
        return out


class ExchangeDp:
    reach = "dp"
    whole = False

    def __init__(self, dp, ctx, parts):
        self.count, self.parts = dp, parts
        shape = (dp,) + parts.shape if self.whole else parts.shape
        self.result = jax.ShapeDtypeStruct(shape, parts.dtype)
        self.scratch = pair_sems(dp)

    def copies(self, source, target, send, receive, local):
        row = lax.axis_index("dp")

        def part(index):
            return source if self.whole else source.at[index]

        out = [pltpu.make_async_copy(part(row), target.at[row], local)]
        for step in range(1, self.count):
            other = (row + step) % self.count
            out.append(
                remote(part(other), target.at[row], send.at[step], receive.at[step], {"dp": other})
            )
        return out


class GatherDp(ExchangeDp):
    whole = True


class ExchangeAll:
    reach = "all"
    whole = False

    def __init__(self, dp, ctx, parts):
        self.dp, self.ctx, self.parts = dp, ctx, parts
        shape = (dp, ctx) + parts.shape if self.whole else parts.shape
        self.result = jax.ShapeDtypeStruct(shape, parts.dtype)
        self.scratch = pair_sems(dp * ctx)

    def copies(self, source, target, send, receive, local):
        row, place = lax.axis_index("dp"), lax.axis_index("ctx")

        def part(index):
            return source if self.whole else source.at[index[0], index[1]]

        out = [pltpu.make_async_copy(part((row, place)), target.at[row, place], local)]
        for index, other in enumerate(everyone(self.dp, self.ctx)):
            out.append(
                remote(
                    part(other), target.at[row, place], send.at[index], receive.at[index],
                    {"dp": other[0], "ctx": other[1]},
                )
            )
        return out


class GatherAll(ExchangeAll):
    whole = True


class GatherLine:
    reach = "ctx"
    held = False
    extra_held = True

    def __init__(self, dp, ctx, parts):
        self.parts = parts
        self.result = [jax.ShapeDtypeStruct((ctx,) + parts.shape, parts.dtype)]
        self.in_vmem = [False]
        self.scratch = gather_sems(ctx)

    def run(self, line, extra, source, results, sems):
        gather_line(line, source, results[0], sems)


class LatentLine:
    reach = "ctx"
    held = True

    def __init__(self, dp, ctx, parts):
        shape = parts.shape[1:]
        self.parts = parts
        self.result = [
            jax.ShapeDtypeStruct(shape, single), jax.ShapeDtypeStruct(parts.shape, bfloat)
        ]
        self.in_vmem = [True, False]
        self.scratch = [pltpu.VMEM(shape, bfloat)] + scatter_scratch(ctx, shape, bfloat) + gather_sems(ctx)

    def finish_own(self, extra, sums_ref, own_ref):
        gain_ref, table_ref = extra
        for span in (QUERY_SPAN, LATENT_SPAN):
            normed, _ = normalize(sums_ref[:, span])
            own_ref[:, span] = (normed * gain_ref[:, span]).astype(bfloat)
        own_ref[:, ROPE_SPAN] = turn(sums_ref[:, ROPE_SPAN], table_ref, 1.0).astype(bfloat)

    def run(self, line, extra, source, results, scratch):
        sums_ref, all_ref = results
        own_ref = scratch[0]
        scatter_line(line, source, *scratch[1:3], scratch[3:9])
        scatter_total(line, source, *scratch[1:3], scratch[3:9], sums_ref)
        self.finish_own(extra, sums_ref, own_ref)
        gather_line(line, own_ref, all_ref, scratch[9:])


class OpenLine:
    reach = "ctx"
    held = True

    def __init__(self, dp, ctx, parts):
        self.dp, self.ctx, self.parts = dp, ctx, parts
        rows, width = parts.shape
        self.cut = jax.ShapeDtypeStruct((ctx, rows, width // ctx), bfloat)
        self.result = [self.cut] * 2
        self.in_vmem = [False] * 2
        self.scratch = [pltpu.VMEM((2,) + self.cut.shape, bfloat)] + pair_sems(ctx) * 2

    def run(self, line, extra, source, results, scratch):
        cut_ref, copies = scratch[0], []
        for index, matrix in enumerate((source, extra[0])):
            regroup(matrix, cut_ref.at[index], self.dp, self.ctx, True)
            sems = scratch[1 + 3 * index : 4 + 3 * index]
            pieces = ExchangeCtx(self.dp, self.ctx, self.cut).copies(cut_ref.at[index], results[index], *sems)
            for copy in pieces:
                copy.start()
            copies += pieces
        for copy in copies:
            copy.wait()


class ForwardLine(LatentLine):
    reach = "both"

    def __init__(self, dp, ctx, parts, heads, batch, matrices, ups, out_heads):
        super().__init__(dp, ctx, parts)
        own = parts.shape[1]
        group, wide = ctx * own, heads * LANES
        self.dp, self.ctx, self.heads, self.batch = dp, ctx, heads, batch
        self.pieces = {
            "heads": ExchangeCtx(dp, ctx, out_heads),
            "queries": GatherDp(dp, ctx, ups[0]),
            "latents": GatherDp(dp, ctx, ups[1]),
            "gates": GatherDp(dp, ctx, matrices[0]),
            "ups": GatherDp(dp, ctx, matrices[1]),
        }
        self.elsewhere = (4, 5)
        self.result += [
            jax.ShapeDtypeStruct((ctx, own, wide), bfloat),
            jax.ShapeDtypeStruct((ctx, own, wide), bfloat),
            jax.ShapeDtypeStruct((ctx, own, LANES), single),
            jax.ShapeDtypeStruct((ctx, heads * VDIM, group), bfloat),
        ]
        self.result += [
            self.pieces[name].result for name in ("queries", "latents", "gates", "ups", "heads")
        ]
        self.in_vmem = [True, True, True, True, True, False, True, True] + [False] * 3
        self.base = len(self.scratch)
        self.scratch = self.scratch + [pltpu.VMEM((heads * VDIM, group), bfloat)]
        for piece in self.pieces.values():
            self.scratch = self.scratch + piece.scratch
        self.scratch = self.scratch + gather_sems(ctx)

    def run(self, line, extra, source, results, scratch):
        gain_ref, table_ref, length_ref, slot_table_ref = extra[:4]
        matrices, ups, out_heads_ref = extra[4:6], extra[6:8], extra[8]
        sums_ref, all_ref, query_ref, kv_ref, total_ref, attn_all_ref = results[:6]
        query_ups_ref, latent_ups_ref, gates_ref, ups_ref, heads_ref = results[6:]
        attn_ref = scratch[self.base]
        later = list(scratch[self.base + 1 :])
        ends = {
            "heads": (out_heads_ref, heads_ref), "queries": (ups[0], query_ups_ref),
            "latents": (ups[1], latent_ups_ref),
            "gates": (matrices[0], gates_ref), "ups": (matrices[1], ups_ref),
        }
        copies = {}
        for name, piece in self.pieces.items():
            copies[name] = piece.copies(*ends[name], *later[: len(piece.scratch)])
            del later[: len(piece.scratch)]

        def start(*names):
            for name in names:
                for copy in copies[name]:
                    copy.start()

        def wait(*names):
            for name in names:
                for copy in copies[name]:
                    copy.wait()

        start("queries", "latents", "gates", "ups")
        scatter_line(line, source, *scratch[1:3], scratch[3:9])
        scatter_total(line, source, *scratch[1:3], scratch[3:9], sums_ref)
        self.finish_own((gain_ref, table_ref), sums_ref, scratch[0])
        gather_line(line, scratch[0], all_ref, scratch[9 : self.base])
        wait("queries", "latents")
        start("heads")

        def slot(index, carry):
            attend_slot(
                self.heads, index, self.batch, length_ref, all_ref, query_ups_ref, latent_ups_ref,
                slot_table_ref, query_ref, kv_ref, attn_ref, total_ref,
            )
            return carry

        lax.fori_loop(0, self.batch, slot, 0)
        gather_line(line, attn_ref, attn_all_ref, later)
        wait("heads", "gates", "ups")


class BackwardLine(LatentLine):
    reach = "both"

    def __init__(self, dp, ctx, branch, heads, batch, columns):
        own = branch.shape[1]
        parts = jax.ShapeDtypeStruct((ctx, own, LATENT), bfloat)
        super().__init__(dp, ctx, parts)
        self.parts = branch
        self.dp, self.ctx, self.heads, self.batch = dp, ctx, heads, batch
        rows, wide = D // (dp * ctx), heads * LANES
        self.ups = [
            ExchangeDp(dp, ctx, jax.ShapeDtypeStruct((dp, rank // dp, wide), bfloat))
            for rank in (QRANK, KVRANK)
        ]
        self.out = ExchangeDp(dp, ctx, jax.ShapeDtypeStruct((dp, rows, columns), bfloat))
        self.result += [self.out.result]
        self.result += [piece.result for piece in self.ups]
        self.in_vmem += [False, False, False]
        self.base = len(self.scratch)
        total = ctx * own // batch
        self.scratch = self.scratch + [
            pltpu.VMEM((ctx * own, rows), bfloat), pltpu.VMEM(parts.shape, bfloat),
        ]
        self.scratch = self.scratch + [pltpu.VMEM((total, wide), bfloat)] * 3
        self.scratch = self.scratch + [pltpu.VMEM((rank, wide), single) for rank in (QRANK, KVRANK)]
        self.scratch = self.scratch + [pltpu.VMEM(piece.parts.shape, bfloat) for piece in self.ups]
        for piece in self.ups + [self.out]:
            self.scratch = self.scratch + piece.scratch
        self.scratch = self.scratch + [pltpu.VMEM(self.out.parts.shape, bfloat)]

    def run(self, line, extra, source, results, scratch):
        branch_ref, attn_ref = source, extra[3]
        parts_ref = scratch[self.base + 1]
        work_refs = scratch[self.base + 2 : self.base + 5]
        sum_refs = scratch[self.base + 5 : self.base + 7]
        send_refs = scratch[self.base + 7 : self.base + 9]
        sems = scratch[self.base + 9 :]
        for ref in sum_refs:
            ref[...] = jnp.zeros_like(ref)

        def slot(index, carry):
            attend_back_slot(
                self.heads, index, self.batch, extra[4], extra[5], extra[6], extra[7], extra[8],
                branch_ref, *extra[9:13], parts_ref, *work_refs, *sum_refs,
            )
            return carry

        lax.fori_loop(0, self.batch, slot, 0)
        copies = []
        for index, piece in enumerate(self.ups):
            send_refs[index][...] = sum_refs[index][...].astype(bfloat).reshape(piece.parts.shape)
            copies += piece.copies(
                send_refs[index], results[3 + index], *sems[3 * index : 3 * index + 3]
            )
        for copy in copies:
            copy.start()
        out_ref, slice_ref = scratch[-1], scratch[self.base]
        out_copies = self.out.copies(out_ref, results[2], *scratch[-4:-1])
        rows = D // (self.dp * self.ctx)
        height = D // self.dp
        own = branch_ref.shape[1]
        span = own // self.batch

        def work(index):
            row = lax.broadcasted_iota(jnp.int32, (height, rows), 0)
            col = lax.broadcasted_iota(jnp.int32, (height, rows), 1)
            chosen = (row == line.place * rows + col).astype(single).astype(bfloat)
            block = branch_ref[:, :, index * height : (index + 1) * height]
            picked = dot(block.reshape(self.ctx * own, height), chosen).astype(bfloat)
            for place in range(self.ctx):
                for slot in range(self.batch):
                    start = (place * self.batch + slot) * span
                    goal = (slot * self.ctx + place) * span
                    slice_ref[goal : goal + span] = picked[start : start + span]
            columns = out_ref.shape[2]
            out_ref[index] = dot(slice_ref[...].T, attn_ref[:columns], 1, 1).astype(bfloat)

        todo = list(range(self.dp))

        def idle():
            if todo:
                work(todo.pop(0))
                if not todo:
                    for copy in out_copies:
                        copy.start()

        sums_ref, all_ref = results[:2]
        own_ref = scratch[0]
        scatter_line(line, parts_ref, *scratch[1:3], scratch[3:9], idle)
        scatter_total(line, parts_ref, *scratch[1:3], scratch[3:9], sums_ref)
        self.finish_own(extra[:3], sums_ref, own_ref)
        gather_line(line, own_ref, all_ref, scratch[9 : self.base], idle)
        while todo:
            idle()
        for copy in copies + out_copies:
            copy.wait()

    def finish_own(self, extra, sums_ref, own_ref):
        gain_ref, table_ref, latents_ref = extra
        for span in (QUERY_SPAN, LATENT_SPAN):
            normed, factor = normalize(latents_ref[:, span])
            scaled = sums_ref[:, span] * gain_ref[:, span]
            own_ref[:, span] = norm_back(scaled, normed, factor).astype(bfloat)
        own_ref[:, ROPE_SPAN] = turn(sums_ref[:, ROPE_SPAN], table_ref, -1.0).astype(bfloat)


class MiddleLine:
    reach = "ctx"
    held = False

    def __init__(self, dp, ctx, parts, f_part):
        self.dp, self.ctx, self.parts = dp, ctx, parts
        own, cut = parts.shape[0] * parts.shape[2], parts.shape[3]
        group = ctx * own
        self.result = [
            jax.ShapeDtypeStruct((own, D), single), jax.ShapeDtypeStruct((ctx, own, D), bfloat),
            jax.ShapeDtypeStruct((ctx, own, D), bfloat),
        ]
        self.result += [jax.ShapeDtypeStruct((group, f_part), bfloat)] * 3
        self.in_vmem = [True] + [False] * 5
        self.scratch = (
            [pltpu.VMEM((ctx, parts.shape[0], parts.shape[2], cut), bfloat), pltpu.VMEM((own, D), bfloat)]
            + pair_sems(ctx) + gather_sems(ctx)
        )
        self.base = len(self.scratch)
        self.scratch = self.scratch + [pltpu.VMEM((ctx, own, D), bfloat)] * 2
        self.scratch = self.scratch + [pltpu.VMEM((group, f_part), bfloat)] * 3
        self.scratch = self.scratch + [pltpu.SemaphoreType.DMA((ctx // 2,))] * 5
        shapes = [(D, f_part), (D, f_part), (f_part, D), (group, D)]
        self.scratch = self.scratch + [pltpu.VMEM(shape, bfloat) for shape in shapes]
        self.scratch = self.scratch + [pltpu.SemaphoreType.DMA] * 4
        self.elsewhere = (2, 3, 4, 5)

    def run(self, line, extra, source, results, scratch):
        tokens_ref, gain_ref = extra[:2]
        middle_ref = results[0]
        landed_ref, own_ref = scratch[:2]
        kept = scratch[self.base : self.base + 5]
        kept_sems = scratch[self.base + 5 : self.base + 10]
        weights = scratch[self.base + 10 : self.base + 14]
        all_ref, branch_out_ref, hidden_ref, grad_gate_ref, grad_up_ref = kept
        gate_ref, up_ref, down_ref, branch_ref = weights
        loads = [
            pltpu.make_async_copy(extra[2 + index], ref, scratch[self.base + 14 + index])
            for index, ref in enumerate(weights)
        ]
        copies = ExchangeCtx(self.dp, self.ctx, self.parts).copies(source, landed_ref, *scratch[2:5])
        for copy in copies + loads:
            copy.start()
        for copy in copies:
            copy.wait()
        ungroup(landed_ref, middle_ref, self.dp, self.ctx)

        def chunk(rows):
            middle = tokens_ref[rows].astype(single) + branch_scale * middle_ref[rows]
            middle_ref[rows] = middle
            normed, _ = normalize(middle)
            own_ref[rows] = (normed * gain_ref[...]).astype(bfloat)

        by_chunks(own_ref.shape[0], chunk)
        todo = list(loads)

        def out_copies(slot):
            height = 2 * own_ref.shape[0]
            for index, (ref, sem) in enumerate(zip(kept, kept_sems)):
                rows = pl.ds(slot * 2, 2) if index < 2 else pl.ds(slot * height, height)
                yield pltpu.make_async_copy(ref.at[rows], results[1 + index].at[rows], sem.at[slot])

        def arrived(slot):
            while todo:
                todo.pop(0).wait()
            height = 2 * own_ref.shape[0]
            rows = pl.ds(pl.multiple_of(slot * height, height), height)
            normed = all_ref[pl.ds(slot * 2, 2)].reshape(height, D)
            gate_act = dot(normed, gate_ref[...])
            up_act = dot(normed, up_ref[...])
            grad_hidden = dot(branch_ref[rows], down_ref[...], 1, 1)
            sigma = jax.nn.sigmoid(gate_act)
            silu = gate_act * sigma
            hidden = (silu * up_act).astype(bfloat)
            hidden_ref[rows] = hidden
            slope = sigma * (1.0 + gate_act * (1.0 - sigma))
            grad_gate_ref[rows] = (grad_hidden * up_act * slope).astype(bfloat)
            grad_up_ref[rows] = (grad_hidden * silu).astype(bfloat)
            out = dot(hidden, down_ref[...]).astype(bfloat)
            branch_out_ref[pl.ds(slot * 2, 2)] = out.reshape((2,) + own_ref.shape)
            for copy in out_copies(slot):
                copy.start()

        gather_line(line, own_ref, all_ref, scratch[5:self.base], arrived=arrived)
        for slot in range(line.pairs):
            for copy in out_copies(slot):
                copy.wait()


class MiddleBackLine:
    reach = "both"
    held = True

    def __init__(self, dp, ctx, parts, shape, f_part, fused):
        self.dp, self.ctx, self.parts, self.fused = dp, ctx, parts, fused
        own = shape[0]
        self.cut = (dp, D // dp, f_part)
        self.f_part = f_part
        self.result = [
            jax.ShapeDtypeStruct(shape, single),
            jax.ShapeDtypeStruct((1, D), single),
            jax.ShapeDtypeStruct((ctx, own, D), bfloat),
            jax.ShapeDtypeStruct((f_part, D), bfloat),
            jax.ShapeDtypeStruct(self.cut[1:], bfloat),
            jax.ShapeDtypeStruct(self.cut[1:], bfloat),
        ]
        self.in_vmem = [True, True, False, True, False, False]
        self.scratch = (
            [pltpu.VMEM(shape, bfloat), pltpu.VMEM((2,) + self.cut, bfloat)]
            + scatter_scratch(ctx, (own // 2, D), bfloat) + gather_sems(ctx)
            + [pltpu.SemaphoreType.DMA((2, dp - 1))] * 2 + [pltpu.VMEM((2, dp - 1) + self.cut[1:], bfloat)]
            + [pltpu.SemaphoreType.DMA]
            + ([pltpu.VMEM((ctx,) + shape, bfloat)] if fused else [])
        )
        self.base = len(self.scratch)
        self.second = self.base + 6
        group = ctx * own
        for size in (D, f_part):
            self.scratch = self.scratch + [pltpu.VMEM((group, size), bfloat), pltpu.SemaphoreType.DMA]
        self.scratch = self.scratch + [
            pltpu.VMEM((2, group, D // 4), bfloat), pltpu.SemaphoreType.DMA((2,))
        ]
        self.scratch = self.scratch + scatter_scratch(ctx, (own // 2, D), bfloat) + gather_sems(ctx)
        self.elsewhere = (3, 6, 7)

    def run(self, line, extra, source, results, scratch):
        middle_ref, cotangent_ref, gain_ref, grads = extra[0], extra[1], extra[2], extra[4:6]
        normed_mid_ref, hidden_ref, branch_ref = scratch[self.base : self.second : 2]
        loads = [
            pltpu.make_async_copy(extra[place], scratch[self.base + 2 * index], scratch[self.base + 2 * index + 1])
            for index, place in enumerate(self.elsewhere[:2])
        ]

        def branch_load(part):
            span = slice(part * (D // 4), (part + 1) * (D // 4))
            sem = scratch[self.base + 5].at[part % 2]
            return pltpu.make_async_copy(extra[7].at[:, span], branch_ref.at[part % 2], sem)

        for load in loads + [branch_load(0), branch_load(1)]:
            load.start()
        grad_middle_ref, gain_sum_ref, all_ref, down_ref = results[:4]
        landed = results[4:]
        own_ref, cut_ref = scratch[:2]
        send, receive, halves_ref = scratch[16:19]
        row = lax.axis_index("dp")
        height = D // self.dp

        levels = [list(range(self.dp.bit_length() - 1)), list(range(self.dp.bit_length() - 1))[::-1]]

        def bit(level):
            return (row // (1 << level)) % 2

        def flipped(step):
            return sum(((bit(level) + (step >> level)) % 2) * (1 << level) for level in levels[0])

        def target_of(index, phase, part, own):
            order = levels[index]
            level = order[phase]
            total = sum(bit(done) * (1 << done) for done in order[:phase])
            total += (bit(level) if own else 1 - bit(level)) * (1 << level)
            return total + sum(((part // (1 << k)) % 2) * (1 << rest) for k, rest in enumerate(order[phase + 1 :]))

        def exchange(index, phase, part):
            level = levels[index][phase]
            place = self.dp - (self.dp >> phase) + part
            return remote(
                cut_ref.at[index, target_of(index, phase, part, False)], halves_ref.at[index, place],
                send.at[index, place], receive.at[index, place],
                {"dp": row + (1 - 2 * bit(level)) * (1 << level)},
            )

        def parts_in(phase):
            return self.dp >> (phase + 1)

        def reduce(index, phase):
            last = phase == len(levels[index]) - 1
            for part in range(parts_in(phase)):
                exchange(index, phase, part).wait_recv()
                goal = target_of(index, phase, part, True)
                place = self.dp - (self.dp >> phase) + part
                total = cut_ref[index, goal].astype(single) + halves_ref[index, place].astype(single)
                cut_ref[index, goal] = total.astype(bfloat)
            if not last:
                for part in range(parts_in(phase + 1)):
                    exchange(index, phase + 1, part).start()

        def rows_work(step):
            if step == 1:
                loads[0].wait()
            aligned = height % LANES == 0
            if aligned:
                target = flipped(step % self.dp)
                columns = pl.ds(pl.multiple_of(target * height, LANES), height)
            else:
                target = step % self.dp
                columns = slice(target * height, (target + 1) * height)
            left = normed_mid_ref[:, columns].T
            for index in range(2):
                cut_ref[index, target] = dot(left, grads[index][...]).astype(bfloat)
                level = levels[index][0]
                if aligned and (step % self.dp >> level) % 2:
                    rest = enumerate(levels[index][1:])
                    part = sum(((bit(low) + (step >> low)) % 2) * (1 << k) for k, low in rest)
                    exchange(index, 0, part).start()
                elif not aligned and step == self.dp:
                    for part in range(parts_in(0)):
                        exchange(index, 0, part).start()

        def down_work(part):
            width = D // 4
            if part == 0:
                loads[1].wait()
            branch_load(part).wait()
            span = slice(part * width, (part + 1) * width)
            down_ref[:, span] = dot(hidden_ref[...].T, branch_ref[part % 2]).astype(bfloat)
            if part < 2:
                branch_load(part + 2).start()

        todo = [functools.partial(rows_work, step) for step in range(1, self.dp + 1)]
        todo += [functools.partial(down_work, part) for part in range(4)]

        def idle(count=2):
            for _ in range(min(count, len(todo))):
                todo.pop(0)()

        parts_ref = scratch[20] if self.fused else source

        def make(slot):
            pair_rows = 2 * own_ref.shape[0]
            rows = pl.ds(pl.multiple_of(slot * pair_rows, pair_rows), pair_rows)
            total = dot(grads[0][rows], source[...], 1, 1) + dot(grads[1][rows], extra[8][...], 1, 1)
            parts_ref[pl.ds(slot * 2, 2)] = total.astype(bfloat).reshape((2,) + own_ref.shape)

        half = own_ref.shape[0] // 2
        spans = [pl.ds(0, half), pl.ds(half, half)]
        parts = [parts_ref.at[:, span] for span in spans]
        travel = [scratch[2:10], scratch[self.second : self.second + 8]]
        gather = [scratch[10:16], scratch[self.second + 8 : self.second + 14]]

        def make_both(slot):
            if self.fused:
                make(slot)
            travels(line, parts[1], *travel[1][:2], travel[1][2:])[0](slot).start()

        sums = [
            scatter_steps(line, parts[0], *travel[0][:2], travel[0][2:], make_both),
            scatter_steps(line, parts[1], *travel[1][:2], travel[1][2:], None, True),
        ]
        gathers = [
            gather_steps(line, own_ref.at[span], all_ref.at[:, span], sems)
            for span, sems in zip(spans, gather)
        ]
        gain_sum_ref[...] = jnp.zeros_like(gain_sum_ref)

        def finish(index):
            span = spans[index]
            scatter_total(line, parts[index], *travel[index][:2], travel[index][2:], grad_middle_ref.at[span])

            def chunk(rows):
                normed, factor = normalize(middle_ref[rows])
                gradient = grad_middle_ref[rows]
                gain_sum_ref[...] += jnp.sum(gradient * normed, axis=0, keepdims=True)
                back = norm_back(gradient * gain_ref[...], normed, factor)
                back = cotangent_ref[rows].astype(single) + back
                grad_middle_ref[rows] = back
                own_ref[rows] = (branch_scale * back).astype(bfloat)

            by_chunks(half, chunk, index * half)

        for _ in sums[0]:
            idle()
        next(sums[1], None)
        finish(0)
        next(gathers[0])
        for _ in range(line.pairs - 1):
            next(sums[1], None)
            next(gathers[0])
            idle(1)
        finish(1)
        next(gathers[1])
        idle(len(todo))
        phases = len(levels[0])
        for phase in range(phases - 1):
            for index in range(2):
                reduce(index, phase)
            next(gathers[1])
        for _ in gathers[1]:
            pass
        next(gathers[0], None)
        for index in range(2):
            reduce(index, phases - 1)
            out = pltpu.make_async_copy(cut_ref.at[index, row], landed[index], scratch[19])
            out.start()
            out.wait()
            for phase in range(phases):
                for part in range(parts_in(phase)):
                    exchange(index, phase, part).wait_send()


class CloseLine:
    reach = "ctx"
    held = False

    def __init__(self, dp, ctx, parts):
        self.dp, self.ctx, self.parts = dp, ctx, parts
        own = parts.shape[1]
        self.result = [jax.ShapeDtypeStruct((own, D), single)]
        self.in_vmem = [True]
        self.scratch = [pltpu.VMEM(parts.shape, bfloat)] + pair_sems(ctx)

    def lay_out(self, rows, width):
        self.result += [jax.ShapeDtypeStruct((rows, width), single)] * 2
        self.in_vmem += [True] * 2
        return self

    def run(self, line, extra, source, results, scratch):
        tokens_ref, grad_middle_ref = extra[:2]
        out_ref, landed_ref = results[0], scratch[0]
        copies = ExchangeCtx(self.dp, self.ctx, self.parts).copies(source, landed_ref, *scratch[1:4])
        for copy in copies:
            copy.start()
        for index in range(2):
            regroup(extra[2 + index], results[1 + index], self.dp, self.ctx, False)
        for copy in copies:
            copy.wait()
        ungroup(landed_ref, out_ref, self.dp, self.ctx)

        def chunk(rows):
            normed, factor = normalize(tokens_ref[rows].astype(single))
            out_ref[rows] = grad_middle_ref[rows] + norm_back(out_ref[rows], normed, factor)

        by_chunks(out_ref.shape[0], chunk)


def by_chunks(total, work, first=0):
    def step(index, carry):
        work(pl.ds(pl.multiple_of(first + index * 16, 16), 16))
        return carry

    lax.fori_loop(0, total // 16, step, 0)


def regroup(source, target, dp, ctx, forward):
    whole, parts = (source, target) if forward else (target, source)
    width = whole.shape[1] // (dp * ctx)
    for place in range(ctx):
        for row in range(dp):
            start = (row * ctx + place) * width
            wide, narrow = slice(start, start + width), slice(row * width, (row + 1) * width)
            if forward:
                target[place, :, narrow] = source[:, wide]
            else:
                target[:, wide] = source[place, :, narrow].astype(single)


def ungroup(landed_ref, out_ref, dp, ctx):
    width = D // (dp * ctx)
    for place in range(ctx):
        block = landed_ref[place]
        block = block.reshape(out_ref.shape[0], dp * width).astype(single)
        for row in range(dp):
            start = (row * ctx + place) * width
            out_ref[:, start : start + width] = block[:, row * width : (row + 1) * width]


QUERY_SPAN = slice(0, QRANK)
LATENT_SPAN = slice(QRANK, QRANK + KVRANK)
ROPE_SPAN = slice(QRANK + KVRANK, LATENT)


def turn(values, table_ref, sign):
    return (
        values * table_ref[0]
        + sign * pltpu.roll(values, LANES - ROPE // 2, 1) * table_ref[1]
        + sign * pltpu.roll(values, ROPE // 2, 1) * table_ref[2]
    )


def everyone(dp, ctx):
    row, place = lax.axis_index("dp"), lax.axis_index("ctx")
    steps = [(a, b) for a in range(dp) for b in range(ctx) if a or b]
    return [((row + a) % dp, (place + b) % ctx) for a, b in steps]


def greet(dp, ctx, reach):
    row, place = lax.axis_index("dp"), lax.axis_index("ctx")
    if "all" in reach:
        targets = [{"dp": a, "ctx": b} for a, b in everyone(dp, ctx)]
    else:
        targets = []
        if "ctx" in reach:
            targets += [{"ctx": (place + step) % ctx} for step in range(1, ctx)]
        if "dp" in reach:
            targets += [{"dp": (row + step) % dp} for step in range(1, dp)]
    barrier = pltpu.get_barrier_semaphore()
    for target in targets:
        pl.semaphore_signal(barrier, inc=1, device_id=target, device_id_type=MESH)
    pl.semaphore_wait(barrier, len(targets))


def transfer_kernel(dp, ctx, line_piece, direct, extras, *refs):
    refs = list(refs)

    def take(count):
        taken = refs[:count]
        del refs[:count]
        return taken

    line_source = take(1) if line_piece else []
    sources = take(len(direct))
    extra = take(extras)
    line_results = take(len(line_piece.result)) if line_piece else []
    results = take(len(direct))
    line_scratch = take(len(line_piece.scratch)) if line_piece else []
    greet(dp, ctx, [piece.reach for piece in direct] + line_reach(line_piece))
    copies = []
    for piece, source, result in zip(direct, sources, results):
        copies += piece.copies(source, result, *take(len(piece.scratch)))
    for copy in copies:
        copy.start()
    if line_piece:
        line_piece.run(Line(ctx), extra, line_source[0], line_results, line_scratch)
    for copy in copies:
        copy.wait()


def line_reach(line_piece):
    if line_piece is None:
        return []
    return ["ctx", "dp"] if line_piece.reach == "both" else ["ctx"]


def transfer(dp, ctx, collective_id, name, line=None, direct=(), extra=(), mebibytes=8):
    pieces = [item[0](dp, ctx, item[1]) for item in direct]
    vmem, anywhere = pl.BlockSpec(memory_space=pltpu.VMEM), pl.BlockSpec(memory_space=pl.ANY)
    operands, in_specs, shapes, out_specs, scratch = [], [], [], [], []
    if line:
        operands.append(line.parts)
        in_specs.append(vmem if line.held else anywhere)
        shapes += line.result
        out_specs += [vmem if held else anywhere for held in line.in_vmem]
        scratch += line.scratch
    for piece in pieces:
        operands.append(piece.parts)
        in_specs.append(anywhere)
        shapes.append(piece.result)
        out_specs.append(anywhere)
        scratch += piece.scratch
    return pl.pallas_call(
        functools.partial(transfer_kernel, dp, ctx, line, pieces, len(extra)),
        out_shape=shapes,
        in_specs=in_specs + [
            pl.BlockSpec(memory_space=pltpu.SMEM) if item.dtype == jnp.int32
            else anywhere if index in getattr(line, "elsewhere", ()) else vmem
            for index, item in enumerate(extra)
        ],
        out_specs=out_specs,
        scratch_shapes=scratch,
        compiler_params=comm_params(collective_id, mebibytes),
        cost_estimate=link_cost(150 << 20),
        name=name,
    )(*operands, *extra)


def valid_pairs(total, length):
    row = lax.broadcasted_iota(jnp.int32, (total, total), 0)
    col = lax.broadcasted_iota(jnp.int32, (total, total), 1)
    return (col <= row) & (col < length)


def slot_rows(ref, index, batch):
    span = ref.shape[1] // batch
    block = ref[:, pl.ds(pl.multiple_of(index * span, span), span), :]
    return block.reshape(ref.shape[0] * span, ref.shape[2])


def store_slot(ref, index, batch, lanes, values):
    span = ref.shape[1] // batch
    rows = pl.ds(pl.multiple_of(index * span, span), span)
    ref[:, rows, lanes] = values.reshape(ref.shape[0], span, values.shape[-1])


def attend_slot(
    heads, index, batch, length_ref, latent_ref, query_up_ref, latent_up_ref, table_ref,
    query_ref, kv_ref, attn_ref, total_ref,
):
    wide = heads * LANES
    latent = slot_rows(latent_ref, index, batch)
    total = latent.shape[0]
    query_normed, latent_normed, rope = latent[:, QUERY_SPAN], latent[:, LATENT_SPAN], latent[:, ROPE_SPAN]
    allowed = valid_pairs(total, length_ref[index])
    lane = lax.broadcasted_iota(jnp.int32, (total, LANES), 1)
    totals = jnp.zeros((total, LANES), single)
    query_up = query_up_ref[...].reshape(QRANK, wide)
    latent_up = latent_up_ref[...].reshape(KVRANK, wide)
    columns = pl.ds(pl.multiple_of(index * total, LANES), total)
    for head in range(heads):
        span = slice(head * LANES, (head + 1) * LANES)
        query = turn(dot(query_normed, query_up[:, span]), table_ref, 1.0).astype(bfloat)
        kv = dot(latent_normed, latent_up[:, span]).astype(bfloat)
        key = jnp.where(lane < NOPE, kv, rope)
        store_slot(query_ref, index, batch, span, query)
        store_slot(kv_ref, index, batch, span, kv)
        scores = dot(query, key, 1, 1) * score_scale
        masked = jnp.where(allowed, scores, neg_large)
        top = jnp.max(masked, axis=-1, keepdims=True)
        exponent = jnp.exp(masked - top)
        weight = jnp.sum(exponent, axis=-1, keepdims=True)
        totals = jnp.where(lane == head, top + jnp.log(weight), totals)
        probs = (exponent * (1.0 / weight)).astype(bfloat)
        out = dot(probs, kv).T[NOPE:]
        attn_ref[head * VDIM : (head + 1) * VDIM, columns] = out.astype(bfloat)
    store_slot(total_ref, index, batch, slice(0, LANES), totals)


def attend_back_slot(
    heads, index, batch, length_ref, query_ref, kv_ref, latent_ref, total_ref, branch_ref,
    out_heads_ref, query_up_ref, latent_up_ref, table_ref, parts_ref,
    grad_query_ref, grad_high_ref, grad_low_ref, query_sum_ref, latent_sum_ref,
):
    wide = heads * LANES
    latent = slot_rows(latent_ref, index, batch)
    rope = latent[:, ROPE_SPAN]
    total = rope.shape[0]
    totals = slot_rows(total_ref, index, batch)
    allowed = valid_pairs(total, length_ref[index])
    lane = lax.broadcasted_iota(jnp.int32, (total, LANES), 1)
    grad_rope = jnp.zeros((total, LANES), single)
    queries, kvs = slot_rows(query_ref, index, batch), slot_rows(kv_ref, index, batch)
    grads = dot(slot_rows(branch_ref, index, batch), out_heads_ref[...].reshape(D, heads * VDIM))
    grads = grads.astype(bfloat)
    blank = jnp.zeros((total, NOPE), bfloat)
    for head in range(heads):
        span = slice(head * LANES, (head + 1) * LANES)
        query, kv = queries[:, span], kvs[:, span]
        grad_attn = jnp.concatenate([blank, grads[:, head * VDIM : (head + 1) * VDIM]], axis=1)
        key = jnp.where(lane < NOPE, kv, rope)
        scores = dot(query, key, 1, 1) * score_scale
        probs = jnp.where(allowed, jnp.exp(scores - totals[:, head : head + 1]), 0.0)
        grad_probs = dot(grad_attn, kv, 1, 1)
        delta = jnp.sum(probs * grad_probs, axis=-1, keepdims=True)
        grad_scores = (probs * (grad_probs - delta)).astype(bfloat)
        grad_query = (dot(grad_scores, key) * score_scale).astype(bfloat).astype(single)
        grad_query_ref[:, span] = turn(grad_query, table_ref, -1.0).astype(bfloat)
        grad_key = dot(grad_scores, query, 0, 0) * score_scale
        grad_value = dot(probs.astype(bfloat), grad_attn, 0, 0)
        grad_kv = jnp.where(lane < NOPE, grad_key, grad_value)
        high = grad_kv.astype(bfloat)
        grad_high_ref[:, span] = high
        grad_low_ref[:, span] = (grad_kv - high.astype(single)).astype(bfloat)
        grad_rope = grad_rope + jnp.where(lane < NOPE, 0.0, grad_key)
    grad_query, high, low = grad_query_ref[...], grad_high_ref[...], grad_low_ref[...]
    query_up = query_up_ref[...].reshape(QRANK, wide)
    latent_up = latent_up_ref[...].reshape(KVRANK, wide)
    grad_latent = dot(high, latent_up, 1, 1) + dot(low, latent_up, 1, 1)
    for span, values in (
        (QUERY_SPAN, dot(grad_query, query_up, 1, 1)), (LATENT_SPAN, grad_latent), (ROPE_SPAN, grad_rope),
    ):
        store_slot(parts_ref, index, batch, span, values.astype(bfloat))
    latent_normed = latent[:, LATENT_SPAN]
    query_sum_ref[...] += dot(latent[:, QUERY_SPAN], grad_query, 0, 0)
    latent_sum_ref[...] += dot(latent_normed, high, 0, 0) + dot(latent_normed, low, 0, 0)


def head_table(total):
    freqs = np.float32(10000.0) ** (-(2.0 * np.arange(ROPE // 2, dtype=np.float32)) / ROPE)
    angles = np.arange(total, dtype=np.float32)[:, None] * freqs.astype(np.float32)[None, :]
    cosine, sine = np.cos(angles), np.sin(angles)
    table = np.zeros((3, total, LANES), np.float32)
    half, end = NOPE + ROPE // 2, NOPE + ROPE
    table[0, :, :NOPE] = 1.0
    table[0, :, NOPE:half] = table[0, :, half:end] = cosine
    table[1, :, NOPE:half] = -sine
    table[2, :, half:end] = sine
    return jnp.asarray(table)


def pad_rope(values):
    return jnp.pad(values, ((0, 0), (NOPE, LANES - NOPE - ROPE)))


def on_device(
    dp,
    ctx,
    tokens,
    lengths,
    cotangent,
    input_gain,
    query_gain,
    latent_gain,
    post_gain,
    query_down,
    query_up,
    latent_down,
    latent_up,
    out_proj,
    gate_proj,
    up_proj,
    down_proj,
):
    batch, span, _ = tokens.shape
    own = batch * span
    group = ctx * own
    heads = -(-HEADS // ctx)
    spare = heads * ctx - HEADS
    d_rows, q_rows, l_rows, f_rows = (
        query_down.shape[0], query_up.shape[0], latent_up.shape[0], down_proj.shape[0],
    )
    d_part, f_part = dp * d_rows, dp * f_rows
    place = lax.axis_index("ctx")

    def slices(values):
        return values.reshape(own, dp, ctx, d_rows).transpose(2, 0, 1, 3).reshape(ctx, own, d_part)

    def row_sums(values):
        return jnp.sum(values.astype(single), axis=0)

    wide = heads * LANES
    up_rows = q_rows + l_rows
    run = functools.partial(transfer, dp, ctx)

    grad_out = cotangent.reshape(own, D).astype(single)
    grad_branch = (branch_scale * grad_out).astype(bfloat)

    flat = tokens.reshape(own, D)
    inputs = flat.astype(single)
    normed_first, factor_first = normalize(inputs)
    gains = jnp.concatenate([input_gain, query_gain, latent_gain, post_gain]).astype(single)
    tile = 8 * LANES
    small = jnp.concatenate(
        [jnp.pad(gains, (0, tile - gains.shape[0])), jnp.pad(factor_first[:, 0], (0, tile - own))]
    )
    down_own = jnp.concatenate(
        [query_down, latent_down[:, :KVRANK], pad_rope(latent_down[:, KVRANK:])], axis=1
    )
    up_query = query_up.reshape(q_rows, HEADS, NOPE + ROPE)
    up_query = jnp.pad(up_query, ((0, 0), (0, spare), (0, LANES - NOPE - ROPE)))
    up_latent = jnp.pad(latent_up.reshape(l_rows, HEADS, NOPE + VDIM), ((0, 0), (0, spare), (0, 0)))
    up_query = up_query.reshape(q_rows, ctx, wide).transpose(1, 0, 2)
    up_latent = up_latent.reshape(l_rows, ctx, wide).transpose(1, 0, 2)
    out_padded = jnp.pad(out_proj, ((0, 0), (0, spare * VDIM)))
    gate, up, token_slices, up_query, up_latent, down_rows, smalls, out_rows, down = run(
        1, "open", OpenLine(dp, ctx, gate_proj),
        [
            (ExchangeCtx, slices(flat)), (ExchangeCtx, up_query), (ExchangeCtx, up_latent),
            (GatherDp, down_own),
            (GatherAll, small.reshape(16, LANES)), (GatherDp, out_padded), (GatherDp, down_proj),
        ],
        (up_proj,), 16,
    )
    smalls, grad_branch = lax.optimization_barrier((smalls, grad_branch))
    grad_branch = gather_xla(grad_branch)
    down = down.reshape(f_part, D)
    down_rows = down_rows.reshape(d_part, LATENT)
    smalls = smalls.reshape(dp, ctx, 2 * tile)
    factor_all = smalls[lax.axis_index("dp"), :, tile : tile + own].reshape(group, 1)
    cuts = (d_rows, d_rows + q_rows, d_rows + up_rows, d_rows + up_rows + d_rows)
    gain_in = lax.dynamic_index_in_dim(smalls[:, :, : cuts[0]], place, 1, keepdims=False)
    gain_in = gain_in.reshape(1, d_part)
    gain_query = smalls[:, :, cuts[0] : cuts[1]].reshape(1, QRANK)
    gain_latent = smalls[:, :, cuts[1] : cuts[2]].reshape(1, KVRANK)
    gain_post = smalls[:, :, cuts[2] : cuts[3]].reshape(1, D)
    gain_down = jnp.concatenate([gain_query, gain_latent, jnp.zeros((1, LANES), single)], axis=1)

    normed_slices = token_slices.reshape(group, d_part).astype(single) * factor_all
    normed_in = (normed_slices * gain_in).astype(bfloat)
    table = head_table(ctx * span)
    own_table = lax.dynamic_slice_in_dim(table, place * span, span, 1)
    own_table = jnp.tile(own_table, (1, batch, 1))
    parts = dot(normed_in, down_rows).astype(bfloat).reshape(ctx, own, LATENT)
    out_heads = out_padded.reshape(d_rows, ctx, heads * VDIM).transpose(1, 0, 2)
    ups = (up_query.reshape(ctx * q_rows, wide), up_latent.reshape(ctx * l_rows, wide))
    outs = run(
        2, "forward",
        ForwardLine(dp, ctx, parts, heads, batch, (gate, up), ups, out_heads),
        (),
        (gain_down, own_table, lengths, table, gate, up) + ups + (out_heads,),
        56,
    )
    latents, latent_all, query, kv, totals, attn_all = outs[:6]
    query_ups, latent_ups, gate, up, out_heads = outs[6:]
    attn_all = attn_all.reshape(ctx * heads * VDIM, group)
    branch = dot(attn_all, out_rows.reshape(d_part, ctx * heads * VDIM), 0, 1).astype(bfloat).reshape(batch, ctx, span, d_part)
    gate, up = gate.reshape(D, f_part), up.reshape(D, f_part)
    middle, normed_mid, branch_out, hidden, grad_gate, grad_up, out_heads = run(
        4, "middle", MiddleLine(dp, ctx, branch, f_part),
        [(GatherDp, out_heads.reshape(ctx * d_rows, heads * VDIM))],
        (flat, gain_post, gate, up, down, grad_branch), 60,
    )
    normed_mid = normed_mid.reshape(group, D)
    fused = group <= 1024
    if fused:
        parts, last = gate, (up,)
    else:
        parts = dot(grad_gate, gate, 1, 1) + dot(grad_up, up, 1, 1)
        parts, last = parts.astype(bfloat).reshape(ctx, own, D), ()
    grad_middle, post_sum, grad_attn_branch, grad_down_proj, grad_gate_proj, grad_up_proj = run(
        5, "middle_back",
        MiddleBackLine(dp, ctx, parts, (own, D), f_part, fused),
        (),
        (
            middle, cotangent.reshape(own, D), gain_post, normed_mid, grad_gate, grad_up, hidden,
            grad_branch,
        ) + last,
        62,
    )
    columns_shape = (ctx, d_rows, f_part)
    grad_gate_proj = grad_gate_proj.reshape(columns_shape)
    grad_up_proj = grad_up_proj.reshape(columns_shape)

    outs = run(
        8, "backward", BackwardLine(dp, ctx, grad_attn_branch, heads, batch, HEADS * VDIM),
        [
            (ExchangeDp, grad_down_proj.reshape(dp, f_rows, D)), (ExchangeCtx, grad_gate_proj),
            (ExchangeCtx, grad_up_proj),
        ],
        (
            gain_down, own_table, latents, attn_all, lengths, query, kv, latent_all, totals, out_heads,
            query_ups, latent_ups, table,
        ),
        62,
    )
    grad_latents, grad_down, grad_out_proj, grad_query_ups, grad_latent_ups = outs[:5]
    grad_down_proj, grad_gate_proj, grad_up_proj = outs[5:]
    branch_out, grad_down = lax.optimization_barrier((branch_out, grad_down))
    branch_out = scatter_xla(branch_out.reshape(group, D)).astype(single)
    layer_out = (middle + branch_scale * branch_out).astype(bfloat)
    grad_down = grad_down.reshape(group, LATENT)
    grad_normed_in = dot(grad_down, down_rows, 1, 1)
    grad_scaled = (grad_normed_in * gain_in).astype(bfloat).reshape(ctx, own, d_part)
    grad_rows = dot(normed_in, grad_down, 0, 0)
    last = jnp.sum(grad_normed_in * normed_slices, axis=0)[:, None]
    grad_rows = jnp.concatenate([grad_rows[:, : LATENT - 1], last], axis=1)
    normed_query, _ = normalize(latents[:, :QRANK])
    normed_latent, _ = normalize(latents[:, QRANK : QRANK + KVRANK])
    grad_query_normed = grad_latents[:, :QRANK]
    grad_latent_normed = grad_latents[:, QRANK : QRANK + KVRANK]
    gain_sums = jnp.concatenate(
        [
            post_sum.reshape(dp, ctx, d_rows),
            jnp.sum(grad_query_normed * normed_query, axis=0).reshape(dp, ctx, q_rows),
            jnp.sum(grad_latent_normed * normed_latent, axis=0).reshape(dp, ctx, l_rows),
        ],
        axis=2,
    )
    gain_sums = jnp.pad(gain_sums, ((0, 0), (0, 0), (0, tile - gain_sums.shape[2])))
    outs = run(
        9, "close", CloseLine(dp, ctx, grad_scaled).lay_out(d_rows, FF),
        [
            (ExchangeDp, grad_rows.reshape(dp, d_rows, LATENT)),
            (ExchangeCtx, row_sums(grad_query_ups).astype(bfloat).reshape(ctx, q_rows, wide)),
            (ExchangeCtx, row_sums(grad_latent_ups).astype(bfloat).reshape(ctx, l_rows, wide)),
            (ExchangeAll, gain_sums.reshape(dp, ctx, 8, LANES)),
        ],
        (flat, grad_middle, grad_gate_proj, grad_up_proj),
        32,
    )
    input_grad, grad_gate_proj, grad_up_proj, grad_rows = outs[:4]
    grad_query_ups, grad_latent_ups, gain_sums = outs[4:]
    grad_rows = jnp.sum(grad_rows, axis=0)
    gain_sums = jnp.sum(gain_sums.reshape(dp * ctx, tile), axis=0)

    def by_heads(values, rows):
        return values.transpose(1, 0, 2).reshape(rows, ctx * heads, LANES)[:, :HEADS].astype(single)

    grad_query_up = by_heads(grad_query_ups, q_rows)[:, :, : NOPE + ROPE]
    grad_query_up = grad_query_up.reshape(q_rows, HEADS * (NOPE + ROPE))
    grad_latent_up = by_heads(grad_latent_ups, l_rows).reshape(l_rows, HEADS * (NOPE + VDIM))
    rope_start = QRANK + KVRANK + NOPE
    return (
        layer_out.reshape(batch, span, D),
        input_grad.reshape(batch, span, D),
        grad_rows[:, LATENT - 1],
        gain_sums[d_rows : d_rows + q_rows],
        gain_sums[d_rows + q_rows : d_rows + up_rows],
        gain_sums[:d_rows],
        grad_rows[:, :QRANK],
        grad_query_up,
        jnp.concatenate(
            [grad_rows[:, QRANK : QRANK + KVRANK], grad_rows[:, rope_start : rope_start + ROPE]], axis=1
        ),
        grad_latent_up,
        row_sums(grad_out_proj),
        grad_gate_proj,
        grad_up_proj,
        row_sums(grad_down_proj),
    )


def solution(mesh):
    both = ("dp", "ctx")
    tokens, vector, matrix = P("dp", "ctx", None), P(both), P(both, None)
    return jax.shard_map(
        functools.partial(on_device, mesh.shape["dp"], mesh.shape["ctx"]),
        mesh=mesh,
        in_specs=(tokens, P("dp"), tokens) + (vector,) * 4 + (matrix,) * 8,
        out_specs=(tokens, tokens) + (vector,) * 4 + (matrix,) * 8,
        check_vma=False,
    )
```

```python
import functools

import jax
import jax.numpy as jnp
import numpy as np
from jax import lax
from jax.experimental import pallas as pl
from jax.experimental.pallas import tpu as pltpu
from jax.sharding import PartitionSpec as P

D = 2560
FF = 6400
HEADS = 40
QRANK = 768
KVRANK = 256
NOPE = 64
ROPE = 32
VDIM = 64

LANES = 128
LATENT = QRANK + KVRANK + LANES

epsilon = 1e-05
branch_scale = 1.4 / 62**0.5
score_scale = 1.0 / (NOPE + ROPE) ** 0.5
neg_large = -1e30
bfloat = jnp.bfloat16
MESH = pl.DeviceIdType.MESH
single = jnp.float32
highest = lax.Precision.HIGHEST


def dot(left, right, left_dim=1, right_dim=0, precision=None):
    return lax.dot_general(
        left,
        right,
        (((left_dim,), (right_dim,)), ((), ())),
        precision=precision,
        preferred_element_type=single,
    )


def normalize(values):
    factor = lax.rsqrt(jnp.mean(values * values, axis=-1, keepdims=True) + epsilon)
    return (values * factor, factor)


def norm_back(grad_scaled, normed, factor):
    return factor * (grad_scaled - normed * jnp.mean(grad_scaled * normed, axis=-1, keepdims=True))


def gather_xla(values):
    return lax.all_gather(values, "ctx", axis=0, tiled=True)


def scatter_xla(values):
    return lax.psum_scatter(values, "ctx", scatter_dimension=0, tiled=True)


def exchange_xla(values):
    return lax.all_to_all(values, "ctx", 0, 0, tiled=True)


class Line:
    def __init__(self, ctx):
        self.pairs = ctx // 2
        self.place = lax.axis_index("ctx")
        self.pair, self.core = self.place // 2, self.place % 2
        self.has_left, self.has_right = self.pair > 0, self.pair < self.pairs - 1
        self.left = {"ctx": jnp.maximum(self.place - 2, 0)}
        self.right = {"ctx": jnp.minimum(self.place + 2, ctx - 1)}
        self.twin = {"ctx": self.place + 1 - 2 * self.core}


def remote(source, target, send, receive, device):
    return pltpu.make_async_remote_copy(
        src_ref=source, dst_ref=target, send_sem=send, recv_sem=receive,
        device_id=device, device_id_type=MESH,
    )


def nothing():
    pass


def gather_line(line, own_ref, all_ref, sems, idle=nothing, arrived=None):
    steps = gather_steps(line, own_ref, all_ref, sems, arrived)
    for step, _ in enumerate(steps):
        if step < line.pairs - 1:
            idle()


def gather_steps(line, own_ref, all_ref, sems, arrived=None):
    send_left, send_right, send_twin, receive, receive_twin, local = sems
    pairs, pair, core = line.pairs, line.pair, line.core

    def to_side(source, slot, sem, device):
        return remote(source, all_ref.at[slot * 2 + core], sem.at[slot], receive.at[slot], device)

    def to_twin(source, slot):
        return remote(source, all_ref.at[slot * 2 + core], send_twin.at[slot], receive_twin.at[slot], line.twin)

    pl.when(line.has_right)(lambda: to_side(own_ref, pair, send_right, line.right).start())
    pl.when(line.has_left)(lambda: to_side(own_ref, pair, send_left, line.left).start())
    to_twin(own_ref, pair).start()
    keep = pltpu.make_async_copy(own_ref, all_ref.at[line.place], local)
    keep.start()
    if arrived:
        keep.wait()
        to_twin(own_ref, pair).wait_recv()
        arrived(pair)
    for step in range(1, pairs):
        yield

        def from_left(slot=pair - step):
            block = all_ref.at[slot * 2 + core]
            to_side(block, slot, send_left, line.left).wait_recv()
            pl.when(line.has_right)(lambda: to_side(block, slot, send_right, line.right).start())
            to_twin(block, slot).start()

        def from_right(slot=pair + step):
            block = all_ref.at[slot * 2 + core]
            to_side(block, slot, send_right, line.right).wait_recv()
            pl.when(line.has_left)(lambda: to_side(block, slot, send_left, line.left).start())
            to_twin(block, slot).start()

        pl.when(pair - step >= 0)(from_left)
        pl.when(pair + step < pairs)(from_right)
        if arrived:
            slot = nearest(line, step)
            to_twin(own_ref, slot).wait_recv()
            arrived(slot)
    yield
    if not arrived:
        keep.wait()
    for slot in range(pairs):
        if arrived:
            to_twin(own_ref, slot).wait_send()
        else:
            to_twin(own_ref, slot).wait()
        pl.when((slot <= pair) & line.has_right)(
            lambda slot=slot: to_side(own_ref, slot, send_right, line.right).wait_send())
        pl.when((slot >= pair) & line.has_left)(
            lambda slot=slot: to_side(own_ref, slot, send_left, line.left).wait_send())


def nearest(line, order):
    shorter = jnp.minimum(line.pair, line.pairs - 1 - line.pair)
    distance = (order + 1) // 2
    both = line.pair + (distance if order % 2 == 0 else -distance)
    ahead = jnp.where(line.pair < line.pairs - 1 - line.pair, order - shorter, shorter - order)
    return jnp.where(order <= 2 * shorter, both, line.pair + ahead)


def comm_params(collective_id, mebibytes):
    return pltpu.CompilerParams(
        collective_id=collective_id, has_side_effects=True, vmem_limit_bytes=mebibytes << 20
    )


def link_cost(size):
    return pl.CostEstimate(flops=0, transcendentals=0, bytes_accessed=size)


def scatter_line(line, parts_ref, twin_ref, landed_ref, sems, idle=nothing):
    for _ in scatter_steps(line, parts_ref, twin_ref, landed_ref, sems):
        idle()


def scatter_steps(line, parts_ref, twin_ref, landed_ref, sems, make=None, begun=False):
    send_twin, receive_twin, send_left, send_right, from_left, from_right = sems
    pairs, pair = line.pairs, line.pair
    to_twin, to_right, to_left = travels(line, parts_ref, twin_ref, landed_ref, sems)

    def both_cores(slot):
        return parts_ref[slot * 2 + line.core].astype(single) + twin_ref[slot].astype(single)

    def prepare(order):
        ahead = (pair + pairs - 1 - order) % pairs
        slot = jnp.where(pair < pairs // 2, ahead, (pair + 1 + order) % pairs)
        if make:
            make(slot)
        to_twin(slot).start()

    todo = [] if begun else list(range(pairs))
    for _ in range(2 if make else len(todo)):
        prepare(todo.pop(0))
    for step in range(pairs - 1, 0, -1):
        yield

        def pass_on(slot, arrives, travel):
            to_twin(slot).wait_recv()

            @pl.when(arrives)
            def _():
                travel(slot).wait_recv()
                total = both_cores(slot) + landed_ref[slot].astype(single)
                twin_ref[slot] = total.astype(twin_ref.dtype)

            @pl.when(jnp.logical_not(arrives))
            def _():
                twin_ref[slot] = both_cores(slot).astype(twin_ref.dtype)

            travel(slot).start()

        pl.when(pair + step < pairs)(lambda slot=pair + step: pass_on(slot, line.has_left, to_right))
        pl.when(pair - step >= 0)(lambda slot=pair - step: pass_on(slot, line.has_right, to_left))
        if todo:
            prepare(todo.pop(0))
    to_twin(pair).wait_recv()


def travels(line, parts_ref, twin_ref, landed_ref, sems):
    send_twin, receive_twin, send_left, send_right, from_left, from_right = sems
    pairs = line.pairs

    def to_twin(slot):
        source = parts_ref.at[slot * 2 + 1 - line.core]
        return remote(source, twin_ref.at[slot], send_twin.at[slot], receive_twin.at[slot], line.twin)

    def to_right(slot):
        return remote(
            twin_ref.at[slot], landed_ref.at[slot], send_right.at[slot], from_left.at[slot], line.right
        )

    def to_left(slot):
        goal = jnp.where(slot == line.pair - 1, pairs, slot)
        return remote(
            twin_ref.at[slot], landed_ref.at[goal], send_left.at[slot], from_right.at[slot], line.left
        )

    return (to_twin, to_right, to_left)


def scatter_total(line, parts_ref, twin_ref, landed_ref, sems, out_ref):
    pairs, pair = line.pairs, line.pair
    to_twin, to_right, to_left = travels(line, parts_ref, twin_ref, landed_ref, sems)
    out_ref[...] = parts_ref[pair * 2 + line.core].astype(single) + twin_ref[pair].astype(single)

    @pl.when(line.has_left)
    def _():
        to_right(pair).wait_recv()
        out_ref[...] += landed_ref[pair].astype(single)

    @pl.when(line.has_right)
    def _():
        to_left(pair).wait_recv()
        out_ref[...] += landed_ref[pairs].astype(single)

    for slot in range(pairs):
        to_twin(slot).wait_send()
        pl.when(slot > pair)(lambda slot=slot: to_right(slot).wait_send())
        pl.when(slot < pair)(lambda slot=slot: to_left(slot).wait_send())


def gather_sems(ctx):
    return [pltpu.SemaphoreType.DMA((ctx // 2,))] * 5 + [pltpu.SemaphoreType.DMA]


def scatter_scratch(ctx, shape, dtype):
    pairs = ctx // 2
    slots = [pltpu.VMEM((count,) + shape, dtype) for count in (pairs, pairs + 1)]
    return slots + [pltpu.SemaphoreType.DMA((pairs,))] * 6


def pair_sems(count):
    return [pltpu.SemaphoreType.DMA((count,))] * 2 + [pltpu.SemaphoreType.DMA]


class ExchangeCtx:
    reach = "ctx"

    def __init__(self, dp, ctx, parts):
        self.count, self.parts = ctx, parts
        self.axis = len(parts.shape) - 3
        shape = parts.shape if not self.axis else (ctx, parts.shape[0]) + parts.shape[2:]
        self.result = jax.ShapeDtypeStruct(shape, parts.dtype)
        self.scratch = pair_sems(ctx)

    def copies(self, source, target, send, receive, local):
        place = lax.axis_index("ctx")

        def part(index):
            return source.at[:, index] if self.axis else source.at[index]

        out = [pltpu.make_async_copy(part(place), target.at[place], local)]
        for step in range(1, self.count):
            other = (place + step) % self.count
            out.append(
                remote(
                    part(other), target.at[place], send.at[step], receive.at[step], {"ctx": other}
                )
            )
        return out


class ExchangeDp:
    reach = "dp"
    whole = False

    def __init__(self, dp, ctx, parts):
        self.count, self.parts = dp, parts
        shape = (dp,) + parts.shape if self.whole else parts.shape
        self.result = jax.ShapeDtypeStruct(shape, parts.dtype)
        self.scratch = pair_sems(dp)

    def copies(self, source, target, send, receive, local):
        row = lax.axis_index("dp")

        def part(index):
            return source if self.whole else source.at[index]

        out = [pltpu.make_async_copy(part(row), target.at[row], local)]
        for step in range(1, self.count):
            other = (row + step) % self.count
            out.append(
                remote(part(other), target.at[row], send.at[step], receive.at[step], {"dp": other})
            )
        return out


class GatherDp(ExchangeDp):
    whole = True


class ExchangeAll:
    reach = "all"
    whole = False

    def __init__(self, dp, ctx, parts):
        self.dp, self.ctx, self.parts = dp, ctx, parts
        shape = (dp, ctx) + parts.shape if self.whole else parts.shape
        self.result = jax.ShapeDtypeStruct(shape, parts.dtype)
        self.scratch = pair_sems(dp * ctx)

    def copies(self, source, target, send, receive, local):
        row, place = lax.axis_index("dp"), lax.axis_index("ctx")

        def part(index):
            return source if self.whole else source.at[index[0], index[1]]

        out = [pltpu.make_async_copy(part((row, place)), target.at[row, place], local)]
        for index, other in enumerate(everyone(self.dp, self.ctx)):
            out.append(
                remote(
                    part(other), target.at[row, place], send.at[index], receive.at[index],
                    {"dp": other[0], "ctx": other[1]},
                )
            )
        return out


class GatherAll(ExchangeAll):
    whole = True


class GatherLine:
    reach = "ctx"
    held = False
    extra_held = True

    def __init__(self, dp, ctx, parts):
        self.parts = parts
        self.result = [jax.ShapeDtypeStruct((ctx,) + parts.shape, parts.dtype)]
        self.in_vmem = [False]
        self.scratch = gather_sems(ctx)

    def run(self, line, extra, source, results, sems):
        gather_line(line, source, results[0], sems)


class LatentLine:
    reach = "ctx"
    held = True

    def __init__(self, dp, ctx, parts):
        shape = parts.shape[1:]
        self.parts = parts
        self.result = [
            jax.ShapeDtypeStruct(shape, single), jax.ShapeDtypeStruct(parts.shape, bfloat)
        ]
        self.in_vmem = [True, False]
        self.scratch = [pltpu.VMEM(shape, bfloat)] + scatter_scratch(ctx, shape, bfloat) + gather_sems(ctx)

    def finish_own(self, extra, sums_ref, own_ref):
        gain_ref, table_ref = extra
        for span in (QUERY_SPAN, LATENT_SPAN):
            normed, _ = normalize(sums_ref[:, span])
            own_ref[:, span] = (normed * gain_ref[:, span]).astype(bfloat)
        own_ref[:, ROPE_SPAN] = turn(sums_ref[:, ROPE_SPAN], table_ref, 1.0).astype(bfloat)

    def run(self, line, extra, source, results, scratch):
        sums_ref, all_ref = results
        own_ref = scratch[0]
        scatter_line(line, source, *scratch[1:3], scratch[3:9])
        scatter_total(line, source, *scratch[1:3], scratch[3:9], sums_ref)
        self.finish_own(extra, sums_ref, own_ref)
        gather_line(line, own_ref, all_ref, scratch[9:])


class OpenLine:
    reach = "ctx"
    held = True

    def __init__(self, dp, ctx, parts):
        self.dp, self.ctx, self.parts = dp, ctx, parts
        rows, width = parts.shape
        self.cut = jax.ShapeDtypeStruct((ctx, rows, width // ctx), bfloat)
        self.result = [self.cut] * 2
        self.in_vmem = [False] * 2
        self.scratch = [pltpu.VMEM((2,) + self.cut.shape, bfloat)] + pair_sems(ctx) * 2

    def run(self, line, extra, source, results, scratch):
        cut_ref, copies = scratch[0], []
        for index, matrix in enumerate((source, extra[0])):
            regroup(matrix, cut_ref.at[index], self.dp, self.ctx, True)
            sems = scratch[1 + 3 * index : 4 + 3 * index]
            pieces = ExchangeCtx(self.dp, self.ctx, self.cut).copies(cut_ref.at[index], results[index], *sems)
            for copy in pieces:
                copy.start()
            copies += pieces
        for copy in copies:
            copy.wait()


class ForwardLine(LatentLine):
    reach = "both"

    def __init__(self, dp, ctx, parts, heads, batch, matrices, ups, out_heads):
        super().__init__(dp, ctx, parts)
        own = parts.shape[1]
        group, wide = ctx * own, heads * LANES
        self.dp, self.ctx, self.heads, self.batch = dp, ctx, heads, batch
        self.pieces = {
            "heads": ExchangeCtx(dp, ctx, out_heads),
            "queries": GatherDp(dp, ctx, ups[0]),
            "latents": GatherDp(dp, ctx, ups[1]),
            "gates": GatherDp(dp, ctx, matrices[0]),
            "ups": GatherDp(dp, ctx, matrices[1]),
        }
        self.elsewhere = (4, 5)
        self.result += [
            jax.ShapeDtypeStruct((ctx, own, wide), bfloat),
            jax.ShapeDtypeStruct((ctx, own, wide), bfloat),
            jax.ShapeDtypeStruct((ctx, own, LANES), single),
            jax.ShapeDtypeStruct((ctx, heads * VDIM, group), bfloat),
        ]
        self.result += [
            self.pieces[name].result for name in ("queries", "latents", "gates", "ups", "heads")
        ]
        self.in_vmem = [True, True, True, True, True, False, True, True] + [False] * 3
        self.base = len(self.scratch)
        self.scratch = self.scratch + [pltpu.VMEM((heads * VDIM, group), bfloat)]
        for piece in self.pieces.values():
            self.scratch = self.scratch + piece.scratch
        self.scratch = self.scratch + gather_sems(ctx)

    def run(self, line, extra, source, results, scratch):
        gain_ref, table_ref, length_ref, slot_table_ref = extra[:4]
        matrices, ups, out_heads_ref = extra[4:6], extra[6:8], extra[8]
        sums_ref, all_ref, query_ref, kv_ref, total_ref, attn_all_ref = results[:6]
        query_ups_ref, latent_ups_ref, gates_ref, ups_ref, heads_ref = results[6:]
        attn_ref = scratch[self.base]
        later = list(scratch[self.base + 1 :])
        ends = {
            "heads": (out_heads_ref, heads_ref), "queries": (ups[0], query_ups_ref),
            "latents": (ups[1], latent_ups_ref),
            "gates": (matrices[0], gates_ref), "ups": (matrices[1], ups_ref),
        }
        copies = {}
        for name, piece in self.pieces.items():
            copies[name] = piece.copies(*ends[name], *later[: len(piece.scratch)])
            del later[: len(piece.scratch)]

        def start(*names):
            for name in names:
                for copy in copies[name]:
                    copy.start()

        def wait(*names):
            for name in names:
                for copy in copies[name]:
                    copy.wait()

        start("queries", "latents", "gates", "ups")
        scatter_line(line, source, *scratch[1:3], scratch[3:9])
        scatter_total(line, source, *scratch[1:3], scratch[3:9], sums_ref)
        self.finish_own((gain_ref, table_ref), sums_ref, scratch[0])
        gather_line(line, scratch[0], all_ref, scratch[9 : self.base])
        wait("queries", "latents")
        start("heads")

        def slot(index, carry):
            attend_slot(
                self.heads, index, self.batch, length_ref, all_ref, query_ups_ref, latent_ups_ref,
                slot_table_ref, query_ref, kv_ref, attn_ref, total_ref,
            )
            return carry

        lax.fori_loop(0, self.batch, slot, 0)
        gather_line(line, attn_ref, attn_all_ref, later)
        wait("heads", "gates", "ups")


class BackwardLine(LatentLine):
    reach = "both"

    def __init__(self, dp, ctx, branch, heads, batch, columns):
        own = branch.shape[1]
        parts = jax.ShapeDtypeStruct((ctx, own, LATENT), bfloat)
        super().__init__(dp, ctx, parts)
        self.parts = branch
        self.dp, self.ctx, self.heads, self.batch = dp, ctx, heads, batch
        rows, wide = D // (dp * ctx), heads * LANES
        self.ups = [
            ExchangeDp(dp, ctx, jax.ShapeDtypeStruct((dp, rank // dp, wide), bfloat))
            for rank in (QRANK, KVRANK)
        ]
        self.out = ExchangeDp(dp, ctx, jax.ShapeDtypeStruct((dp, rows, columns), bfloat))
        self.result += [self.out.result]
        self.result += [piece.result for piece in self.ups]
        self.in_vmem += [False, False, False]
        self.base = len(self.scratch)
        total = ctx * own // batch
        self.scratch = self.scratch + [
            pltpu.VMEM((ctx * own, rows), bfloat), pltpu.VMEM(parts.shape, bfloat),
        ]
        self.scratch = self.scratch + [pltpu.VMEM((total, wide), bfloat)] * 3
        self.scratch = self.scratch + [pltpu.VMEM((rank, wide), single) for rank in (QRANK, KVRANK)]
        self.scratch = self.scratch + [pltpu.VMEM(piece.parts.shape, bfloat) for piece in self.ups]
        for piece in self.ups + [self.out]:
            self.scratch = self.scratch + piece.scratch
        self.scratch = self.scratch + [pltpu.VMEM(self.out.parts.shape, bfloat)]

    def run(self, line, extra, source, results, scratch):
        branch_ref, attn_ref = source, extra[3]
        parts_ref = scratch[self.base + 1]
        work_refs = scratch[self.base + 2 : self.base + 5]
        sum_refs = scratch[self.base + 5 : self.base + 7]
        send_refs = scratch[self.base + 7 : self.base + 9]
        sems = scratch[self.base + 9 :]
        for ref in sum_refs:
            ref[...] = jnp.zeros_like(ref)

        def slot(index, carry):
            attend_back_slot(
                self.heads, index, self.batch, extra[4], extra[5], extra[6], extra[7], extra[8],
                branch_ref, *extra[9:13], parts_ref, *work_refs, *sum_refs,
            )
            return carry

        lax.fori_loop(0, self.batch, slot, 0)
        copies = []
        for index, piece in enumerate(self.ups):
            send_refs[index][...] = sum_refs[index][...].astype(bfloat).reshape(piece.parts.shape)
            copies += piece.copies(
                send_refs[index], results[3 + index], *sems[3 * index : 3 * index + 3]
            )
        for copy in copies:
            copy.start()
        out_ref, slice_ref = scratch[-1], scratch[self.base]
        out_copies = self.out.copies(out_ref, results[2], *scratch[-4:-1])
        rows = D // (self.dp * self.ctx)
        height = D // self.dp
        own = branch_ref.shape[1]
        span = own // self.batch

        def work(index):
            row = lax.broadcasted_iota(jnp.int32, (height, rows), 0)
            col = lax.broadcasted_iota(jnp.int32, (height, rows), 1)
            chosen = (row == line.place * rows + col).astype(single).astype(bfloat)
            block = branch_ref[:, :, index * height : (index + 1) * height]
            picked = dot(block.reshape(self.ctx * own, height), chosen).astype(bfloat)
            for place in range(self.ctx):
                for slot in range(self.batch):
                    start = (place * self.batch + slot) * span
                    goal = (slot * self.ctx + place) * span
                    slice_ref[goal : goal + span] = picked[start : start + span]
            columns = out_ref.shape[2]
            out_ref[index] = dot(slice_ref[...].T, attn_ref[:columns], 1, 1).astype(bfloat)

        todo = list(range(self.dp))

        def idle():
            if todo:
                work(todo.pop(0))
                if not todo:
                    for copy in out_copies:
                        copy.start()

        sums_ref, all_ref = results[:2]
        own_ref = scratch[0]
        scatter_line(line, parts_ref, *scratch[1:3], scratch[3:9], idle)
        scatter_total(line, parts_ref, *scratch[1:3], scratch[3:9], sums_ref)
        self.finish_own(extra[:3], sums_ref, own_ref)
        gather_line(line, own_ref, all_ref, scratch[9 : self.base], idle)
        while todo:
            idle()
        for copy in copies + out_copies:
            copy.wait()

    def finish_own(self, extra, sums_ref, own_ref):
        gain_ref, table_ref, latents_ref = extra
        for span in (QUERY_SPAN, LATENT_SPAN):
            normed, factor = normalize(latents_ref[:, span])
            scaled = sums_ref[:, span] * gain_ref[:, span]
            own_ref[:, span] = norm_back(scaled, normed, factor).astype(bfloat)
        own_ref[:, ROPE_SPAN] = turn(sums_ref[:, ROPE_SPAN], table_ref, -1.0).astype(bfloat)


class MiddleLine:
    reach = "ctx"
    held = False

    def __init__(self, dp, ctx, parts, f_part):
        self.dp, self.ctx, self.parts = dp, ctx, parts
        own, cut = parts.shape[0] * parts.shape[2], parts.shape[3]
        group = ctx * own
        self.result = [
            jax.ShapeDtypeStruct((own, D), single), jax.ShapeDtypeStruct((ctx, own, D), bfloat),
            jax.ShapeDtypeStruct((ctx, own, D), bfloat),
        ]
        self.result += [jax.ShapeDtypeStruct((group, f_part), bfloat)] * 3
        self.in_vmem = [True] + [False] * 5
        self.scratch = (
            [pltpu.VMEM((ctx, parts.shape[0], parts.shape[2], cut), bfloat), pltpu.VMEM((own, D), bfloat)]
            + pair_sems(ctx) + gather_sems(ctx)
        )
        self.base = len(self.scratch)
        self.scratch = self.scratch + [pltpu.VMEM((ctx, own, D), bfloat)] * 2
        self.scratch = self.scratch + [pltpu.VMEM((group, f_part), bfloat)] * 3
        self.scratch = self.scratch + [pltpu.SemaphoreType.DMA((ctx // 2,))] * 5
        shapes = [(D, f_part), (D, f_part), (f_part, D), (group, D)]
        self.scratch = self.scratch + [pltpu.VMEM(shape, bfloat) for shape in shapes]
        self.scratch = self.scratch + [pltpu.SemaphoreType.DMA] * 4
        self.elsewhere = (2, 3, 4, 5)

    def run(self, line, extra, source, results, scratch):
        tokens_ref, gain_ref = extra[:2]
        middle_ref = results[0]
        landed_ref, own_ref = scratch[:2]
        kept = scratch[self.base : self.base + 5]
        kept_sems = scratch[self.base + 5 : self.base + 10]
        weights = scratch[self.base + 10 : self.base + 14]
        all_ref, branch_out_ref, hidden_ref, grad_gate_ref, grad_up_ref = kept
        gate_ref, up_ref, down_ref, branch_ref = weights
        loads = [
            pltpu.make_async_copy(extra[2 + index], ref, scratch[self.base + 14 + index])
            for index, ref in enumerate(weights)
        ]
        copies = ExchangeCtx(self.dp, self.ctx, self.parts).copies(source, landed_ref, *scratch[2:5])
        for copy in copies + loads:
            copy.start()
        for copy in copies:
            copy.wait()
        ungroup(landed_ref, middle_ref, self.dp, self.ctx)

        def chunk(rows):
            middle = tokens_ref[rows].astype(single) + branch_scale * middle_ref[rows]
            middle_ref[rows] = middle
            normed, _ = normalize(middle)
            own_ref[rows] = (normed * gain_ref[...]).astype(bfloat)

        by_chunks(own_ref.shape[0], chunk)
        todo = list(loads)

        def out_copies(slot):
            height = 2 * own_ref.shape[0]
            for index, (ref, sem) in enumerate(zip(kept, kept_sems)):
                rows = pl.ds(slot * 2, 2) if index < 2 else pl.ds(slot * height, height)
                yield pltpu.make_async_copy(ref.at[rows], results[1 + index].at[rows], sem.at[slot])

        def arrived(slot):
            while todo:
                todo.pop(0).wait()
            height = 2 * own_ref.shape[0]
            rows = pl.ds(pl.multiple_of(slot * height, height), height)
            normed = all_ref[pl.ds(slot * 2, 2)].reshape(height, D)
            gate_act = dot(normed, gate_ref[...])
            up_act = dot(normed, up_ref[...])
            grad_hidden = dot(branch_ref[rows], down_ref[...], 1, 1)
            sigma = jax.nn.sigmoid(gate_act)
            silu = gate_act * sigma
            hidden = (silu * up_act).astype(bfloat)
            hidden_ref[rows] = hidden
            slope = sigma * (1.0 + gate_act * (1.0 - sigma))
            grad_gate_ref[rows] = (grad_hidden * up_act * slope).astype(bfloat)
            grad_up_ref[rows] = (grad_hidden * silu).astype(bfloat)
            out = dot(hidden, down_ref[...]).astype(bfloat)
            branch_out_ref[pl.ds(slot * 2, 2)] = out.reshape((2,) + own_ref.shape)
            for copy in out_copies(slot):
                copy.start()

        gather_line(line, own_ref, all_ref, scratch[5:self.base], arrived=arrived)
        for slot in range(line.pairs):
            for copy in out_copies(slot):
                copy.wait()


class MiddleBackLine:
    reach = "both"
    held = True

    def __init__(self, dp, ctx, parts, shape, f_part, fused):
        self.dp, self.ctx, self.parts, self.fused = dp, ctx, parts, fused
        own = shape[0]
        self.cut = (dp, D // dp, f_part)
        self.f_part = f_part
        self.result = [
            jax.ShapeDtypeStruct(shape, single),
            jax.ShapeDtypeStruct((1, D), single),
            jax.ShapeDtypeStruct((ctx, own, D), bfloat),
            jax.ShapeDtypeStruct((f_part, D), bfloat),
            jax.ShapeDtypeStruct(self.cut[1:], bfloat),
            jax.ShapeDtypeStruct(self.cut[1:], bfloat),
        ]
        self.in_vmem = [True, True, False, True, False, False]
        self.scratch = (
            [pltpu.VMEM(shape, bfloat), pltpu.VMEM((2,) + self.cut, bfloat)]
            + scatter_scratch(ctx, (own // 2, D), bfloat) + gather_sems(ctx)
            + [pltpu.SemaphoreType.DMA((2, dp - 1))] * 2 + [pltpu.VMEM((2, dp - 1) + self.cut[1:], bfloat)]
            + [pltpu.SemaphoreType.DMA]
            + ([pltpu.VMEM((ctx,) + shape, bfloat)] if fused else [])
        )
        self.base = len(self.scratch)
        self.second = self.base + 6
        group = ctx * own
        for size in (D, f_part):
            self.scratch = self.scratch + [pltpu.VMEM((group, size), bfloat), pltpu.SemaphoreType.DMA]
        self.scratch = self.scratch + [
            pltpu.VMEM((2, group, D // 4), bfloat), pltpu.SemaphoreType.DMA((2,))
        ]
        self.scratch = self.scratch + scatter_scratch(ctx, (own // 2, D), bfloat) + gather_sems(ctx)
        self.elsewhere = (3, 6, 7)

    def run(self, line, extra, source, results, scratch):
        middle_ref, cotangent_ref, gain_ref, grads = extra[0], extra[1], extra[2], extra[4:6]
        normed_mid_ref, hidden_ref, branch_ref = scratch[self.base : self.second : 2]
        loads = [
            pltpu.make_async_copy(extra[place], scratch[self.base + 2 * index], scratch[self.base + 2 * index + 1])
            for index, place in enumerate(self.elsewhere[:2])
        ]

        def branch_load(part):
            span = slice(part * (D // 4), (part + 1) * (D // 4))
            sem = scratch[self.base + 5].at[part % 2]
            return pltpu.make_async_copy(extra[7].at[:, span], branch_ref.at[part % 2], sem)

        for load in loads + [branch_load(0), branch_load(1)]:
            load.start()
        grad_middle_ref, gain_sum_ref, all_ref, down_ref = results[:4]
        landed = results[4:]
        own_ref, cut_ref = scratch[:2]
        send, receive, halves_ref = scratch[16:19]
        row = lax.axis_index("dp")
        height = D // self.dp

        levels = [list(range(self.dp.bit_length() - 1)), list(range(self.dp.bit_length() - 1))[::-1]]

        def bit(level):
            return (row // (1 << level)) % 2

        def flipped(step):
            return sum(((bit(level) + (step >> level)) % 2) * (1 << level) for level in levels[0])

        def target_of(index, phase, part, own):
            order = levels[index]
            level = order[phase]
            total = sum(bit(done) * (1 << done) for done in order[:phase])
            total += (bit(level) if own else 1 - bit(level)) * (1 << level)
            return total + sum(((part // (1 << k)) % 2) * (1 << rest) for k, rest in enumerate(order[phase + 1 :]))

        def exchange(index, phase, part):
            level = levels[index][phase]
            place = self.dp - (self.dp >> phase) + part
            return remote(
                cut_ref.at[index, target_of(index, phase, part, False)], halves_ref.at[index, place],
                send.at[index, place], receive.at[index, place],
                {"dp": row + (1 - 2 * bit(level)) * (1 << level)},
            )

        def parts_in(phase):
            return self.dp >> (phase + 1)

        def reduce(index, phase):
            last = phase == len(levels[index]) - 1
            for part in range(parts_in(phase)):
                exchange(index, phase, part).wait_recv()
                goal = target_of(index, phase, part, True)
                place = self.dp - (self.dp >> phase) + part
                total = cut_ref[index, goal].astype(single) + halves_ref[index, place].astype(single)
                cut_ref[index, goal] = total.astype(bfloat)
            if not last:
                for part in range(parts_in(phase + 1)):
                    exchange(index, phase + 1, part).start()

        def rows_work(step):
            if step == 1:
                loads[0].wait()
            aligned = height % LANES == 0
            if aligned:
                target = flipped(step % self.dp)
                columns = pl.ds(pl.multiple_of(target * height, LANES), height)
            else:
                target = step % self.dp
                columns = slice(target * height, (target + 1) * height)
            left = normed_mid_ref[:, columns].T
            for index in range(2):
                cut_ref[index, target] = dot(left, grads[index][...]).astype(bfloat)
                level = levels[index][0]
                if aligned and (step % self.dp >> level) % 2:
                    rest = enumerate(levels[index][1:])
                    part = sum(((bit(low) + (step >> low)) % 2) * (1 << k) for k, low in rest)
                    exchange(index, 0, part).start()
                elif not aligned and step == self.dp:
                    for part in range(parts_in(0)):
                        exchange(index, 0, part).start()

        def down_work(part):
            width = D // 4
            if part == 0:
                loads[1].wait()
            branch_load(part).wait()
            span = slice(part * width, (part + 1) * width)
            down_ref[:, span] = dot(hidden_ref[...].T, branch_ref[part % 2]).astype(bfloat)
            if part < 2:
                branch_load(part + 2).start()

        todo = [functools.partial(rows_work, step) for step in range(1, self.dp + 1)]
        todo += [functools.partial(down_work, part) for part in range(4)]

        def idle(count=2):
            for _ in range(min(count, len(todo))):
                todo.pop(0)()

        parts_ref = scratch[20] if self.fused else source

        def make(slot):
            pair_rows = 2 * own_ref.shape[0]
            rows = pl.ds(pl.multiple_of(slot * pair_rows, pair_rows), pair_rows)
            total = dot(grads[0][rows], source[...], 1, 1) + dot(grads[1][rows], extra[8][...], 1, 1)
            parts_ref[pl.ds(slot * 2, 2)] = total.astype(bfloat).reshape((2,) + own_ref.shape)

        half = own_ref.shape[0] // 2
        spans = [pl.ds(0, half), pl.ds(half, half)]
        parts = [parts_ref.at[:, span] for span in spans]
        travel = [scratch[2:10], scratch[self.second : self.second + 8]]
        gather = [scratch[10:16], scratch[self.second + 8 : self.second + 14]]

        def make_both(slot):
            if self.fused:
                make(slot)
            travels(line, parts[1], *travel[1][:2], travel[1][2:])[0](slot).start()

        sums = [
            scatter_steps(line, parts[0], *travel[0][:2], travel[0][2:], make_both),
            scatter_steps(line, parts[1], *travel[1][:2], travel[1][2:], None, True),
        ]
        gathers = [
            gather_steps(line, own_ref.at[span], all_ref.at[:, span], sems)
            for span, sems in zip(spans, gather)
        ]
        gain_sum_ref[...] = jnp.zeros_like(gain_sum_ref)

        def finish(index):
            span = spans[index]
            scatter_total(line, parts[index], *travel[index][:2], travel[index][2:], grad_middle_ref.at[span])

            def chunk(rows):
                normed, factor = normalize(middle_ref[rows])
                gradient = grad_middle_ref[rows]
                gain_sum_ref[...] += jnp.sum(gradient * normed, axis=0, keepdims=True)
                back = norm_back(gradient * gain_ref[...], normed, factor)
                back = cotangent_ref[rows].astype(single) + back
                grad_middle_ref[rows] = back
                own_ref[rows] = (branch_scale * back).astype(bfloat)

            by_chunks(half, chunk, index * half)

        for _ in sums[0]:
            idle()
        next(sums[1], None)
        finish(0)
        next(gathers[0])
        for _ in range(line.pairs - 1):
            next(sums[1], None)
            next(gathers[0])
            idle(1)
        finish(1)
        next(gathers[1])
        idle(len(todo))
        phases = len(levels[0])
        for phase in range(phases - 1):
            for index in range(2):
                reduce(index, phase)
            next(gathers[1])
        for _ in gathers[1]:
            pass
        next(gathers[0], None)
        for index in range(2):
            reduce(index, phases - 1)
            out = pltpu.make_async_copy(cut_ref.at[index, row], landed[index], scratch[19])
            out.start()
            out.wait()
            for phase in range(phases):
                for part in range(parts_in(phase)):
                    exchange(index, phase, part).wait_send()


class CloseLine:
    reach = "both"
    held = True

    def __init__(self, dp, ctx, parts, rows, width, arrived):
        self.dp, self.ctx, self.parts = dp, ctx, parts
        own, latent = parts.shape[1:]
        cut = jax.ShapeDtypeStruct((ctx, own, dp * rows), bfloat)
        self.scaled = ExchangeCtx(dp, ctx, cut)
        self.sums = [
            ExchangeDp(dp, ctx, jax.ShapeDtypeStruct(shape, single))
            for shape in ((dp, rows, latent), (dp, 8, LANES))
        ]
        self.result = [jax.ShapeDtypeStruct((own, D), single)]
        self.result += [jax.ShapeDtypeStruct((rows, width), single)] * 2
        self.result += [jax.ShapeDtypeStruct(item.shape[1:], single) for item in arrived]
        self.result += [piece.result for piece in self.sums]
        self.in_vmem = [True] * 5 + [False] * 2
        self.scratch = [pltpu.VMEM(cut.shape, bfloat)] * 2 + pair_sems(ctx)
        for piece in self.sums:
            self.scratch = self.scratch + [pltpu.VMEM(piece.parts.shape, single)] + piece.scratch
        for item in arrived:
            self.scratch = self.scratch + [pltpu.VMEM(item.shape, bfloat), pltpu.SemaphoreType.DMA]
        self.elsewhere = (8, 9)

    def run(self, line, extra, source, results, scratch):
        tokens_ref, grad_middle_ref = extra[:2]
        down_rows_ref, normed_ref, slices_ref, gain_ref = extra[4:8]
        out_ref, landed_ref, send_ref = results[0], scratch[0], scratch[1]
        rows_ref, small_ref = scratch[5], scratch[9]
        loads = [
            pltpu.make_async_copy(extra[8 + k], scratch[13 + 2 * k], scratch[14 + 2 * k]) for k in range(2)
        ]
        for load in loads:
            load.start()
        group = self.ctx * source.shape[1]
        height = rows_ref.shape[1]
        gradient = source[...].reshape(group, source.shape[2])
        grad_in = dot(gradient, down_rows_ref[...], 1, 1)
        send_ref[...] = (grad_in * gain_ref[...]).astype(bfloat).reshape(send_ref.shape)
        copies = self.scaled.copies(send_ref, landed_ref, *scratch[2:5])
        for copy in copies:
            copy.start()
        sums = dot(normed_ref[...].T, gradient)
        gains = jnp.sum(grad_in * slices_ref[...], axis=0, keepdims=True)
        small_ref[...] = jnp.zeros_like(small_ref)
        for row in range(self.dp):
            span = slice(row * height, (row + 1) * height)
            rows_ref[row] = sums[span]
            small_ref[row, 0:1, 0:height] = gains[:, span]
        later = self.sums[0].copies(rows_ref, results[5], *scratch[6:9])
        later += self.sums[1].copies(small_ref, results[6], *scratch[10:13])
        for copy in later:
            copy.start()
        for index in range(2):
            regroup(extra[2 + index], results[1 + index], self.dp, self.ctx, False)
        for index, load in enumerate(loads):
            load.wait()
            parts = scratch[13 + 2 * index]
            total = parts[0].astype(single)
            for row in range(1, self.dp):
                total = total + parts[row].astype(single)
            results[3 + index][...] = total
        for copy in copies:
            copy.wait()
        ungroup(landed_ref, out_ref, self.dp, self.ctx)

        def chunk(rows):
            normed, factor = normalize(tokens_ref[rows].astype(single))
            out_ref[rows] = grad_middle_ref[rows] + norm_back(out_ref[rows], normed, factor)

        by_chunks(out_ref.shape[0], chunk)
        for copy in later:
            copy.wait()


def by_chunks(total, work, first=0):
    def step(index, carry):
        work(pl.ds(pl.multiple_of(first + index * 16, 16), 16))
        return carry

    lax.fori_loop(0, total // 16, step, 0)


def regroup(source, target, dp, ctx, forward):
    whole, parts = (source, target) if forward else (target, source)
    width = whole.shape[1] // (dp * ctx)
    for place in range(ctx):
        for row in range(dp):
            start = (row * ctx + place) * width
            wide, narrow = slice(start, start + width), slice(row * width, (row + 1) * width)
            if forward:
                target[place, :, narrow] = source[:, wide]
            else:
                target[:, wide] = source[place, :, narrow].astype(single)


def ungroup(landed_ref, out_ref, dp, ctx):
    width = D // (dp * ctx)
    for place in range(ctx):
        block = landed_ref[place]
        block = block.reshape(out_ref.shape[0], dp * width).astype(single)
        for row in range(dp):
            start = (row * ctx + place) * width
            out_ref[:, start : start + width] = block[:, row * width : (row + 1) * width]


QUERY_SPAN = slice(0, QRANK)
LATENT_SPAN = slice(QRANK, QRANK + KVRANK)
ROPE_SPAN = slice(QRANK + KVRANK, LATENT)


def turn(values, table_ref, sign):
    return (
        values * table_ref[0]
        + sign * pltpu.roll(values, LANES - ROPE // 2, 1) * table_ref[1]
        + sign * pltpu.roll(values, ROPE // 2, 1) * table_ref[2]
    )


def everyone(dp, ctx):
    row, place = lax.axis_index("dp"), lax.axis_index("ctx")
    steps = [(a, b) for a in range(dp) for b in range(ctx) if a or b]
    return [((row + a) % dp, (place + b) % ctx) for a, b in steps]


def greet(dp, ctx, reach):
    row, place = lax.axis_index("dp"), lax.axis_index("ctx")
    if "all" in reach:
        targets = [{"dp": a, "ctx": b} for a, b in everyone(dp, ctx)]
    else:
        targets = []
        if "ctx" in reach:
            targets += [{"ctx": (place + step) % ctx} for step in range(1, ctx)]
        if "dp" in reach:
            targets += [{"dp": (row + step) % dp} for step in range(1, dp)]
    barrier = pltpu.get_barrier_semaphore()
    for target in targets:
        pl.semaphore_signal(barrier, inc=1, device_id=target, device_id_type=MESH)
    pl.semaphore_wait(barrier, len(targets))


def transfer_kernel(dp, ctx, line_piece, direct, extras, *refs):
    refs = list(refs)

    def take(count):
        taken = refs[:count]
        del refs[:count]
        return taken

    line_source = take(1) if line_piece else []
    sources = take(len(direct))
    extra = take(extras)
    line_results = take(len(line_piece.result)) if line_piece else []
    results = take(len(direct))
    line_scratch = take(len(line_piece.scratch)) if line_piece else []
    greet(dp, ctx, [piece.reach for piece in direct] + line_reach(line_piece))
    copies = []
    for piece, source, result in zip(direct, sources, results):
        copies += piece.copies(source, result, *take(len(piece.scratch)))
    for copy in copies:
        copy.start()
    if line_piece:
        line_piece.run(Line(ctx), extra, line_source[0], line_results, line_scratch)
    for copy in copies:
        copy.wait()


def line_reach(line_piece):
    if line_piece is None:
        return []
    return ["ctx", "dp"] if line_piece.reach == "both" else ["ctx"]


def transfer(dp, ctx, collective_id, name, line=None, direct=(), extra=(), mebibytes=8):
    pieces = [item[0](dp, ctx, item[1]) for item in direct]
    vmem, anywhere = pl.BlockSpec(memory_space=pltpu.VMEM), pl.BlockSpec(memory_space=pl.ANY)
    operands, in_specs, shapes, out_specs, scratch = [], [], [], [], []
    if line:
        operands.append(line.parts)
        in_specs.append(vmem if line.held else anywhere)
        shapes += line.result
        out_specs += [vmem if held else anywhere for held in line.in_vmem]
        scratch += line.scratch
    for piece in pieces:
        operands.append(piece.parts)
        in_specs.append(anywhere)
        shapes.append(piece.result)
        out_specs.append(anywhere)
        scratch += piece.scratch
    return pl.pallas_call(
        functools.partial(transfer_kernel, dp, ctx, line, pieces, len(extra)),
        out_shape=shapes,
        in_specs=in_specs + [
            pl.BlockSpec(memory_space=pltpu.SMEM) if item.dtype == jnp.int32
            else anywhere if index in getattr(line, "elsewhere", ()) else vmem
            for index, item in enumerate(extra)
        ],
        out_specs=out_specs,
        scratch_shapes=scratch,
        compiler_params=comm_params(collective_id, mebibytes),
        cost_estimate=link_cost(150 << 20),
        name=name,
    )(*operands, *extra)


def valid_pairs(total, length):
    row = lax.broadcasted_iota(jnp.int32, (total, total), 0)
    col = lax.broadcasted_iota(jnp.int32, (total, total), 1)
    return (col <= row) & (col < length)


def slot_rows(ref, index, batch):
    span = ref.shape[1] // batch
    block = ref[:, pl.ds(pl.multiple_of(index * span, span), span), :]
    return block.reshape(ref.shape[0] * span, ref.shape[2])


def store_slot(ref, index, batch, lanes, values):
    span = ref.shape[1] // batch
    rows = pl.ds(pl.multiple_of(index * span, span), span)
    ref[:, rows, lanes] = values.reshape(ref.shape[0], span, values.shape[-1])


def attend_slot(
    heads, index, batch, length_ref, latent_ref, query_up_ref, latent_up_ref, table_ref,
    query_ref, kv_ref, attn_ref, total_ref,
):
    wide = heads * LANES
    latent = slot_rows(latent_ref, index, batch)
    total = latent.shape[0]
    query_normed, latent_normed, rope = latent[:, QUERY_SPAN], latent[:, LATENT_SPAN], latent[:, ROPE_SPAN]
    allowed = valid_pairs(total, length_ref[index])
    lane = lax.broadcasted_iota(jnp.int32, (total, LANES), 1)
    totals = jnp.zeros((total, LANES), single)
    query_up = query_up_ref[...].reshape(QRANK, wide)
    latent_up = latent_up_ref[...].reshape(KVRANK, wide)
    columns = pl.ds(pl.multiple_of(index * total, LANES), total)
    for head in range(heads):
        span = slice(head * LANES, (head + 1) * LANES)
        query = turn(dot(query_normed, query_up[:, span]), table_ref, 1.0).astype(bfloat)
        kv = dot(latent_normed, latent_up[:, span]).astype(bfloat)
        key = jnp.where(lane < NOPE, kv, rope)
        store_slot(query_ref, index, batch, span, query)
        store_slot(kv_ref, index, batch, span, kv)
        scores = dot(query, key, 1, 1) * score_scale
        masked = jnp.where(allowed, scores, neg_large)
        top = jnp.max(masked, axis=-1, keepdims=True)
        exponent = jnp.exp(masked - top)
        weight = jnp.sum(exponent, axis=-1, keepdims=True)
        totals = jnp.where(lane == head, top + jnp.log(weight), totals)
        probs = (exponent * (1.0 / weight)).astype(bfloat)
        out = dot(probs, kv).T[NOPE:]
        attn_ref[head * VDIM : (head + 1) * VDIM, columns] = out.astype(bfloat)
    store_slot(total_ref, index, batch, slice(0, LANES), totals)


def attend_back_slot(
    heads, index, batch, length_ref, query_ref, kv_ref, latent_ref, total_ref, branch_ref,
    out_heads_ref, query_up_ref, latent_up_ref, table_ref, parts_ref,
    grad_query_ref, grad_high_ref, grad_low_ref, query_sum_ref, latent_sum_ref,
):
    wide = heads * LANES
    latent = slot_rows(latent_ref, index, batch)
    rope = latent[:, ROPE_SPAN]
    total = rope.shape[0]
    totals = slot_rows(total_ref, index, batch)
    allowed = valid_pairs(total, length_ref[index])
    lane = lax.broadcasted_iota(jnp.int32, (total, LANES), 1)
    grad_rope = jnp.zeros((total, LANES), single)
    queries, kvs = slot_rows(query_ref, index, batch), slot_rows(kv_ref, index, batch)
    grads = dot(slot_rows(branch_ref, index, batch), out_heads_ref[...].reshape(D, heads * VDIM))
    grads = grads.astype(bfloat)
    blank = jnp.zeros((total, NOPE), bfloat)
    for head in range(heads):
        span = slice(head * LANES, (head + 1) * LANES)
        query, kv = queries[:, span], kvs[:, span]
        grad_attn = jnp.concatenate([blank, grads[:, head * VDIM : (head + 1) * VDIM]], axis=1)
        key = jnp.where(lane < NOPE, kv, rope)
        scores = dot(query, key, 1, 1) * score_scale
        probs = jnp.where(allowed, jnp.exp(scores - totals[:, head : head + 1]), 0.0)
        grad_probs = dot(grad_attn, kv, 1, 1)
        delta = jnp.sum(probs * grad_probs, axis=-1, keepdims=True)
        grad_scores = (probs * (grad_probs - delta)).astype(bfloat)
        grad_query = (dot(grad_scores, key) * score_scale).astype(bfloat).astype(single)
        grad_query_ref[:, span] = turn(grad_query, table_ref, -1.0).astype(bfloat)
        grad_key = dot(grad_scores, query, 0, 0) * score_scale
        grad_value = dot(probs.astype(bfloat), grad_attn, 0, 0)
        grad_kv = jnp.where(lane < NOPE, grad_key, grad_value)
        high = grad_kv.astype(bfloat)
        grad_high_ref[:, span] = high
        grad_low_ref[:, span] = (grad_kv - high.astype(single)).astype(bfloat)
        grad_rope = grad_rope + jnp.where(lane < NOPE, 0.0, grad_key)
    grad_query, high, low = grad_query_ref[...], grad_high_ref[...], grad_low_ref[...]
    query_up = query_up_ref[...].reshape(QRANK, wide)
    latent_up = latent_up_ref[...].reshape(KVRANK, wide)
    grad_latent = dot(high, latent_up, 1, 1) + dot(low, latent_up, 1, 1)
    for span, values in (
        (QUERY_SPAN, dot(grad_query, query_up, 1, 1)), (LATENT_SPAN, grad_latent), (ROPE_SPAN, grad_rope),
    ):
        store_slot(parts_ref, index, batch, span, values.astype(bfloat))
    latent_normed = latent[:, LATENT_SPAN]
    query_sum_ref[...] += dot(latent[:, QUERY_SPAN], grad_query, 0, 0)
    latent_sum_ref[...] += dot(latent_normed, high, 0, 0) + dot(latent_normed, low, 0, 0)


def head_table(total):
    freqs = np.float32(10000.0) ** (-(2.0 * np.arange(ROPE // 2, dtype=np.float32)) / ROPE)
    angles = np.arange(total, dtype=np.float32)[:, None] * freqs.astype(np.float32)[None, :]
    cosine, sine = np.cos(angles), np.sin(angles)
    table = np.zeros((3, total, LANES), np.float32)
    half, end = NOPE + ROPE // 2, NOPE + ROPE
    table[0, :, :NOPE] = 1.0
    table[0, :, NOPE:half] = table[0, :, half:end] = cosine
    table[1, :, NOPE:half] = -sine
    table[2, :, half:end] = sine
    return jnp.asarray(table)


def pad_rope(values):
    return jnp.pad(values, ((0, 0), (NOPE, LANES - NOPE - ROPE)))


def on_device(
    dp,
    ctx,
    tokens,
    lengths,
    cotangent,
    input_gain,
    query_gain,
    latent_gain,
    post_gain,
    query_down,
    query_up,
    latent_down,
    latent_up,
    out_proj,
    gate_proj,
    up_proj,
    down_proj,
):
    batch, span, _ = tokens.shape
    own = batch * span
    group = ctx * own
    heads = -(-HEADS // ctx)
    spare = heads * ctx - HEADS
    d_rows, q_rows, l_rows, f_rows = (
        query_down.shape[0], query_up.shape[0], latent_up.shape[0], down_proj.shape[0],
    )
    d_part, f_part = dp * d_rows, dp * f_rows
    place = lax.axis_index("ctx")

    def slices(values):
        return values.reshape(own, dp, ctx, d_rows).transpose(2, 0, 1, 3).reshape(ctx, own, d_part)

    def row_sums(values):
        return jnp.sum(values.astype(single), axis=0)

    wide = heads * LANES
    up_rows = q_rows + l_rows
    run = functools.partial(transfer, dp, ctx)

    grad_out = cotangent.reshape(own, D).astype(single)
    grad_branch = (branch_scale * grad_out).astype(bfloat)

    flat = tokens.reshape(own, D)
    inputs = flat.astype(single)
    normed_first, factor_first = normalize(inputs)
    gains = jnp.concatenate([input_gain, query_gain, latent_gain, post_gain]).astype(single)
    tile = 8 * LANES
    small = jnp.concatenate(
        [jnp.pad(gains, (0, tile - gains.shape[0])), jnp.pad(factor_first[:, 0], (0, tile - own))]
    )
    down_own = jnp.concatenate(
        [query_down, latent_down[:, :KVRANK], pad_rope(latent_down[:, KVRANK:])], axis=1
    )
    up_query = query_up.reshape(q_rows, HEADS, NOPE + ROPE)
    up_query = jnp.pad(up_query, ((0, 0), (0, spare), (0, LANES - NOPE - ROPE)))
    up_latent = jnp.pad(latent_up.reshape(l_rows, HEADS, NOPE + VDIM), ((0, 0), (0, spare), (0, 0)))
    up_query = up_query.reshape(q_rows, ctx, wide).transpose(1, 0, 2)
    up_latent = up_latent.reshape(l_rows, ctx, wide).transpose(1, 0, 2)
    out_padded = jnp.pad(out_proj, ((0, 0), (0, spare * VDIM)))
    gate, up, token_slices, up_query, up_latent, down_rows, smalls, out_rows, down = run(
        1, "open", OpenLine(dp, ctx, gate_proj),
        [
            (ExchangeCtx, slices(flat)), (ExchangeCtx, up_query), (ExchangeCtx, up_latent),
            (GatherDp, down_own),
            (GatherAll, small.reshape(16, LANES)), (GatherDp, out_padded), (GatherDp, down_proj),
        ],
        (up_proj,), 16,
    )
    smalls, grad_branch = lax.optimization_barrier((smalls, grad_branch))
    grad_branch = gather_xla(grad_branch)
    down = down.reshape(f_part, D)
    down_rows = down_rows.reshape(d_part, LATENT)
    smalls = smalls.reshape(dp, ctx, 2 * tile)
    factor_all = smalls[lax.axis_index("dp"), :, tile : tile + own].reshape(group, 1)
    cuts = (d_rows, d_rows + q_rows, d_rows + up_rows, d_rows + up_rows + d_rows)
    gain_in = lax.dynamic_index_in_dim(smalls[:, :, : cuts[0]], place, 1, keepdims=False)
    gain_in = gain_in.reshape(1, d_part)
    gain_query = smalls[:, :, cuts[0] : cuts[1]].reshape(1, QRANK)
    gain_latent = smalls[:, :, cuts[1] : cuts[2]].reshape(1, KVRANK)
    gain_post = smalls[:, :, cuts[2] : cuts[3]].reshape(1, D)
    gain_down = jnp.concatenate([gain_query, gain_latent, jnp.zeros((1, LANES), single)], axis=1)

    normed_slices = token_slices.reshape(group, d_part).astype(single) * factor_all
    normed_in = (normed_slices * gain_in).astype(bfloat)
    table = head_table(ctx * span)
    own_table = lax.dynamic_slice_in_dim(table, place * span, span, 1)
    own_table = jnp.tile(own_table, (1, batch, 1))
    parts = dot(normed_in, down_rows).astype(bfloat).reshape(ctx, own, LATENT)
    out_heads = out_padded.reshape(d_rows, ctx, heads * VDIM).transpose(1, 0, 2)
    ups = (up_query.reshape(ctx * q_rows, wide), up_latent.reshape(ctx * l_rows, wide))
    outs = run(
        2, "forward",
        ForwardLine(dp, ctx, parts, heads, batch, (gate, up), ups, out_heads),
        (),
        (gain_down, own_table, lengths, table, gate, up) + ups + (out_heads,),
        56,
    )
    latents, latent_all, query, kv, totals, attn_all = outs[:6]
    query_ups, latent_ups, gate, up, out_heads = outs[6:]
    attn_all = attn_all.reshape(ctx * heads * VDIM, group)
    branch = dot(attn_all, out_rows.reshape(d_part, ctx * heads * VDIM), 0, 1).astype(bfloat).reshape(batch, ctx, span, d_part)
    gate, up = gate.reshape(D, f_part), up.reshape(D, f_part)
    middle, normed_mid, branch_out, hidden, grad_gate, grad_up, out_heads = run(
        4, "middle", MiddleLine(dp, ctx, branch, f_part),
        [(GatherDp, out_heads.reshape(ctx * d_rows, heads * VDIM))],
        (flat, gain_post, gate, up, down, grad_branch), 60,
    )
    normed_mid = normed_mid.reshape(group, D)
    fused = group <= 1024
    if fused:
        parts, last = gate, (up,)
    else:
        parts = dot(grad_gate, gate, 1, 1) + dot(grad_up, up, 1, 1)
        parts, last = parts.astype(bfloat).reshape(ctx, own, D), ()
    grad_middle, post_sum, grad_attn_branch, grad_down_proj, grad_gate_proj, grad_up_proj = run(
        5, "middle_back",
        MiddleBackLine(dp, ctx, parts, (own, D), f_part, fused),
        (),
        (
            middle, cotangent.reshape(own, D), gain_post, normed_mid, grad_gate, grad_up, hidden,
            grad_branch,
        ) + last,
        62,
    )
    columns_shape = (ctx, d_rows, f_part)
    grad_gate_proj = grad_gate_proj.reshape(columns_shape)
    grad_up_proj = grad_up_proj.reshape(columns_shape)

    outs = run(
        8, "backward", BackwardLine(dp, ctx, grad_attn_branch, heads, batch, HEADS * VDIM),
        [
            (ExchangeDp, grad_down_proj.reshape(dp, f_rows, D)), (ExchangeCtx, grad_gate_proj),
            (ExchangeCtx, grad_up_proj),
        ],
        (
            gain_down, own_table, latents, attn_all, lengths, query, kv, latent_all, totals, out_heads,
            query_ups, latent_ups, table,
        ),
        62,
    )
    grad_latents, grad_down, grad_out_proj, grad_query_ups, grad_latent_ups = outs[:5]
    grad_down_proj, grad_gate_proj, grad_up_proj = outs[5:]
    branch_out, grad_down = lax.optimization_barrier((branch_out, grad_down))
    branch_out = scatter_xla(branch_out.reshape(group, D)).astype(single)
    layer_out = (middle + branch_scale * branch_out).astype(bfloat)
    normed_query, _ = normalize(latents[:, :QRANK])
    normed_latent, _ = normalize(latents[:, QRANK : QRANK + KVRANK])
    grad_query_normed = grad_latents[:, :QRANK]
    grad_latent_normed = grad_latents[:, QRANK : QRANK + KVRANK]
    gain_sums = jnp.concatenate(
        [
            post_sum.reshape(dp, ctx, d_rows),
            jnp.sum(grad_query_normed * normed_query, axis=0).reshape(dp, ctx, q_rows),
            jnp.sum(grad_latent_normed * normed_latent, axis=0).reshape(dp, ctx, l_rows),
        ],
        axis=2,
    )
    gain_sums = jnp.pad(gain_sums, ((0, 0), (0, 0), (0, tile - gain_sums.shape[2])))
    outs = run(
        9, "close",
        CloseLine(dp, ctx, grad_down, d_rows, FF, (grad_down_proj, grad_out_proj)),
        [
            (ExchangeCtx, row_sums(grad_query_ups).astype(bfloat).reshape(ctx, q_rows, wide)),
            (ExchangeCtx, row_sums(grad_latent_ups).astype(bfloat).reshape(ctx, l_rows, wide)),
            (ExchangeAll, gain_sums.reshape(dp, ctx, 8, LANES)),
        ],
        (
            flat, grad_middle, grad_gate_proj, grad_up_proj, down_rows, normed_in, normed_slices, gain_in,
            grad_down_proj, grad_out_proj,
        ),
        48,
    )
    input_grad, grad_gate_proj, grad_up_proj, grad_down_proj, grad_out_proj, grad_rows, in_sums = outs[:7]
    grad_query_ups, grad_latent_ups, gain_sums = outs[7:]
    grad_rows = jnp.sum(grad_rows, axis=0)
    gain_sums = jnp.sum(gain_sums.reshape(dp * ctx, tile), axis=0)

    def by_heads(values, rows):
        return values.transpose(1, 0, 2).reshape(rows, ctx * heads, LANES)[:, :HEADS].astype(single)

    grad_query_up = by_heads(grad_query_ups, q_rows)[:, :, : NOPE + ROPE]
    grad_query_up = grad_query_up.reshape(q_rows, HEADS * (NOPE + ROPE))
    grad_latent_up = by_heads(grad_latent_ups, l_rows).reshape(l_rows, HEADS * (NOPE + VDIM))
    rope_start = QRANK + KVRANK + NOPE
    return (
        layer_out.reshape(batch, span, D),
        input_grad.reshape(batch, span, D),
        jnp.sum(in_sums, axis=0)[0, :d_rows],
        gain_sums[d_rows : d_rows + q_rows],
        gain_sums[d_rows + q_rows : d_rows + up_rows],
        gain_sums[:d_rows],
        grad_rows[:, :QRANK],
        grad_query_up,
        jnp.concatenate(
            [grad_rows[:, QRANK : QRANK + KVRANK], grad_rows[:, rope_start : rope_start + ROPE]], axis=1
        ),
        grad_latent_up,
        grad_out_proj,
        grad_gate_proj,
        grad_up_proj,
        grad_down_proj,
    )


def solution(mesh):
    both = ("dp", "ctx")
    tokens, vector, matrix = P("dp", "ctx", None), P(both), P(both, None)
    return jax.shard_map(
        functools.partial(on_device, mesh.shape["dp"], mesh.shape["ctx"]),
        mesh=mesh,
        in_specs=(tokens, P("dp"), tokens) + (vector,) * 4 + (matrix,) * 8,
        out_specs=(tokens, tokens) + (vector,) * 4 + (matrix,) * 8,
        check_vma=False,
    )
```
